32 devices in a mesh: rep: 4 (over x, core), stripe: 8 (over z, y).
Axes of the slice: x: 2, y: 2, z: 4, core: 2. Of those that a mesh axis runs over, the one named last changes fastest.
Arguments:
- activations: bfloat16 [1024, 1024], P('rep'), may hold values from -6 to 6
- out_grads: bfloat16 [1024, 4096], P('rep', 'stripe'), may hold values from -4 to 4
- statistics: float32 [4, 8, 512, 512], P('rep', 'stripe'), may hold values from -48 to 4608, as said below
- owner_blocks: int32 [8, 2], P('stripe'), may hold values from 0 to 1, each once within a row
Outputs:
- preconditioned: float32 [1024, 4096], P(None, 'stripe')
- new_stats: float32 [4, 8, 512, 512], P('rep', 'stripe')
The draws below stay inside these ranges and needn't reach their ends.
Inputs may be any that keep to these rules, and one draw needn't show every extreme that they name: statistics[p, s] is symmetric positive definite for every p and s. `owner_blocks`: each row lists every row block 0 to 1 exactly once.
All inputs are finite; a program needn't handle non-finite values.
Results may differ from the reference program's by a relative error of at most 0.0003.
Values sent between devices are 32-bit elements; how exact they have to be, the bound alone decides.
No kernel may reach another device: no remote copies, remote signals or barrier semaphores. Data moves between devices by JAX's collectives and lax.ppermute only.
A program may use at most 128 MiB of HBM per device.

```python
import math
import jax
import jax.numpy as jnp
from jax import lax

BLOCK = 512
ITERS = 2
PAIRS = 2
STRIPES = 8
DIN = 1024
DOUT = 4096
TOKENS = 1024
N_REP = 4
N_STRIPE = 8


def draw_statistics(key, part):
    key_diag = jax.random.fold_in(key, 101)
    key_noise = jax.random.fold_in(key, 202)
    owners = 2 * PAIRS
    diagonal = BLOCK * jnp.exp(jax.random.uniform(key_diag, (owners, STRIPES, BLOCK), jnp.float32, math.log(0.3), math.log(3.0)))
    rising = 3.0 ** (jnp.arange(owners, dtype=jnp.float32) / max(owners - 1, 1))
    diagonal = diagonal * rising[:, None, None]
    noise = jnp.clip(jax.random.normal(key_noise, (owners, STRIPES, BLOCK, BLOCK), jnp.float32), -6.0, 6.0)
    symmetric = (noise + jnp.swapaxes(noise, -1, -2)) / math.sqrt(2.0)
    root_diag = jnp.sqrt(diagonal)
    offdiag = 0.5 * symmetric * root_diag[..., :, None] * root_diag[..., None, :] / BLOCK
    identity = jnp.eye(BLOCK, dtype=jnp.float32)
    return offdiag * (1.0 - identity) + diagonal[..., :, None] * identity


def draw_out_grads(key, part):
    key_base = jax.random.fold_in(key, 303)
    key_cols = jax.random.fold_in(key, 404)
    base = jnp.clip(jax.random.normal(key_base, (TOKENS, DOUT), jnp.float32), -6.0, 6.0)
    columns = jnp.exp(jax.random.uniform(key_cols, (DOUT,), jnp.float32, -0.7, 0.7))
    stripe_pos = (jnp.arange(DOUT, dtype=jnp.int32) // BLOCK).astype(jnp.float32)
    rising = math.sqrt(3.0) ** (stripe_pos / max(STRIPES - 1, 1))
    return (base * columns * rising / math.sqrt(TOKENS)).astype(jnp.bfloat16)


def level_of(rng, extent, split, least, high):
    def one(position, blocks):
        heights = jax.random.uniform(jax.random.fold_in(jax.random.fold_in(rng, 6), position), (blocks,), jnp.float32, least / len(split), high / len(split))
        return jnp.repeat(jnp.exp(heights), extent[position] // blocks).reshape((-1,) + (1,) * (len(extent) - position - 1))

    gain = one(*split[0])
    for cut in split[1:]:
        gain = gain * one(*cut)
    return gain


def scatter_about(stream_key, dims, width, limit, pieces=(), held_as=jnp.bfloat16):
    gain = level_of(stream_key, dims, pieces, -0.22, 0.18) if pieces else 1.0
    drawn = jax.random.normal(stream_key, dims, jnp.float32) * width * gain
    return jnp.minimum(jnp.maximum(drawn, -limit), limit).astype(held_as)


def setup_inputs(seed: int = 0) -> dict:
    arg_keys = jax.random.split(jax.random.key(seed), 5)
    return {
        "activations": scatter_about(arg_keys[0], (TOKENS, DIN), 1.0, 6.0, ((0, 4),)),
        "out_grads": draw_out_grads(jax.random.fold_in(arg_keys[4], 71), 0),
        "statistics": draw_statistics(jax.random.fold_in(arg_keys[4], 71), 0),
        "owner_blocks": jax.vmap(lambda own: jax.random.permutation(own, PAIRS))(jax.random.split(arg_keys[3], STRIPES)).reshape((STRIPES, PAIRS)).astype(jnp.int32),
    }


decay_rate = 0.95
damping = 0.25
epsilon = 1e-06
highest = lax.Precision.HIGHEST

def inverse_root(damped):
    identity = jnp.eye(damped.shape[-1], dtype=damped.dtype)
    frob_norm = jnp.sqrt(lax.optimization_barrier(jnp.sum(damped * damped, axis=(-2, -1), keepdims=True)) + epsilon)
    scaled = damped / frob_norm
    root_now = identity * frob_norm ** (-0.25)
    for sweep in range(ITERS):
        factor = (5.0 * identity - scaled) * 0.25
        root_now = jnp.matmul(root_now, factor, precision=highest)
        if sweep + 1 < ITERS:
            square = jnp.matmul(factor, factor, precision=highest)
            fourth = jnp.matmul(square, square, precision=highest)
            scaled = jnp.matmul(fourth, scaled, precision=highest)
    return root_now

def reference(activations, out_grads, statistics, owner_blocks):
    pair_count = N_REP // 2
    stripe_count = N_STRIPE
    gradient = jnp.dot(activations.T, out_grads, preferred_element_type=jnp.float32)
    blocks = gradient.reshape(pair_count, BLOCK, stripe_count, BLOCK).transpose(0, 2, 1, 3)
    stripe_ids = jnp.arange(stripe_count, dtype=jnp.int32)[None, :]
    owned_blocks = blocks[owner_blocks.T, stripe_ids]
    flipped = jnp.swapaxes(owned_blocks, -1, -2)
    left_stats = decay_rate * statistics[:pair_count] + jnp.matmul(owned_blocks, flipped, precision=highest)
    right_stats = decay_rate * statistics[pair_count:] + jnp.matmul(flipped, owned_blocks, precision=highest)
    new_stats = jnp.concatenate([left_stats, right_stats], axis=0)
    trace_sum = jnp.sum(jnp.diagonal(new_stats, axis1=-2, axis2=-1))
    mean_diag = trace_sum / (N_REP * N_STRIPE * BLOCK)
    identity = jnp.eye(BLOCK, dtype=new_stats.dtype)
    left_root = inverse_root(left_stats + damping * mean_diag * identity)
    right_root = inverse_root(right_stats + damping * mean_diag * identity)
    precond = jnp.matmul(jnp.matmul(left_root, owned_blocks, precision=highest), right_root, precision=highest)
    grad_sq = jnp.sum(gradient * gradient)
    prec_sq = jnp.sum(precond * precond)
    precond = precond * jnp.sqrt(grad_sq / (prec_sq + epsilon))
    pair_ids = jnp.arange(pair_count, dtype=jnp.int32)
    inverse = lax.optimization_barrier(jnp.sum(pair_ids[None, :, None] * (owner_blocks[:, :, None] == pair_ids[None, None, :]).astype(jnp.int32), axis=1))
    placed = precond[inverse.T, stripe_ids]
    placed = placed.transpose(0, 2, 1, 3).reshape(pair_count * BLOCK, stripe_count * BLOCK)
    return (placed, new_stats)
```

```python
import math

import jax
import jax.numpy as jnp
from jax import lax
from jax.sharding import PartitionSpec as P

BLOCK = 512
HALF = BLOCK // 2

decay_rate = 0.95
damping = 0.25
epsilon = 1e-06
high = lax.Precision.HIGH
AXES = ("rep", "stripe")

ROOT_COEFFS = (
    25 / 16,
    -5 / 16 - 3125 / 4096,
    3125 / 4096,
    -1250 / 4096,
    250 / 4096,
    -25 / 4096,
    1 / 4096,
)


def flip(x, mask):
    return lax.ppermute(x, "rep", [(i, i ^ mask) for i in range(lax.axis_size("rep"))])


def share(partials):
    devices = lax.axis_size("rep") * lax.axis_size("stripe")
    spread = jnp.broadcast_to(partials[None], (devices,) + partials.shape)
    return lax.all_to_all(spread, AXES, 0, 0)


def lane_sums(x):
    return jnp.sum(x.reshape(-1, x.shape[-1] // 128, 128), axis=(0, 1))


def powers(stat):
    norm_sq = jnp.sum(stat * stat)
    trace = jnp.trace(stat)
    norm = jnp.sqrt(norm_sq + epsilon)
    t1 = stat * (1.0 / norm)
    t2 = jnp.dot(t1, t1, precision=high)
    t3 = jnp.dot(t1, t2, precision=high)
    return (t1, t2, t3), norm, norm_sq, trace


def shifted(norm, norm_sq, trace, shift):
    frob = jnp.sqrt(norm_sq + 2.0 * shift * trace + BLOCK * shift * shift + epsilon)
    a, e = norm / frob, shift / frob
    outer = frob ** (-0.25)
    out = []
    for i in range(7):
        total = 0.0
        for j in range(6, i - 1, -1):
            total = total * e + math.comb(j, i) * ROOT_COEFFS[j]
        out.append(outer * total)
        outer = outer * a
    return out


def root_of(t, t3_rows, rows, eye_rows, k):
    inner = k[4] * t[0] + k[5] * t[1] + k[6] * t[2]
    return k[0] * eye_rows + k[1] * rows[0] + k[2] * rows[1] + k[3] * t3_rows + jnp.dot(t3_rows, inner, precision=high)


def per_device(activations, out_grads, statistics, owner_blocks):
    rep_count = lax.axis_size("rep")
    pairs = rep_count // 2
    devices = rep_count * lax.axis_size("stripe")
    me = lax.axis_index("rep")
    chip, core = me // 2, me % 2
    first = core == 0
    owners = owner_blocks[0]
    stat_in = statistics[0, 0]
    tokens = activations.shape[0]

    def term(j, half):
        block = jnp.take(owners, chip ^ j)
        cols = lax.dynamic_slice(activations, (jnp.int32(0), block * BLOCK + half * HALF), (tokens, HALF))
        return lax.dot_general(cols, out_grads, (((0,), (0,)), ((), ())), preferred_element_type=jnp.float32)

    send = jnp.stack([term(j, 1 - core) for j in range(pairs)])
    keep = jnp.stack([term(j, core) for j in range(pairs)])
    acc = keep + flip(send, 1)
    shuffle = [(s * pairs + p, 2 * p + s) for s in range(2) for p in range(pairs)]
    stat_own = lax.ppermute(stat_in, "rep", shuffle)
    stat_other = flip(stat_own, 1)
    m = pairs // 2
    while m:
        acc = acc[:m] + flip(acc[m : 2 * m], 2 * m)
        m //= 2
    g_half = acc[0]
    g_other = flip(g_half, 1)
    grad = jnp.where(first, jnp.concatenate([g_half, g_other]), jnp.concatenate([g_other, g_half]))
    eye = jnp.eye(BLOCK, dtype=jnp.float32)
    diag = jnp.sum(stat_in * eye, axis=0).reshape(-1, 128).sum(axis=0)
    sums = jnp.sum(share(jnp.stack([lane_sums(g_half * g_half), diag])), axis=(0, 2))
    grad_sq = sums[0]
    shift = damping * (decay_rate * sums[1] + 2.0 * grad_sq) / (devices * BLOCK)

    stat_left = decay_rate * jnp.where(first, stat_own, stat_other) + jnp.dot(grad, grad.T, precision=high)
    stat_right = decay_rate * jnp.where(first, stat_other, stat_own) + jnp.dot(grad.T, grad, precision=high)
    new_stat = lax.ppermute(jnp.where(first, stat_left, stat_right), "rep", [(b, a) for a, b in shuffle])
    t_left, *left = powers(stat_left)
    t_right, *right = powers(stat_right)

    k_left = shifted(*left, shift)
    k_right = shifted(*right, shift)
    rows = [lax.dynamic_slice_in_dim(x, core * HALF, HALF, 0) for x in t_left]
    left_rows = root_of(t_left, rows[2], rows, lax.dynamic_slice_in_dim(eye, core * HALF, HALF, 0), k_left)
    right_root = root_of(t_right, t_right[2], t_right, eye, k_right)
    mine = jnp.dot(jnp.dot(left_rows, grad, precision=high), right_root, precision=high)
    prec_sq = jnp.sum(share(lane_sums(mine * mine)[None]))
    scale = jnp.sqrt(grad_sq / (prec_sq + epsilon))

    direct = mine[None]
    across = flip(direct, 1)
    m = 1
    while m < pairs:
        got = flip(direct, 2 * m)
        across = jnp.concatenate([across, flip(got, 1)])
        direct = jnp.concatenate([direct, got])
        m *= 2
    pieces = jnp.concatenate([direct, across])
    ids = jnp.arange(pairs, dtype=jnp.int32)
    inverse = jnp.sum(ids[:, None] * (owners[:, None] == ids[None, :]).astype(jnp.int32), axis=0)
    order = (chip ^ inverse)[:, None] + pairs * (jnp.arange(2, dtype=jnp.int32)[None] != core)
    placed = jnp.take(pieces, order.reshape(-1), axis=0) * scale
    return placed.reshape(pairs * BLOCK, -1), new_stat[None, None]


def solution(mesh):
    in_specs = (
        P("rep", None),
        P("rep", "stripe"),
        P("rep", "stripe", None, None),
        P("stripe", None),
    )
    out_specs = (P(None, "stripe"), P("rep", "stripe", None, None))
    return jax.shard_map(per_device, mesh=mesh, in_specs=in_specs, out_specs=out_specs, check_vma=False)
```

```python
import functools
import math

import jax
import jax.numpy as jnp
from jax import lax
from jax.experimental import pallas as pl
from jax.experimental.pallas import tpu as pltpu
from jax.sharding import PartitionSpec as P

BLOCK = 512
HALF = BLOCK // 2
PACKED = HALF + 8

decay_rate = 0.95
damping = 0.25
epsilon = 1e-06
AXES = ("rep", "stripe")
f32 = jnp.float32
bf16 = jnp.bfloat16

ROOT_COEFFS = (
    25 / 16,
    -5 / 16 - 3125 / 4096,
    3125 / 4096,
    -1250 / 4096,
    250 / 4096,
    -25 / 4096,
    1 / 4096,
)

VMEM = pl.BlockSpec(memory_space=pltpu.VMEM)
SMEM = pl.BlockSpec(memory_space=pltpu.SMEM)
ANY = pl.BlockSpec(memory_space=pl.ANY)
LOW = pl.ds(0, HALF)
TOP = pl.ds(HALF, HALF)


def call(body, out_shapes, in_specs, scratch=(), limit=24, flops=0, out_specs=None, **kwargs):
    return pl.pallas_call(
        body,
        out_shape=[jax.ShapeDtypeStruct(s, f32) for s in out_shapes],
        in_specs=in_specs,
        out_specs=out_specs or [VMEM] * len(out_shapes),
        scratch_shapes=list(scratch),
        compiler_params=pltpu.CompilerParams(vmem_limit_bytes=limit << 20),
        cost_estimate=pl.CostEstimate(flops=flops, bytes_accessed=1 << 20, transcendentals=0),
        name=body.func.__name__ if isinstance(body, functools.partial) else body.__name__,
        **kwargs,
    )


def flip(x, mask):
    return lax.ppermute(x, "rep", [(i, i ^ mask) for i in range(lax.axis_size("rep"))])


def chip_core():
    me = lax.axis_index("rep")
    return lax.shift_right_logical(me, 1), lax.bitwise_and(me, 1)


def split(x):
    hi = x.astype(bf16)
    return hi, (x - hi.astype(f32)).astype(bf16)


def mm(a, b):
    return jnp.dot(a, b, preferred_element_type=f32)


def dot3(a, b):
    return mm(a[0], b[0]) + (mm(a[0], b[1]) + mm(a[1], b[0]))


def triangle():
    i = lax.broadcasted_iota(jnp.int32, (HALF, HALF), 0)
    j = lax.broadcasted_iota(jnp.int32, (HALF, HALF), 1)
    return i, j


def lanes(x):
    rows = jnp.sum(x, axis=0, keepdims=True)
    return sum(rows[:, k : k + 128] for k in range(0, x.shape[1], 128))


def pack_into(out, a, b, c):
    i, j = triangle()
    out[LOW, LOW] = jnp.where(i <= j, a, c)
    out[LOW, TOP] = b
    out[HALF:, LOW] = jnp.broadcast_to(jnp.sum(jnp.where(i == j, c, 0.0), axis=0, keepdims=True), (8, HALF))


def unpack(u, diag):
    i, j = triangle()
    ut = u.T
    return jnp.where(i <= j, u, ut), jnp.where(i > j, u, jnp.where(i < j, ut, diag))


def pack_stat(stat, out, trace):
    i, j = triangle()
    a, c = stat[LOW, LOW], stat[TOP, TOP]
    pack_into(out, a, stat[LOW, TOP], c)
    trace[...] = lanes(jnp.where(i == j, a + c, 0.0))


def grad_terms(pairs, acts, grads, owners, send, keep):
    chip, core = chip_core()
    cotangent = grads[...]
    for out, half in ((send, 1 - core), (keep, core)):
        for j in range(pairs):
            start = owners[0, chip ^ j] * BLOCK + half * HALF
            cols = acts[:, pl.ds(pl.multiple_of(start, HALF), HALF)]
            out[j] = lax.dot_general(cols, cotangent, (((0,), (0,)), ((), ())), preferred_element_type=f32)


def finish_half(devices, a, b, c, trace, half, sums):
    total = a[0] + b[0] + c[0]
    half[...] = total
    both = jnp.concatenate([lanes(total * total), trace[...]], axis=0)
    sums[...] = jnp.broadcast_to(both[None], (devices, 2, 128))


def update_stats(half, other, near, far, left, right, out, g, gt):
    _, core = chip_core()
    mine = pl.ds(pl.multiple_of(core * HALF, HALF), HALF)
    theirs = pl.ds(pl.multiple_of(HALF - core * HALF, HALF), HALF)
    for rows, src in ((mine, half), (theirs, other)):
        g[0, rows], g[1, rows] = split(src[...])
    for k in range(2):
        gt[k] = g[k].T
    for side, res, a, b in ((0, left, g, gt), (1, right, gt, g)):
        old = lambda r, c: jnp.where(core == side, far[r, c], near[r, c])
        a0 = (a[0, LOW], a[1, LOW])
        a1 = (a[0, TOP], a[1, TOP])
        top = dot3(a0, (b[0], b[1]))
        corner = dot3(a1, (b[0, :, TOP], b[1, :, TOP]))
        sa, sc = unpack(old(LOW, LOW), old(pl.ds(HALF, 1), LOW))
        res[LOW, LOW] = decay_rate * sa + top[:, :HALF]
        off = decay_rate * old(LOW, TOP) + top[:, HALF:]
        res[LOW, TOP] = off
        res[TOP, LOW] = off.T
        res[TOP, TOP] = decay_rate * sc + corner

    @pl.when(core == 1)
    def _():
        pack_into(out, left[LOW, LOW], left[LOW, TOP], left[TOP, TOP])

    @pl.when(core == 0)
    def _():
        pack_into(out, right[LOW, LOW], right[LOW, TOP], right[TOP, TOP])


def symmetric_product(a, b, out):
    top = dot3((a[0, LOW], a[1, LOW]), (b[0], b[1]))
    out[LOW] = top
    out[TOP, TOP] = dot3((a[0, TOP], a[1, TOP]), (b[0, :, TOP], b[1, :, TOP]))
    out[TOP, LOW] = top[:, HALF:].T


def stat_powers(left, right, left_t, right_t, facts, s1, s2):
    i, j = triangle()
    norms, traces = [], []
    for stat, t in ((left, left_t), (right, right_t)):
        x = stat[...]
        norm_sq = jnp.sum(jnp.sum(x * x, axis=0, keepdims=True), axis=1, keepdims=True)
        diag = jnp.where(i == j, stat[LOW, LOW] + stat[TOP, TOP], 0.0)
        norms.append(norm_sq)
        traces.append(jnp.sum(jnp.sum(diag, axis=0, keepdims=True), axis=1, keepdims=True))
        t1 = x * (1.0 / jnp.sqrt(norm_sq + epsilon))
        t[0] = t1
        s1[0], s1[1] = split(t1)
        symmetric_product(s1, s1, t.at[1])
        s2[0], s2[1] = split(t[1])
        symmetric_product(s1, s2, t.at[2])
    facts[...] = jnp.concatenate([jnp.broadcast_to(x, (1, 128)) for x in norms + traces], axis=0)


def precondition(devices, half, other, left_t, right_t, facts, sums, mine, spread, totals, g):
    _, core = chip_core()
    own = pl.ds(pl.multiple_of(core * HALF, HALF), HALF)
    theirs = pl.ds(pl.multiple_of(HALF - core * HALF, HALF), HALF)
    for rows, src in ((own, half), (theirs, other)):
        g[0, rows], g[1, rows] = split(src[...])
    both = jnp.sum(jnp.sum(sums[...], axis=0), axis=1, keepdims=True)
    grad_sq, trace = both[0:1], both[1:2]
    shift = (decay_rate * trace + 2.0 * grad_sq) * (damping / (devices * BLOCK))
    norm_sq, traces = facts[0:2, :], facts[2:4, :]
    shift = jnp.broadcast_to(shift, (2, 128))
    frob = jnp.sqrt(norm_sq + 2.0 * shift * traces + BLOCK * shift * shift + epsilon)
    a = jnp.sqrt(norm_sq + epsilon) / frob
    e = shift / frob
    outer = 1.0 / jnp.sqrt(jnp.sqrt(frob))
    k = []
    for i in range(7):
        total = jnp.full_like(e, ROOT_COEFFS[6] * math.comb(6, i))
        for j in range(5, i - 1, -1):
            total = total * e + math.comb(j, i) * ROOT_COEFFS[j]
        k.append(outer * total)
        outer = outer * a

    def inner(t, s):
        return k[4][s : s + 1, 0:1] * t[0] + k[5][s : s + 1, 0:1] * t[1] + k[6][s : s + 1, 0:1] * t[2]

    def outside(t, rows, start, s):
        i = lax.broadcasted_iota(jnp.int32, (HALF, BLOCK), 0) + start
        j = lax.broadcasted_iota(jnp.int32, (HALF, BLOCK), 1)
        lin = k[1][s : s + 1, 0:1] * t[0, rows] + k[2][s : s + 1, 0:1] * t[1, rows] + k[3][s : s + 1, 0:1] * t[2, rows]
        return lin + jnp.where(i == j, k[0][s : s + 1, 0:1], 0.0)

    left_rows = outside(left_t, own, core * HALF, 0) + dot3(split(left_t[2, own]), split(inner(left_t, 0)))
    y = dot3(split(left_rows), (g[0], g[1]))
    right_in = split(inner(right_t, 1))
    r0 = outside(right_t, LOW, 0, 1) + dot3(split(right_t[2, LOW]), right_in)
    r1 = outside(right_t, TOP, HALF, 1) + dot3(split(right_t[2, TOP]), right_in)
    z = dot3(split(y[:, :HALF]), split(r0)) + dot3(split(y[:, HALF:]), split(r1))
    mine[...] = z
    spread[...] = jnp.broadcast_to(lanes(z * z)[None], (devices, 1, 128))
    totals[...] = jnp.broadcast_to(grad_sq, (1, 128))


def unpack_stat(packed, out):
    sa, sc = unpack(packed[LOW, LOW], packed[HALF : HALF + 1, LOW])
    off = packed[LOW, TOP]
    out[LOW, LOW] = sa
    out[LOW, TOP] = off
    out[TOP, LOW] = off.T
    out[TOP, TOP] = sc


def place(pairs, *refs):
    direct, across = refs[:pairs], refs[pairs : 2 * pairs]
    sums, totals, owners, out, scaled, sems = refs[2 * pairs :]
    chip, core = chip_core()
    prec_sq = jnp.sum(jnp.sum(sums[...], axis=0), axis=1, keepdims=True)
    scale = jnp.sqrt(totals[0:1, 0:1] / (prec_sq + epsilon))
    copies = []
    for j in range(pairs):
        for half, src in ((core, direct[j]), (1 - core, across[j])):
            n = len(copies)
            scaled[n] = src[...] * scale
            start = pl.multiple_of(owners[0, chip ^ j] * BLOCK + half * HALF, HALF)
            copies.append(pltpu.make_async_copy(scaled.at[n], out.at[pl.ds(start, HALF)], sems.at[n]))
            copies[-1].start()
    for copy in copies:
        copy.wait()


def per_device(activations, out_grads, statistics, owner_blocks):
    rep_count = lax.axis_size("rep")
    pairs = rep_count // 2
    devices = rep_count * lax.axis_size("stripe")
    tokens = activations.shape[0]
    piece, square = (HALF, BLOCK), (BLOCK, BLOCK)
    unit = 6 * BLOCK**3

    shuffle = [(s * pairs + p, 2 * p + 1 - s) for s in range(2) for p in range(pairs)]
    send, keep = call(
        functools.partial(grad_terms, pairs),
        [(pairs,) + piece] * 2,
        [VMEM, VMEM, SMEM],
        flops=2 * tokens * pairs * BLOCK * BLOCK,
    )(activations, out_grads, owner_blocks)
    got = flip(send, 1)
    packed, trace = call(pack_stat, [(PACKED, BLOCK), (1, 128)], [VMEM])(statistics[0, 0])
    near = lax.ppermute(packed, "rep", shuffle)
    held = [(keep[j], got[j]) for j in range(pairs)]
    m = pairs // 2
    while m:
        arrived = [flip(sum(held[m + j]), 2 * m) for j in range(m)]
        held = [held[j] + (arrived[j],) for j in range(m)]
        m //= 2
    terms = held[0]
    a, b, c = terms[0], terms[1], sum(terms[2:])
    half, sums = call(
        functools.partial(finish_half, devices), [piece, (devices, 2, 128)], [VMEM] * 4
    )(a[None], b[None], c[None], trace)
    far = flip(near, 1)
    other = flip(half, 1)
    sums = lax.all_to_all(sums, AXES, 0, 0)
    left, right, out_packed = call(
        update_stats,
        [square, square, (PACKED, BLOCK)],
        [VMEM] * 4,
        [pltpu.VMEM((2,) + square, bf16)] * 2,
        flops=2 * unit,
    )(half, other, near, far)
    new_packed = lax.ppermute(out_packed, "rep", [(t, s) for s, t in shuffle])
    left_t, right_t, facts = call(
        stat_powers,
        [(3,) + square] * 2 + [(4, 128)],
        [VMEM] * 2,
        [pltpu.VMEM((2,) + square, bf16)] * 2,
        flops=4 * unit,
    )(left, right)
    mine, spread, totals = call(
        functools.partial(precondition, devices),
        [piece, (devices, 1, 128), (1, 128)],
        [VMEM] * 6,
        [pltpu.VMEM((2,) + square, bf16)],
        flops=3 * unit,
    )(half, other, left_t, right_t, facts, sums)

    direct, m = [mine], 1
    while m < pairs:
        direct = direct + [flip(x, 2 * m) for x in direct]
        m *= 2
    prec = lax.all_to_all(spread, AXES, 0, 0)
    across = [flip(x, 1) for x in direct]
    (new_stat,) = call(unpack_stat, [square], [VMEM])(new_packed)
    (placed,) = call(
        functools.partial(place, pairs),
        [(pairs * BLOCK, out_grads.shape[1])],
        [VMEM] * (2 * pairs + 2) + [SMEM],
        [pltpu.VMEM((2 * pairs,) + piece, f32), pltpu.SemaphoreType.DMA((2 * pairs,))],
        out_specs=[ANY],
    )(*direct, *across, prec, totals, owner_blocks)
    return placed, new_stat[None, None]


def solution(mesh):
    in_specs = (
        P("rep", None),
        P("rep", "stripe"),
        P("rep", "stripe", None, None),
        P("stripe", None),
    )
    out_specs = (P(None, "stripe"), P("rep", "stripe", None, None))
    return jax.shard_map(per_device, mesh=mesh, in_specs=in_specs, out_specs=out_specs, check_vma=False)
```

```python
import functools
import math

import jax
import jax.numpy as jnp
from jax import lax
from jax.experimental import pallas as pl
from jax.experimental.pallas import tpu as pltpu
from jax.sharding import PartitionSpec as P


BLOCK = 512
HALF = BLOCK // 2
PACKED = HALF + 8

decay_rate = 0.95
damping = 0.25
epsilon = 1e-06
AXES = ("rep", "stripe")
f32 = jnp.float32
bf16 = jnp.bfloat16

ROOT_COEFFS = (
    25 / 16,
    -5 / 16 - 3125 / 4096,
    3125 / 4096,
    -1250 / 4096,
    250 / 4096,
    -25 / 4096,
    1 / 4096,
)

VMEM = pl.BlockSpec(memory_space=pltpu.VMEM)
SMEM = pl.BlockSpec(memory_space=pltpu.SMEM)
HBM = pl.BlockSpec(memory_space=pltpu.HBM)
LOW = pl.ds(0, HALF)
TOP = pl.ds(HALF, HALF)


def call(body, out_shapes, in_specs, scratch=(), limit=24, flops=0, out_specs=None, **kwargs):
    return pl.pallas_call(
        body,
        out_shape=[s if isinstance(s, pl.MemoryRef) else jax.ShapeDtypeStruct(s, f32) for s in out_shapes],
        in_specs=in_specs,
        out_specs=out_specs or [VMEM] * len(out_shapes),
        scratch_shapes=list(scratch),
        compiler_params=pltpu.CompilerParams(vmem_limit_bytes=limit << 20),
        cost_estimate=pl.CostEstimate(flops=flops, bytes_accessed=1 << 20, transcendentals=0),
        **kwargs,
    )


def flip(x, mask):
    return lax.ppermute(x, "rep", [(i, i ^ mask) for i in range(lax.axis_size("rep"))])


def in_hbm(x):
    return pltpu.with_memory_space_constraint(x, pltpu.HBM)


def chip_core():
    me = lax.axis_index("rep")
    return lax.shift_right_logical(me, 1), lax.bitwise_and(me, 1)


def split(x):
    hi = x.astype(bf16)
    return hi, (x - hi.astype(f32)).astype(bf16)


def mm(a, b):
    return jnp.dot(a, b, preferred_element_type=f32)


def dot3(a, b):
    return mm(a[0], b[0]) + (mm(a[0], b[1]) + mm(a[1], b[0]))


def triangle():
    i = lax.broadcasted_iota(jnp.int32, (HALF, HALF), 0)
    j = lax.broadcasted_iota(jnp.int32, (HALF, HALF), 1)
    return i, j


def lanes(x):
    rows = jnp.sum(x, axis=0, keepdims=True)
    return sum(rows[:, k : k + 128] for k in range(0, x.shape[1], 128))


def pack_into(out, a, b, c):
    i, j = triangle()
    out[LOW, LOW] = jnp.where(i <= j, a, c)
    out[LOW, TOP] = b
    out[HALF:, LOW] = jnp.broadcast_to(jnp.sum(jnp.where(i == j, c, 0.0), axis=0, keepdims=True), (8, HALF))


def unpack(u, diag):
    i, j = triangle()
    ut = u.T
    return jnp.where(i <= j, u, ut), jnp.where(i > j, u, jnp.where(i < j, ut, diag))


def open_step(pairs, acts, grads, stat, owners, send, keep, out, trace, av, gv, sv, ov, sems):
    chip, core = chip_core()
    copies = [
        pltpu.make_async_copy(src, dst, sems.at[k])
        for k, (src, dst) in enumerate(((owners, ov), (acts, av), (grads, gv), (stat, sv)))
    ]
    for copy in copies:
        copy.start()
    for copy in copies[:3]:
        copy.wait()
    cotangent = gv[...]
    for res, half in ((send, 1 - core), (keep, core)):
        for j in range(pairs):
            start = ov[0, chip ^ j] * BLOCK + half * HALF
            cols = av[:, pl.ds(pl.multiple_of(start, HALF), HALF)]
            res[j] = lax.dot_general(cols, cotangent, (((0,), (0,)), ((), ())), preferred_element_type=f32)
    copies[3].wait()
    i, j = triangle()
    a, c = sv[LOW, LOW], sv[TOP, TOP]
    pack_into(out, a, sv[LOW, TOP], c)
    trace[...] = lanes(jnp.where(i == j, a + c, 0.0))


def finish_half(devices, keep, got, rest, trace, half, sums):
    total = keep[0] + got[0] + rest[...]
    half[...] = total
    both = jnp.concatenate([lanes(total * total), trace[...]], axis=0)
    sums[...] = jnp.broadcast_to(both[None], (devices, 2, 128))


def update_stats(half, other, near, far, left, right, out, g, gt):
    _, core = chip_core()
    mine = pl.ds(pl.multiple_of(core * HALF, HALF), HALF)
    theirs = pl.ds(pl.multiple_of(HALF - core * HALF, HALF), HALF)
    for rows, src in ((mine, half), (theirs, other)):
        g[0, rows], g[1, rows] = split(src[...])
    for k in range(2):
        gt[k] = g[k].T
    for side, res, a, b in ((0, left, g, gt), (1, right, gt, g)):
        old = lambda r, c: jnp.where(core == side, far[r, c], near[r, c])
        a0 = (a[0, LOW], a[1, LOW])
        a1 = (a[0, TOP], a[1, TOP])
        top = dot3(a0, (b[0], b[1]))
        corner = dot3(a1, (b[0, :, TOP], b[1, :, TOP]))
        sa, sc = unpack(old(LOW, LOW), old(pl.ds(HALF, 1), LOW))
        res[LOW, LOW] = decay_rate * sa + top[:, :HALF]
        off = decay_rate * old(LOW, TOP) + top[:, HALF:]
        res[LOW, TOP] = off
        res[TOP, LOW] = off.T
        res[TOP, TOP] = decay_rate * sc + corner

    @pl.when(core == 1)
    def _():
        pack_into(out, left[LOW, LOW], left[LOW, TOP], left[TOP, TOP])

    @pl.when(core == 0)
    def _():
        pack_into(out, right[LOW, LOW], right[LOW, TOP], right[TOP, TOP])


def symmetric_product(a, b, out):
    top = dot3((a[0, LOW], a[1, LOW]), (b[0], b[1]))
    out[LOW] = top
    out[TOP, TOP] = dot3((a[0, TOP], a[1, TOP]), (b[0, :, TOP], b[1, :, TOP]))
    out[TOP, LOW] = top[:, HALF:].T


def stat_powers(left, right, left_out, right_out, facts, left_t, right_t, s1, s2, sems):
    i, j = triangle()
    norms, traces, copies = [], [], []

    def keep(t, k, dst):
        copies.append(pltpu.make_async_copy(t.at[k], dst.at[k], sems.at[len(copies)]))
        copies[-1].start()

    for stat, t, dst in ((left, left_t, left_out), (right, right_t, right_out)):
        x = stat[...]
        norm_sq = jnp.sum(jnp.sum(x * x, axis=0, keepdims=True), axis=1, keepdims=True)
        diag = jnp.where(i == j, stat[LOW, LOW] + stat[TOP, TOP], 0.0)
        norms.append(norm_sq)
        traces.append(jnp.sum(jnp.sum(diag, axis=0, keepdims=True), axis=1, keepdims=True))
        t1 = x * (1.0 / jnp.sqrt(norm_sq + epsilon))
        t[0] = t1
        keep(t, 0, dst)
        s1[0], s1[1] = split(t1)
        symmetric_product(s1, s1, t.at[1])
        keep(t, 1, dst)
        s2[0], s2[1] = split(t[1])
        symmetric_product(s1, s2, t.at[2])
        keep(t, 2, dst)
    facts[...] = jnp.concatenate([jnp.broadcast_to(x, (1, 128)) for x in norms + traces], axis=0)
    for copy in copies:
        copy.wait()


def precondition(devices, half, other, left_in, right_in_hbm, facts, sums, mine, spread, totals, g, left_t, right_t, sems):
    _, core = chip_core()
    copies = [
        pltpu.make_async_copy(src.at[k], dst.at[k], sems.at[3 * n + k])
        for n, (src, dst) in enumerate(((left_in, left_t), (right_in_hbm, right_t)))
        for k in range(3)
    ]
    for copy in copies:
        copy.start()
    own = pl.ds(pl.multiple_of(core * HALF, HALF), HALF)
    theirs = pl.ds(pl.multiple_of(HALF - core * HALF, HALF), HALF)
    for rows, src in ((own, half), (theirs, other)):
        g[0, rows], g[1, rows] = split(src[...])
    both = jnp.sum(jnp.sum(sums[...], axis=0), axis=1, keepdims=True)
    grad_sq, trace = both[0:1], both[1:2]
    shift = (decay_rate * trace + 2.0 * grad_sq) * (damping / (devices * BLOCK))
    norm_sq, traces = facts[0:2, :], facts[2:4, :]
    shift = jnp.broadcast_to(shift, (2, 128))
    frob = jnp.sqrt(norm_sq + 2.0 * shift * traces + BLOCK * shift * shift + epsilon)
    a = jnp.sqrt(norm_sq + epsilon) / frob
    e = shift / frob
    outer = 1.0 / jnp.sqrt(jnp.sqrt(frob))
    k = []
    for i in range(7):
        total = jnp.full_like(e, ROOT_COEFFS[6] * math.comb(6, i))
        for j in range(5, i - 1, -1):
            total = total * e + math.comb(j, i) * ROOT_COEFFS[j]
        k.append(outer * total)
        outer = outer * a

    def inner(t, s):
        return k[4][s : s + 1, 0:1] * t[0] + k[5][s : s + 1, 0:1] * t[1] + k[6][s : s + 1, 0:1] * t[2]

    def outside(t, rows, start, s):
        i = lax.broadcasted_iota(jnp.int32, (HALF, BLOCK), 0) + start
        j = lax.broadcasted_iota(jnp.int32, (HALF, BLOCK), 1)
        lin = k[1][s : s + 1, 0:1] * t[0, rows] + k[2][s : s + 1, 0:1] * t[1, rows] + k[3][s : s + 1, 0:1] * t[2, rows]
        return lin + jnp.where(i == j, k[0][s : s + 1, 0:1], 0.0)

    for copy in copies[:3]:
        copy.wait()
    left_rows = outside(left_t, own, core * HALF, 0) + dot3(split(left_t[2, own]), split(inner(left_t, 0)))
    y = dot3(split(left_rows), (g[0], g[1]))
    for copy in copies[3:]:
        copy.wait()
    right_in = split(inner(right_t, 1))
    r0 = outside(right_t, LOW, 0, 1) + dot3(split(right_t[2, LOW]), right_in)
    r1 = outside(right_t, TOP, HALF, 1) + dot3(split(right_t[2, TOP]), right_in)
    z = dot3(split(y[:, :HALF]), split(r0)) + dot3(split(y[:, HALF:]), split(r1))
    mine[...] = z
    spread[...] = jnp.broadcast_to(lanes(z * z)[None], (devices, 1, 128))
    totals[...] = jnp.broadcast_to(grad_sq, (1, 128))


def unpack_stat(packed, out):
    sa, sc = unpack(packed[LOW, LOW], packed[HALF : HALF + 1, LOW])
    off = packed[LOW, TOP]
    out[LOW, LOW] = sa
    out[LOW, TOP] = off
    out[TOP, LOW] = off.T
    out[TOP, TOP] = sc


def write_pieces(chip, core, pieces, scale, owners, out, scaled, sems):
    copies = []
    for n, (j, swapped, src) in enumerate(pieces):
        scaled[n] = src[...] * scale
        half = 1 - core if swapped else core
        start = pl.multiple_of(owners[0, chip ^ j] * BLOCK + half * HALF, HALF)
        copies.append(pltpu.make_async_copy(scaled.at[n], out.at[pl.ds(start, HALF)], sems.at[n]))
        copies[-1].start()
    for copy in copies:
        copy.wait()


def place_near(direct, across, sums, totals, owners, out, scale, scaled, sems):
    chip, core = chip_core()
    prec_sq = jnp.sum(jnp.sum(sums[...], axis=0), axis=1, keepdims=True)
    factor = jnp.sqrt(totals[0:1, 0:1] / (prec_sq + epsilon))
    scale[...] = jnp.broadcast_to(factor, (1, 128))
    write_pieces(chip, core, ((0, False, direct), (0, True, across)), factor, owners, out, scaled, sems)


def place_far(count, *refs):
    direct, across = refs[:count], refs[count : 2 * count]
    scale, owners, _, out, scaled, sems = refs[2 * count :]
    chip, core = chip_core()
    pieces = [(j + 1, False, x) for j, x in enumerate(direct)] + [(j + 1, True, x) for j, x in enumerate(across)]
    write_pieces(chip, core, pieces, scale[0:1, 0:1], owners, out, scaled, sems)


def per_device(activations, out_grads, statistics, owner_blocks):
    rep_count = lax.axis_size("rep")
    pairs = rep_count // 2
    devices = rep_count * lax.axis_size("stripe")
    tokens = activations.shape[0]
    piece, square = (HALF, BLOCK), (BLOCK, BLOCK)
    unit = 6 * BLOCK**3

    shuffle = [(s * pairs + p, 2 * p + 1 - s) for s in range(2) for p in range(pairs)]
    send, keep, packed, trace = call(
        functools.partial(open_step, pairs),
        [(pairs,) + piece] * 2 + [(PACKED, BLOCK), (1, 128)],
        [HBM] * 4,
        [
            pltpu.VMEM(activations.shape, bf16),
            pltpu.VMEM(out_grads.shape, bf16),
            pltpu.VMEM(square, f32),
            pltpu.SMEM(owner_blocks.shape, jnp.int32),
            pltpu.SemaphoreType.DMA((4,)),
        ],
        flops=2 * tokens * pairs * BLOCK * BLOCK,
    )(*(in_hbm(x) for x in (activations, out_grads, statistics[0, 0], owner_blocks)))
    got = flip(send, 1)
    near = lax.ppermute(packed, "rep", shuffle)
    m = pairs // 2
    held = [None] * pairs
    while m:
        outgoing = [keep[m + j] + got[m + j] for j in range(m)]
        outgoing = [x if held[m + j] is None else x + held[m + j] for j, x in enumerate(outgoing)]
        arrived = [flip(x, 2 * m) for x in outgoing]
        held = [x if held[j] is None else x + held[j] for j, x in enumerate(arrived)]
        m //= 2
    half, sums = call(
        functools.partial(finish_half, devices), [piece, (devices, 2, 128)], [VMEM] * 4
    )(keep, got, held[0], trace)
    far = flip(near, 1)
    other = flip(half, 1)
    sums = lax.all_to_all(sums, AXES, 0, 0)
    left, right, out_packed = call(
        update_stats,
        [square, square, (PACKED, BLOCK)],
        [VMEM] * 4,
        [pltpu.VMEM((2,) + square, bf16)] * 2,
        flops=2 * unit,
    )(half, other, near, far)
    new_packed = lax.ppermute(out_packed, "rep", [(t, s) for s, t in shuffle])
    left_t, right_t, facts = call(
        stat_powers,
        [pltpu.HBM((3,) + square, f32)] * 2 + [(4, 128)],
        [VMEM] * 2,
        [pltpu.VMEM((3,) + square, f32)] * 2 + [pltpu.VMEM((2,) + square, bf16)] * 2 + [pltpu.SemaphoreType.DMA((6,))],
        flops=4 * unit,
        out_specs=[HBM, HBM, VMEM],
    )(left, right)
    mine, spread, totals = call(
        functools.partial(precondition, devices),
        [piece, (devices, 1, 128), (1, 128)],
        [VMEM, VMEM, HBM, HBM, VMEM, VMEM],
        [pltpu.VMEM((2,) + square, bf16)] + [pltpu.VMEM((3,) + square, f32)] * 2 + [pltpu.SemaphoreType.DMA((6,))],
        flops=3 * unit,
    )(half, other, in_hbm(left_t), in_hbm(right_t), facts, sums)

    direct, m = [mine], 1
    while m < pairs:
        direct = direct + [flip(x, 2 * m) for x in direct]
        m *= 2
    across = [flip(mine, 1)]
    prec = lax.all_to_all(spread, AXES, 0, 0)
    (new_stat,) = call(unpack_stat, [square], [VMEM])(new_packed)
    slab = (pairs * BLOCK, out_grads.shape[1])
    placed, scale = call(
        place_near,
        [slab, (1, 128)],
        [VMEM] * 4 + [SMEM],
        [pltpu.VMEM((2,) + piece, f32), pltpu.SemaphoreType.DMA((2,))],
        out_specs=[HBM, VMEM],
    )(mine, across[0], prec, totals, owner_blocks)
    across = [flip(x, 1) for x in direct[1:]]
    count = pairs - 1
    (placed,) = call(
        functools.partial(place_far, count),
        [slab],
        [VMEM] * (2 * count + 1) + [SMEM, HBM],
        [pltpu.VMEM((2 * count,) + piece, f32), pltpu.SemaphoreType.DMA((2 * count,))],
        out_specs=[HBM],
        input_output_aliases={2 * count + 2: 0},
    )(*direct[1:], *across, scale, owner_blocks, placed)
    return placed, new_stat[None, None]


def solution(mesh):
    in_specs = (
        P("rep", None),
        P("rep", "stripe"),
        P("rep", "stripe", None, None),
        P("stripe", None),
    )
    out_specs = (P(None, "stripe"), P("rep", "stripe", None, None))
    return jax.shard_map(per_device, mesh=mesh, in_specs=in_specs, out_specs=out_specs, check_vma=False)
```

```python
import functools
import math

import jax
import jax.numpy as jnp
from jax import lax
from jax.experimental import pallas as pl
from jax.experimental.pallas import tpu as pltpu
from jax.sharding import PartitionSpec as P


BLOCK = 512
HALF = BLOCK // 2
PACKED = HALF + 8

decay_rate = 0.95
damping = 0.25
epsilon = 1e-06
AXES = ("rep", "stripe")
f32 = jnp.float32
bf16 = jnp.bfloat16

ROOT_COEFFS = (
    25 / 16,
    -5 / 16 - 3125 / 4096,
    3125 / 4096,
    -1250 / 4096,
    250 / 4096,
    -25 / 4096,
    1 / 4096,
)

VMEM = pl.BlockSpec(memory_space=pltpu.VMEM)
SMEM = pl.BlockSpec(memory_space=pltpu.SMEM)
HBM = pl.BlockSpec(memory_space=pltpu.HBM)
LOW = pl.ds(0, HALF)
TOP = pl.ds(HALF, HALF)


def call(body, out_shapes, in_specs, scratch=(), limit=16, flops=0, out_specs=None, **kwargs):
    return pl.pallas_call(
        body,
        out_shape=[jax.ShapeDtypeStruct(s, f32) if isinstance(s, tuple) else s for s in out_shapes],
        in_specs=in_specs,
        out_specs=out_specs or [VMEM] * len(out_shapes),
        scratch_shapes=list(scratch),
        compiler_params=pltpu.CompilerParams(vmem_limit_bytes=limit << 20),
        cost_estimate=pl.CostEstimate(flops=flops, bytes_accessed=1 << 20, transcendentals=0),
        **kwargs,
    )


def flip(x, mask):
    return lax.ppermute(x, "rep", [(i, i ^ mask) for i in range(lax.axis_size("rep"))])


def in_hbm(x):
    return pltpu.with_memory_space_constraint(x, pltpu.HBM)


def chip_core():
    me = lax.axis_index("rep")
    return lax.shift_right_logical(me, 1), lax.bitwise_and(me, 1)


def split(x):
    hi = x.astype(bf16)
    return hi, (x - hi.astype(f32)).astype(bf16)


def mm(a, b):
    return jnp.dot(a, b, preferred_element_type=f32)


def dot3(a, b):
    return mm(a[0], b[0]) + (mm(a[0], b[1]) + mm(a[1], b[0]))


def triangle():
    i = lax.broadcasted_iota(jnp.int32, (HALF, HALF), 0)
    j = lax.broadcasted_iota(jnp.int32, (HALF, HALF), 1)
    return i, j


def lanes(x):
    rows = jnp.sum(x, axis=0, keepdims=True)
    return sum(rows[:, k : k + 128] for k in range(0, x.shape[1], 128))


def pack_into(out, a, b, c):
    i, j = triangle()
    out[LOW, LOW] = jnp.where(i <= j, a, c)
    out[LOW, TOP] = b
    out[HALF:, LOW] = jnp.broadcast_to(jnp.sum(jnp.where(i == j, c, 0.0), axis=0, keepdims=True), (8, HALF))


def unpack(u, diag):
    i, j = triangle()
    ut = u.T
    return jnp.where(i <= j, u, ut), jnp.where(i > j, u, jnp.where(i < j, ut, diag))


def pack_stat(stat, out, trace):
    i, j = triangle()
    a, c = stat[LOW, LOW], stat[TOP, TOP]
    pack_into(out, a, stat[LOW, TOP], c)
    trace[...] = lanes(jnp.where(i == j, a + c, 0.0))


def grad_terms(plan, acts, grads, owners, *refs):
    outs, (av, gv, ov, sems) = refs[: len(plan)], refs[len(plan) :]
    chip, core = chip_core()
    copies = [
        pltpu.make_async_copy(src, dst, sems.at[k]) for k, (src, dst) in enumerate(((owners, ov), (acts, av), (grads, gv)))
    ]
    for copy in copies:
        copy.start()
    for copy in copies:
        copy.wait()
    cotangent = gv[...]
    for out, (chips, swapped) in zip(outs, plan):
        half = 1 - core if swapped else core
        for n, j in enumerate(chips):
            start = ov[0, chip ^ j] * BLOCK + half * HALF
            cols = av[:, pl.ds(pl.multiple_of(start, HALF), HALF)]
            out[n] = lax.dot_general(cols, cotangent, (((0,), (0,)), ((), ())), preferred_element_type=f32)


def finish_half(devices, keep, got, rest, trace, half, sums):
    value = keep[0] + got[0] + rest[...]
    half[...] = value
    both = jnp.concatenate([lanes(value * value), trace[...]], axis=0)
    sums[...] = jnp.broadcast_to(both[None], (devices, 2, 128))


def spread(top, corner, out):
    out[0, LOW], out[1, LOW] = split(top)
    out[0, TOP, TOP], out[1, TOP, TOP] = split(corner)
    for k in range(2):
        out[k, TOP, LOW] = out[k, LOW, TOP].T


def upper_product(a, b):
    top = dot3((a[0, LOW], a[1, LOW]), (b[0], b[1]))
    return top, dot3((a[0, TOP], a[1, TOP]), (b[0, :, TOP], b[1, :, TOP]))


def total(x):
    return jnp.sum(jnp.sum(x, axis=0, keepdims=True), axis=1, keepdims=True)


def load_gradient(core, half, other, g):
    mine = pl.ds(pl.multiple_of(core * HALF, HALF), HALF)
    theirs = pl.ds(pl.multiple_of(HALF - core * HALF, HALF), HALF)
    for rows, src in ((mine, half), (theirs, other)):
        g[0, rows], g[1, rows] = split(src[...])


def update_powers(half, other, old, tops, corners, facts, out, g_out, gg, s1, s2, stage, sems):
    _, core = chip_core()
    load_gradient(core, half, other, gg.at[0])
    keep = pltpu.make_async_copy(gg.at[0], g_out, sems.at[0])
    keep.start()
    for k in range(2):
        gg[1, k] = gg[0, k].T
    top, corner = upper_product(gg.at[1 - core], gg.at[core])
    sa, sc = unpack(old[LOW, LOW], old[HALF : HALF + 1, LOW])
    s00 = decay_rate * sa + top[:, :HALF]
    s01 = decay_rate * old[LOW, TOP] + top[:, HALF:]
    s11 = decay_rate * sc + corner
    pack_into(stage, s00, s01, s11)
    copy = pltpu.make_async_copy(stage, out, sems.at[1])
    copy.start()
    i, j = triangle()
    trace = total(jnp.where(i == j, s00 + s11, 0.0))
    norm_sq = total(s00 * s00 + s11 * s11 + 2.0 * (s01 * s01))
    inv = 1.0 / jnp.sqrt(norm_sq + epsilon)
    tops[0, :, LOW], tops[0, :, TOP], corners[0] = s00 * inv, s01 * inv, s11 * inv
    spread(tops[0], corners[0], s1)
    tops[1], corners[1] = upper_product(s1, s1)
    spread(tops[1], corners[1], s2)
    tops[2], corners[2] = upper_product(s1, s2)
    facts[...] = jnp.concatenate([jnp.broadcast_to(x, (1, 128)) for x in (norm_sq, trace)], axis=0)
    keep.wait()
    copy.wait()


def coefficients(devices, facts, sums):
    both = jnp.sum(jnp.sum(sums[...], axis=0), axis=1, keepdims=True)
    grad_sq, trace_all = both[0:1], both[1:2]
    shift = (decay_rate * trace_all + 2.0 * grad_sq) * (damping / (devices * BLOCK))
    shift = jnp.broadcast_to(shift, (1, 128))
    norm_sq, trace = facts[0:1, :], facts[1:2, :]
    frob = jnp.sqrt(norm_sq + 2.0 * shift * trace + BLOCK * shift * shift + epsilon)
    a = jnp.sqrt(norm_sq + epsilon) / frob
    e = shift / frob
    outer = 1.0 / jnp.sqrt(jnp.sqrt(frob))
    k = []
    for i in range(7):
        value = jnp.full_like(e, ROOT_COEFFS[6] * math.comb(6, i))
        for j in range(5, i - 1, -1):
            value = value * e + math.comb(j, i) * ROOT_COEFFS[j]
        k.append((outer * value)[:, 0:1])
        outer = outer * a
    return k, grad_sq


def root(devices, tops, corners, facts, sums, out, totals, inner, cube):
    k, grad_sq = coefficients(devices, facts, sums)
    spread(tops[2], corners[2], cube)
    spread(*(k[4] * t[0] + k[5] * t[1] + k[6] * t[2] for t in (tops, corners)), inner)
    top, corner = upper_product(cube, inner)
    i, j = triangle()
    diag = jnp.where(i == j, k[0], 0.0)
    low = k[1] * tops[0] + k[2] * tops[1] + k[3] * tops[2] + top
    out[LOW, LOW] = low[:, :HALF] + diag
    out[LOW, TOP] = low[:, HALF:]
    corner = k[1] * corners[0] + k[2] * corners[1] + k[3] * corners[2] + corner + diag
    out[HALF:, LOW] = corner[: HALF // 2]
    out[HALF:, TOP] = corner[HALF // 2 :]
    totals[...] = jnp.broadcast_to(grad_sq, (1, 128))


def root_corner(packed):
    return jnp.concatenate([packed[HALF:, LOW], packed[HALF:, TOP]], axis=0)


def half_way(g_in, packed, out, g, x, sem):
    _, core = chip_core()
    copy = pltpu.make_async_copy(g_in, g, sem)
    copy.start()
    spread(packed[LOW], root_corner(packed), x)
    copy.wait()

    @pl.when(core == 1)
    def _():
        y = dot3((x[0, TOP], x[1, TOP]), (g[0], g[1]))
        out[0, LOW], out[1, LOW] = split(y)

    @pl.when(core == 0)
    def _():
        out[0], out[1] = split(dot3((g[0], g[1]), (x[0], x[1])))


def last_product(middle, packed, mine, sums, x):
    _, core = chip_core()

    @pl.when(core == 1)
    def _():
        spread(packed[LOW], root_corner(packed), x)
        mine[...] = dot3((middle[0, LOW], middle[1, LOW]), (x[0], x[1]))

    @pl.when(core == 0)
    def _():
        mine[...] = dot3(split(packed[LOW]), (middle[0], middle[1]))

    sums[...] = lanes(mine[...] * mine[...])


def unpack_stat(source, out, packed, sem):
    copy = pltpu.make_async_copy(source, packed, sem)
    copy.start()
    copy.wait()
    sa, sc = unpack(packed[LOW, LOW], packed[HALF : HALF + 1, LOW])
    off = packed[LOW, TOP]
    out[LOW, LOW] = sa
    out[LOW, TOP] = off
    out[TOP, LOW] = off.T
    out[TOP, TOP] = sc


def write_pieces(chip, core, pieces, scale, owners, out, scaled, sems):
    copies = []
    for n, (j, swapped, src) in enumerate(pieces):
        scaled[n] = src[...] * scale
        half = 1 - core if swapped else core
        start = pl.multiple_of(owners[0, chip ^ j] * BLOCK + half * HALF, HALF)
        copies.append(pltpu.make_async_copy(scaled.at[n], out.at[pl.ds(start, HALF)], sems.at[n]))
        copies[-1].start()
    for copy in copies:
        copy.wait()


def place_near(direct, across, sums, totals, owners, out, scale, scaled, sems):
    chip, core = chip_core()
    prec_sq = jnp.sum(jnp.sum(sums[...], axis=0), axis=1, keepdims=True)
    factor = jnp.sqrt(totals[0:1, 0:1] / (prec_sq + epsilon))
    scale[...] = jnp.broadcast_to(factor, (1, 128))
    write_pieces(chip, core, ((0, False, direct), (0, True, across)), factor, owners, out, scaled, sems)


def place_far(count, *refs):
    direct, across = refs[:count], refs[count : 2 * count]
    scale, owners, _, out, scaled, sems = refs[2 * count :]
    chip, core = chip_core()
    pieces = [(j + 1, False, x) for j, x in enumerate(direct)] + [(j + 1, True, x) for j, x in enumerate(across)]
    write_pieces(chip, core, pieces, scale[0:1, 0:1], owners, out, scaled, sems)


def per_device(activations, out_grads, statistics, owner_blocks):
    rep_count = lax.axis_size("rep")
    pairs = rep_count // 2
    devices = rep_count * lax.axis_size("stripe")
    tokens = activations.shape[0]
    piece, square = (HALF, BLOCK), (BLOCK, BLOCK)
    unit = 6 * BLOCK**3

    whole = jax.ShapeDtypeStruct((2,) + square, bf16)
    split_square = pltpu.VMEM((2,) + square, bf16)
    packed_buffer = pltpu.VMEM((PACKED, BLOCK), f32)
    m = pairs // 2

    def terms(*plan):
        return call(
            functools.partial(grad_terms, plan),
            [(len(chips),) + piece for chips, _ in plan],
            [HBM] * 3,
            [
                pltpu.VMEM(activations.shape, bf16),
                pltpu.VMEM(out_grads.shape, bf16),
                pltpu.SMEM(owner_blocks.shape, jnp.int32),
                pltpu.SemaphoreType.DMA((3,)),
            ],
            flops=2 * tokens * HALF * BLOCK * sum(len(chips) for chips, _ in plan),
        )(*(in_hbm(x) for x in (activations, out_grads, owner_blocks)))

    upper, lower = range(m, pairs), range(m)
    (send_far,) = terms((upper, True))
    got_far = flip(send_far, 1)
    keep_far, send_near, keep_near = terms((upper, False), (lower, True), (lower, False))
    got_near = flip(send_near, 1)
    arrived = [flip(keep_far[j] + got_far[j], 2 * m) for j in range(m)]
    while m > 1:
        m //= 2
        held = [keep_near[j] + got_near[j] + arrived[j] for j in range(m, 2 * m)]
        arrived = [x + flip(y, 2 * m) for x, y in zip(arrived, held)]
    shuffle = [(s * pairs + p, 2 * p + 1 - s) for s in range(2) for p in range(pairs)]
    packed, trace = call(pack_stat, [(PACKED, BLOCK), (1, 128)], [VMEM])(statistics[0, 0])
    old = lax.ppermute(packed, "rep", shuffle)
    half, sums = call(
        functools.partial(finish_half, devices), [piece, (devices, 2, 128)], [VMEM] * 4
    )(keep_near, got_near, arrived[0], trace)
    other = flip(half, 1)
    sums = lax.all_to_all(sums, AXES, 0, 0)
    tops, corners, facts, out_packed, g_split = call(
        update_powers,
        [(3,) + piece, (3, HALF, HALF), (2, 128), pltpu.HBM((PACKED, BLOCK), f32), pltpu.HBM((2,) + square, bf16)],
        [VMEM] * 3,
        [pltpu.VMEM((2, 2) + square, bf16), split_square, split_square]
        + [packed_buffer, pltpu.SemaphoreType.DMA((2,))],
        flops=3 * unit,
        out_specs=[VMEM] * 3 + [HBM] * 2,
    )(half, other, old)
    new_packed = lax.ppermute(out_packed, "rep", [(t, s) for s, t in shuffle])
    mine_root, totals = call(
        functools.partial(root, devices),
        [(HALF + HALF // 2, BLOCK), (1, 128)],
        [VMEM] * 4,
        [split_square] * 2,
        flops=unit,
    )(tops, corners, facts, sums)
    other_root = flip(mine_root, 1)
    (middle,) = call(half_way, [whole], [HBM, VMEM], [split_square] * 2 + [pltpu.SemaphoreType.DMA], flops=unit)(
        in_hbm(g_split), mine_root
    )
    mine, prec = call(last_product, [piece, (1, 128)], [VMEM] * 2, [split_square], flops=unit)(middle, other_root)

    bit = 1
    while bit < rep_count:
        masks = [x for x in (3 * bit, 2 * bit, bit) if x < rep_count]
        prec = sum((flip(prec, x) for x in masks), prec)
        bit *= 4
    direct, m = [mine], 1
    while m < pairs:
        direct = direct + [flip(x, 2 * m) for x in direct]
        m *= 2
    across = [flip(mine, 1)]
    stripes = lax.axis_size("stripe")
    prec = lax.all_to_all(jnp.broadcast_to(prec[None], (stripes, 1, 128)), "stripe", 0, 0)
    (new_stat,) = call(unpack_stat, [square], [HBM], [packed_buffer, pltpu.SemaphoreType.DMA])(in_hbm(new_packed))
    slab = (pairs * BLOCK, out_grads.shape[1])
    placed, scale = call(
        place_near,
        [slab, (1, 128)],
        [VMEM] * 4 + [SMEM],
        [pltpu.VMEM((2,) + piece, f32), pltpu.SemaphoreType.DMA((2,))],
        out_specs=[HBM, VMEM],
    )(mine, across[0], prec, totals, owner_blocks)
    across = [flip(x, 1) for x in direct[1:]]
    count = pairs - 1
    (placed,) = call(
        functools.partial(place_far, count),
        [slab],
        [VMEM] * (2 * count + 1) + [SMEM, HBM],
        [pltpu.VMEM((2 * count,) + piece, f32), pltpu.SemaphoreType.DMA((2 * count,))],
        out_specs=[HBM],
        input_output_aliases={2 * count + 2: 0},
    )(*direct[1:], *across, scale, owner_blocks, placed)
    return placed, new_stat[None, None]


def solution(mesh):
    in_specs = (
        P("rep", None),
        P("rep", "stripe"),
        P("rep", "stripe", None, None),
        P("stripe", None),
    )
    out_specs = (P(None, "stripe"), P("rep", "stripe", None, None))
    return jax.shard_map(per_device, mesh=mesh, in_specs=in_specs, out_specs=out_specs, check_vma=False)
```

```python
import functools
import math

import jax
import jax.numpy as jnp
from jax import lax
from jax.experimental import pallas as pl
from jax.experimental.pallas import tpu as pltpu
from jax.sharding import PartitionSpec as P


BLOCK = 512
HALF = BLOCK // 2
PACKED = HALF + 8
CHUNK = 64

decay_rate = 0.95
damping = 0.25
epsilon = 1e-06
AXES = ("rep", "stripe")
f32 = jnp.float32
bf16 = jnp.bfloat16

ROOT_COEFFS = (
    25 / 16,
    -5 / 16 - 3125 / 4096,
    3125 / 4096,
    -1250 / 4096,
    250 / 4096,
    -25 / 4096,
    1 / 4096,
)

VMEM = pl.BlockSpec(memory_space=pltpu.VMEM)
SMEM = pl.BlockSpec(memory_space=pltpu.SMEM)
HBM = pl.BlockSpec(memory_space=pltpu.HBM)
LOW = pl.ds(0, HALF)
TOP = pl.ds(HALF, HALF)


def call(body, out_shapes, in_specs, scratch=(), limit=16, flops=0, out_specs=None, **kwargs):
    return pl.pallas_call(
        body,
        out_shape=[jax.ShapeDtypeStruct(s, f32) if isinstance(s, tuple) else s for s in out_shapes],
        in_specs=in_specs,
        out_specs=out_specs or [VMEM] * len(out_shapes),
        scratch_shapes=list(scratch),
        compiler_params=pltpu.CompilerParams(vmem_limit_bytes=limit << 20),
        cost_estimate=pl.CostEstimate(flops=flops, bytes_accessed=1 << 20, transcendentals=0),
        **kwargs,
    )


def flip(x, mask):
    return lax.ppermute(x, "rep", [(i, i ^ mask) for i in range(lax.axis_size("rep"))])


def in_hbm(x):
    return pltpu.with_memory_space_constraint(x, pltpu.HBM)


def chip_core():
    me = lax.axis_index("rep")
    return lax.shift_right_logical(me, 1), lax.bitwise_and(me, 1)


def split(x):
    hi = x.astype(bf16)
    return hi, (x - hi.astype(f32)).astype(bf16)


def mm(a, b):
    return jnp.dot(a, b, preferred_element_type=f32)


def dot3(a, b):
    return mm(a[0], b[0]) + (mm(a[0], b[1]) + mm(a[1], b[0]))


def triangle():
    i = lax.broadcasted_iota(jnp.int32, (HALF, HALF), 0)
    j = lax.broadcasted_iota(jnp.int32, (HALF, HALF), 1)
    return i, j


def lanes(x):
    rows = jnp.sum(x, axis=0, keepdims=True)
    return sum(rows[:, k : k + 128] for k in range(0, x.shape[1], 128))


def pack_into(out, a, b, c):
    i, j = triangle()
    out[LOW, LOW] = jnp.where(i <= j, a, c)
    out[LOW, TOP] = b
    out[HALF:, LOW] = jnp.broadcast_to(jnp.sum(jnp.where(i == j, c, 0.0), axis=0, keepdims=True), (8, HALF))


def unpack(u, diag):
    i, j = triangle()
    ut = u.T
    return jnp.where(i <= j, u, ut), jnp.where(i > j, u, jnp.where(i < j, ut, diag))


def pack_stat(stat, out, trace):
    i, j = triangle()
    a, c = stat[LOW, LOW], stat[TOP, TOP]
    pack_into(out, a, stat[LOW, TOP], c)
    trace[...] = lanes(jnp.where(i == j, a + c, 0.0))


def grad_terms(plan, acts, grads, owners, *refs):
    outs, (av, gv, ov, sems) = refs[: len(plan)], refs[len(plan) :]
    chip, core = chip_core()
    copies = [
        pltpu.make_async_copy(src, dst, sems.at[k]) for k, (src, dst) in enumerate(((owners, ov), (acts, av), (grads, gv)))
    ]
    for copy in copies:
        copy.start()
    for copy in copies:
        copy.wait()
    cotangent = gv[...]
    for out, (chips, swapped) in zip(outs, plan):
        half = 1 - core if swapped else core
        for n, j in enumerate(chips):
            start = ov[0, chip ^ j] * BLOCK + half * HALF
            cols = av[:, pl.ds(pl.multiple_of(start, HALF), HALF)]
            out[n] = lax.dot_general(cols, cotangent, (((0,), (0,)), ((), ())), preferred_element_type=f32)


def finish_half(devices, keep, got, rest, trace, half, sums):
    value = keep[0] + got[0] + rest[...]
    half[...] = value
    both = jnp.concatenate([lanes(value * value), trace[...]], axis=0)
    sums[...] = jnp.broadcast_to(both[None], (devices, 2, 128))


def spread(top, corner, out):
    out[0, LOW], out[1, LOW] = split(top)
    out[0, TOP, TOP], out[1, TOP, TOP] = split(corner)
    for k in range(2):
        out[k, TOP, LOW] = out[k, LOW, TOP].T


def upper_product(a, b):
    top = dot3((a[0, LOW], a[1, LOW]), (b[0], b[1]))
    return top, dot3((a[0, TOP], a[1, TOP]), (b[0, :, TOP], b[1, :, TOP]))


def total(x):
    return jnp.sum(jnp.sum(x, axis=0, keepdims=True), axis=1, keepdims=True)


def load_gradient(core, half, other, g):
    mine = pl.ds(pl.multiple_of(core * HALF, HALF), HALF)
    theirs = pl.ds(pl.multiple_of(HALF - core * HALF, HALF), HALF)
    for rows, src in ((mine, half), (theirs, other)):
        g[0, rows], g[1, rows] = split(src[...])


def update_powers(half, other, old, *refs):
    top_out, corner_out, cube_top, cube_corner, facts, out, g_out = refs[:7]
    gg, s1, s2, stage, tops, corners, sems = refs[7:]
    _, core = chip_core()

    def store(k):
        for n, (src, dst) in enumerate(((tops, top_out), (corners, corner_out))):
            copies.append(pltpu.make_async_copy(src.at[k], dst.at[k], sems.at[2 + 2 * k + n]))
            copies[-1].start()

    load_gradient(core, half, other, gg.at[0])
    copies = [pltpu.make_async_copy(gg.at[0], g_out, sems.at[0])]
    copies[0].start()
    for k in range(2):
        gg[1, k] = gg[0, k].T
    top, corner = upper_product(gg.at[1 - core], gg.at[core])
    sa, sc = unpack(old[LOW, LOW], old[HALF : HALF + 1, LOW])
    s00 = decay_rate * sa + top[:, :HALF]
    s01 = decay_rate * old[LOW, TOP] + top[:, HALF:]
    s11 = decay_rate * sc + corner
    pack_into(stage, s00, s01, s11)
    copies.append(pltpu.make_async_copy(stage, out, sems.at[1]))
    copies[-1].start()
    i, j = triangle()
    trace = total(jnp.where(i == j, s00 + s11, 0.0))
    norm_sq = total(s00 * s00 + s11 * s11 + 2.0 * (s01 * s01))
    inv = 1.0 / jnp.sqrt(norm_sq + epsilon)
    tops[0, :, LOW], tops[0, :, TOP], corners[0] = s00 * inv, s01 * inv, s11 * inv
    store(0)
    spread(tops[0], corners[0], s1)
    tops[1], corners[1] = upper_product(s1, s1)
    store(1)
    spread(tops[1], corners[1], s2)
    cube_top[...], cube_corner[...] = upper_product(s1, s2)
    facts[...] = jnp.concatenate([jnp.broadcast_to(x, (1, 128)) for x in (norm_sq, trace)], axis=0)
    for copy in copies:
        copy.wait()


def coefficients(devices, facts, sums):
    both = jnp.sum(jnp.sum(sums[...], axis=0), axis=1, keepdims=True)
    grad_sq, trace_all = both[0:1], both[1:2]
    shift = (decay_rate * trace_all + 2.0 * grad_sq) * (damping / (devices * BLOCK))
    shift = jnp.broadcast_to(shift, (1, 128))
    norm_sq, trace = facts[0:1, :], facts[1:2, :]
    frob = jnp.sqrt(norm_sq + 2.0 * shift * trace + BLOCK * shift * shift + epsilon)
    a = jnp.sqrt(norm_sq + epsilon) / frob
    e = shift / frob
    outer = 1.0 / jnp.sqrt(jnp.sqrt(frob))
    k = []
    for i in range(7):
        value = jnp.full_like(e, ROOT_COEFFS[6] * math.comb(6, i))
        for j in range(5, i - 1, -1):
            value = value * e + math.comb(j, i) * ROOT_COEFFS[j]
        k.append((outer * value)[:, 0:1])
        outer = outer * a
    return k, grad_sq


def root(devices, *refs):
    top_in, corner_in, cube_top, cube_corner, facts, sums, g_in, out, totals, g_out = refs[:10]
    inner, cube, top_v, corner_v, sems = refs[10:]
    copies = [
        pltpu.make_async_copy(src, dst, sems.at[n])
        for n, (src, dst) in enumerate(((top_in, top_v), (corner_in, corner_v), (g_in, g_out)))
    ]
    for copy in copies:
        copy.start()
    k, grad_sq = coefficients(devices, facts, sums)
    spread(cube_top[...], cube_corner[...], cube)
    for copy in copies[:2]:
        copy.wait()
    tops, corners = (top_v[0], top_v[1], cube_top[...]), (corner_v[0], corner_v[1], cube_corner[...])
    spread(*(k[4] * t[0] + k[5] * t[1] + k[6] * t[2] for t in (tops, corners)), inner)
    top, corner = upper_product(cube, inner)
    i, j = triangle()
    diag = jnp.where(i == j, k[0], 0.0)
    low = k[1] * tops[0] + k[2] * tops[1] + k[3] * tops[2] + top
    out[LOW, LOW] = low[:, :HALF] + diag
    out[LOW, TOP] = low[:, HALF:]
    corner = k[1] * corners[0] + k[2] * corners[1] + k[3] * corners[2] + corner + diag
    out[HALF:, LOW] = corner[: HALF // 2]
    out[HALF:, TOP] = corner[HALF // 2 :]
    totals[...] = jnp.broadcast_to(grad_sq, (1, 128))
    copies[2].wait()


def root_corner(packed):
    return jnp.concatenate([packed[HALF:, LOW], packed[HALF:, TOP]], axis=0)


def half_way(g, packed, out, x):
    _, core = chip_core()
    spread(packed[LOW], root_corner(packed), x)

    @pl.when(core == 1)
    def _():
        y = dot3((x[0, TOP], x[1, TOP]), (g[0], g[1]))
        out[0, LOW], out[1, LOW] = split(y)

    @pl.when(core == 0)
    def _():
        out[0], out[1] = split(dot3((g[0], g[1]), (x[0], x[1])))


def last_product(middle, packed, mine, sums, x):
    _, core = chip_core()

    @pl.when(core == 1)
    def _():
        spread(packed[LOW], root_corner(packed), x)
        mine[...] = dot3((middle[0, LOW], middle[1, LOW]), (x[0], x[1]))

    @pl.when(core == 0)
    def _():
        mine[...] = dot3(split(packed[LOW]), (middle[0], middle[1]))

    sums[...] = jnp.broadcast_to(lanes(mine[...] * mine[...])[None], sums.shape)


def unpack_stat(packed, out):
    sa, sc = unpack(packed[LOW, LOW], packed[HALF : HALF + 1, LOW])
    off = packed[LOW, TOP]
    out[LOW, LOW] = sa
    out[LOW, TOP] = off
    out[TOP, LOW] = off.T
    out[TOP, TOP] = sc


def write_pieces(chip, core, pieces, scale, owners, out, scaled, sems):
    copies = []
    for n, (j, swapped, src) in enumerate(pieces):
        half = 1 - core if swapped else core
        base = owners[0, chip ^ j] * BLOCK + half * HALF
        for r in range(0, HALF, CHUNK):
            scaled[n, pl.ds(r, CHUNK)] = src[pl.ds(r, CHUNK)] * scale
            start = pl.multiple_of(base + r, CHUNK)
            copies.append(
                pltpu.make_async_copy(scaled.at[n, pl.ds(r, CHUNK)], out.at[pl.ds(start, CHUNK)], sems.at[len(copies)])
            )
            copies[-1].start()
    for copy in copies:
        copy.wait()


def place_near(direct, across, sums, totals, owners, out, scale, scaled, sems):
    chip, core = chip_core()
    prec_sq = jnp.sum(jnp.sum(sums[...], axis=0), axis=1, keepdims=True)
    factor = jnp.sqrt(totals[0:1, 0:1] / (prec_sq + epsilon))
    scale[...] = jnp.broadcast_to(factor, (1, 128))
    write_pieces(chip, core, ((0, False, direct), (0, True, across)), factor, owners, out, scaled, sems)


def place_more(swapped, count, *refs):
    scale, owners, _, out, scaled, sems = refs[count:]
    chip, core = chip_core()
    pieces = [(j + 1, swapped, x) for j, x in enumerate(refs[:count])]
    write_pieces(chip, core, pieces, scale[0:1, 0:1], owners, out, scaled, sems)


def per_device(activations, out_grads, statistics, owner_blocks):
    rep_count = lax.axis_size("rep")
    pairs = rep_count // 2
    devices = rep_count * lax.axis_size("stripe")
    tokens = activations.shape[0]
    piece, square = (HALF, BLOCK), (BLOCK, BLOCK)
    unit = 6 * BLOCK**3

    whole = jax.ShapeDtypeStruct((2,) + square, bf16)
    split_square = pltpu.VMEM((2,) + square, bf16)
    packed_buffer = pltpu.VMEM((PACKED, BLOCK), f32)
    m = pairs // 2

    def terms(*plan):
        return call(
            functools.partial(grad_terms, plan),
            [(len(chips),) + piece for chips, _ in plan],
            [HBM] * 3,
            [
                pltpu.VMEM(activations.shape, bf16),
                pltpu.VMEM(out_grads.shape, bf16),
                pltpu.SMEM(owner_blocks.shape, jnp.int32),
                pltpu.SemaphoreType.DMA((3,)),
            ],
            flops=2 * tokens * HALF * BLOCK * sum(len(chips) for chips, _ in plan),
        )(*(in_hbm(x) for x in (activations, out_grads, owner_blocks)))

    upper, lower = range(m, pairs), range(m)
    (send_far,) = terms((upper, True))
    got_far = flip(send_far, 1)
    keep_far, send_near, keep_near = terms((upper, False), (lower, True), (lower, False))
    got_near = flip(send_near, 1)
    arrived = [flip(keep_far[j] + got_far[j], 2 * m) for j in range(m)]
    while m > 1:
        m //= 2
        held = [keep_near[j] + got_near[j] + arrived[j] for j in range(m, 2 * m)]
        arrived = [x + flip(y, 2 * m) for x, y in zip(arrived, held)]
    shuffle = [(s * pairs + p, 2 * p + 1 - s) for s in range(2) for p in range(pairs)]
    packed, trace = call(pack_stat, [(PACKED, BLOCK), (1, 128)], [VMEM])(statistics[0, 0])
    old = lax.ppermute(packed, "rep", shuffle)
    half, sums = call(
        functools.partial(finish_half, devices), [piece, (devices, 2, 128)], [VMEM] * 4
    )(keep_near, got_near, arrived[0], trace)
    other = flip(half, 1)
    sums = lax.all_to_all(sums, AXES, 0, 0)
    *powers, facts, out_packed, g_split = call(
        update_powers,
        [pltpu.HBM((2,) + piece, f32), pltpu.HBM((2, HALF, HALF), f32), piece, (HALF, HALF), (2, 128)]
        + [pltpu.HBM((PACKED, BLOCK), f32), pltpu.HBM((2,) + square, bf16)],
        [VMEM] * 3,
        [pltpu.VMEM((2, 2) + square, bf16), split_square, split_square, packed_buffer]
        + [pltpu.VMEM((2,) + piece, f32), pltpu.VMEM((2, HALF, HALF), f32), pltpu.SemaphoreType.DMA((6,))],
        flops=3 * unit,
        out_specs=[HBM] * 2 + [VMEM] * 3 + [HBM] * 2,
    )(half, other, old)
    new_packed = lax.ppermute(out_packed, "rep", [(t, s) for s, t in shuffle])
    mine_root, totals, g_split = call(
        functools.partial(root, devices),
        [(HALF + HALF // 2, BLOCK), (1, 128), whole],
        [HBM] * 2 + [VMEM] * 4 + [HBM],
        [split_square] * 2
        + [pltpu.VMEM((2,) + piece, f32), pltpu.VMEM((2, HALF, HALF), f32), pltpu.SemaphoreType.DMA((3,))],
        flops=unit,
    )(in_hbm(powers[0]), in_hbm(powers[1]), powers[2], powers[3], facts, sums, in_hbm(g_split))
    other_root = flip(mine_root, 1)
    (middle,) = call(half_way, [whole], [VMEM] * 2, [split_square], flops=unit)(g_split, mine_root)
    mine, prec = call(last_product, [piece, (lax.axis_size("stripe"), 1, 128)], [VMEM] * 2, [split_square], flops=unit)(middle, other_root)

    bit = 1
    while bit < rep_count:
        masks = [x for x in (3 * bit, 2 * bit, bit) if x < rep_count]
        prec = sum((flip(prec, x) for x in masks), prec)
        bit *= 4
    direct, m = [mine], 1
    while m < pairs:
        direct = direct + [flip(x, 2 * m) for x in direct]
        m *= 2
    across = [flip(mine, 1)]
    prec = lax.all_to_all(prec, "stripe", 0, 0)
    (new_stat,) = call(unpack_stat, [square], [VMEM])(new_packed)
    slab = (pairs * BLOCK, out_grads.shape[1])

    def landing(count):
        return [pltpu.VMEM((count,) + piece, f32), pltpu.SemaphoreType.DMA((count * HALF // CHUNK,))]

    placed, scale = call(
        place_near, [slab, (1, 128)], [VMEM] * 4 + [SMEM], landing(2), out_specs=[HBM, VMEM]
    )(mine, across[0], prec, totals, owner_blocks)
    across = [flip(x, 1) for x in direct[1:]]
    count = pairs - 1
    for swapped, found in ((False, direct[1:]), (True, across)):
        (placed,) = call(
            functools.partial(place_more, swapped, count),
            [slab],
            [VMEM] * (count + 1) + [SMEM, HBM],
            landing(count),
            out_specs=[HBM],
            input_output_aliases={count + 2: 0},
        )(*found, scale, owner_blocks, placed)
    return placed, new_stat[None, None]


def solution(mesh):
    in_specs = (
        P("rep", None),
        P("rep", "stripe"),
        P("rep", "stripe", None, None),
        P("stripe", None),
    )
    out_specs = (P(None, "stripe"), P("rep", "stripe", None, None))
    return jax.shard_map(per_device, mesh=mesh, in_specs=in_specs, out_specs=out_specs, check_vma=False)
```

```python
import functools
import math

import jax
import jax.numpy as jnp
from jax import lax
from jax.experimental import pallas as pl
from jax.experimental.pallas import tpu as pltpu
from jax.sharding import PartitionSpec as P


BLOCK = 512
HALF = BLOCK // 2
PACKED = HALF + 8
CHUNK = 64

decay_rate = 0.95
damping = 0.25
epsilon = 1e-06
AXES = ("rep", "stripe")
f32 = jnp.float32
bf16 = jnp.bfloat16

ROOT_COEFFS = (
    25 / 16,
    -5 / 16 - 3125 / 4096,
    3125 / 4096,
    -1250 / 4096,
    250 / 4096,
    -25 / 4096,
    1 / 4096,
)

VMEM = pl.BlockSpec(memory_space=pltpu.VMEM)
SMEM = pl.BlockSpec(memory_space=pltpu.SMEM)
HBM = pl.BlockSpec(memory_space=pltpu.HBM)
LOW = pl.ds(0, HALF)
TOP = pl.ds(HALF, HALF)


def call(body, out_shapes, in_specs, scratch=(), limit=16, flops=0, out_specs=None, **kwargs):
    return pl.pallas_call(
        body,
        out_shape=[jax.ShapeDtypeStruct(s, f32) if isinstance(s, tuple) else s for s in out_shapes],
        in_specs=in_specs,
        out_specs=out_specs or [VMEM] * len(out_shapes),
        scratch_shapes=list(scratch),
        compiler_params=pltpu.CompilerParams(vmem_limit_bytes=limit << 20),
        cost_estimate=pl.CostEstimate(flops=flops, bytes_accessed=1 << 20, transcendentals=0),
        **kwargs,
    )


def flip(x, mask):
    return lax.ppermute(x, "rep", [(i, i ^ mask) for i in range(lax.axis_size("rep"))])


def in_hbm(x):
    return pltpu.with_memory_space_constraint(x, pltpu.HBM)


def chip_core():
    me = lax.axis_index("rep")
    return lax.shift_right_logical(me, 1), lax.bitwise_and(me, 1)


def split(x):
    hi = x.astype(bf16)
    return hi, (x - hi.astype(f32)).astype(bf16)


def mm(a, b):
    return jnp.dot(a, b, preferred_element_type=f32)


def dot3(a, b):
    return mm(a[0], b[0]) + (mm(a[0], b[1]) + mm(a[1], b[0]))


def triangle():
    i = lax.broadcasted_iota(jnp.int32, (HALF, HALF), 0)
    j = lax.broadcasted_iota(jnp.int32, (HALF, HALF), 1)
    return i, j


def lanes(x):
    rows = jnp.sum(x, axis=0, keepdims=True)
    return sum(rows[:, k : k + 128] for k in range(0, x.shape[1], 128))


def pack_into(out, a, b, c):
    i, j = triangle()
    out[LOW, LOW] = jnp.where(i <= j, a, c)
    out[LOW, TOP] = b
    out[HALF:, LOW] = jnp.broadcast_to(jnp.sum(jnp.where(i == j, c, 0.0), axis=0, keepdims=True), (8, HALF))


def unpack(u, diag):
    i, j = triangle()
    ut = u.T
    return jnp.where(i <= j, u, ut), jnp.where(i > j, u, jnp.where(i < j, ut, diag))


def pack_stat(stat, out, trace):
    i, j = triangle()
    a, c = stat[LOW, LOW], stat[TOP, TOP]
    pack_into(out, a, stat[LOW, TOP], c)
    trace[...] = lanes(jnp.where(i == j, a + c, 0.0))


def grad_terms(plan, acts, grads, owners, *refs):
    outs, (av, gv, ov, sems) = refs[: len(plan)], refs[len(plan) :]
    chip, core = chip_core()
    copies = [
        pltpu.make_async_copy(src, dst, sems.at[k]) for k, (src, dst) in enumerate(((owners, ov), (acts, av), (grads, gv)))
    ]
    for copy in copies:
        copy.start()
    for copy in copies:
        copy.wait()
    cotangent = gv[...]
    for out, (chips, swapped) in zip(outs, plan):
        half = 1 - core if swapped else core
        for n, j in enumerate(chips):
            start = ov[0, chip ^ j] * BLOCK + half * HALF
            cols = av[:, pl.ds(pl.multiple_of(start, HALF), HALF)]
            out[n] = lax.dot_general(cols, cotangent, (((0,), (0,)), ((), ())), preferred_element_type=f32)


def finish_half(devices, keep, got, rest, trace, half, sums):
    value = keep[0] + got[0] + rest[...]
    half[...] = value
    both = jnp.concatenate([lanes(value * value), trace[...]], axis=0)
    sums[...] = jnp.broadcast_to(both[None], (devices, 2, 128))


def spread(top, corner, out):
    out[0, LOW], out[1, LOW] = split(top)
    out[0, TOP, TOP], out[1, TOP, TOP] = split(corner)
    for k in range(2):
        out[k, TOP, LOW] = out[k, LOW, TOP].T


def upper_product(a, b):
    top = dot3((a[0, LOW], a[1, LOW]), (b[0], b[1]))
    return top, dot3((a[0, TOP], a[1, TOP]), (b[0, :, TOP], b[1, :, TOP]))


def total(x):
    return jnp.sum(jnp.sum(x, axis=0, keepdims=True), axis=1, keepdims=True)


def load_gradient(core, half, other, g):
    mine = pl.ds(pl.multiple_of(core * HALF, HALF), HALF)
    theirs = pl.ds(pl.multiple_of(HALF - core * HALF, HALF), HALF)
    for rows, src in ((mine, half), (theirs, other)):
        g[0, rows], g[1, rows] = split(src[...])


def update_stat(half, other, old, facts, out, g_out, g, sem):
    _, core = chip_core()
    load_gradient(core, half, other, g.at[0])
    copy = pltpu.make_async_copy(g.at[0], g_out, sem)
    copy.start()
    for k in range(2):
        g[1, k] = g[0, k].T
    top, corner = upper_product(g.at[1 - core], g.at[core])
    sa, sc = unpack(old[LOW, LOW], old[HALF : HALF + 1, LOW])
    s00 = decay_rate * sa + top[:, :HALF]
    s01 = decay_rate * old[LOW, TOP] + top[:, HALF:]
    s11 = decay_rate * sc + corner
    pack_into(out, s00, s01, s11)
    i, j = triangle()
    trace = total(jnp.where(i == j, s00 + s11, 0.0))
    norm_sq = total(s00 * s00 + s11 * s11 + 2.0 * (s01 * s01))
    facts[...] = jnp.concatenate([jnp.broadcast_to(x, (1, 128)) for x in (norm_sq, trace)], axis=0)
    copy.wait()


def coefficients(devices, facts, sums):
    both = jnp.sum(jnp.sum(sums[...], axis=0), axis=1, keepdims=True)
    grad_sq, trace_all = both[0:1], both[1:2]
    shift = (decay_rate * trace_all + 2.0 * grad_sq) * (damping / (devices * BLOCK))
    shift = jnp.broadcast_to(shift, (1, 128))
    norm_sq, trace = facts[0:1, :], facts[1:2, :]
    frob = jnp.sqrt(norm_sq + 2.0 * shift * trace + BLOCK * shift * shift + epsilon)
    a = jnp.sqrt(norm_sq + epsilon) / frob
    e = shift / frob
    outer = 1.0 / jnp.sqrt(jnp.sqrt(frob))
    k = []
    for i in range(7):
        value = jnp.full_like(e, ROOT_COEFFS[6] * math.comb(6, i))
        for j in range(5, i - 1, -1):
            value = value * e + math.comb(j, i) * ROOT_COEFFS[j]
        k.append((outer * value)[:, 0:1])
        outer = outer * a
    return k, grad_sq


def root(devices, stat, facts, sums, out, totals, first, inner, cube):
    k, grad_sq = coefficients(devices, facts, sums)
    inv = 1.0 / jnp.sqrt(facts[0:1, 0:1] + epsilon)
    s00, s11 = unpack(stat[LOW, LOW], stat[HALF : HALF + 1, LOW])
    tops, corners = [jnp.concatenate([s00, stat[LOW, TOP]], axis=1) * inv], [s11 * inv]
    spread(tops[0], corners[0], first)
    for x in (first, inner):
        top, corner = upper_product(first, x)
        tops.append(top)
        corners.append(corner)
        spread(top, corner, inner if x is first else cube)
    spread(*(k[4] * t[0] + k[5] * t[1] + k[6] * t[2] for t in (tops, corners)), inner)
    top, corner = upper_product(cube, inner)
    i, j = triangle()
    diag = jnp.where(i == j, k[0], 0.0)
    low = k[1] * tops[0] + k[2] * tops[1] + k[3] * tops[2] + top
    out[LOW, LOW] = low[:, :HALF] + diag
    out[LOW, TOP] = low[:, HALF:]
    corner = k[1] * corners[0] + k[2] * corners[1] + k[3] * corners[2] + corner + diag
    out[HALF:, LOW] = corner[: HALF // 2]
    out[HALF:, TOP] = corner[HALF // 2 :]
    totals[...] = jnp.broadcast_to(grad_sq, (1, 128))


def root_corner(packed):
    return jnp.concatenate([packed[HALF:, LOW], packed[HALF:, TOP]], axis=0)


def half_way(g, packed, out, x):
    _, core = chip_core()
    spread(packed[LOW], root_corner(packed), x)

    @pl.when(core == 1)
    def _():
        y = dot3((x[0, TOP], x[1, TOP]), (g[0], g[1]))
        out[0, LOW], out[1, LOW] = split(y)

    @pl.when(core == 0)
    def _():
        out[0], out[1] = split(dot3((g[0], g[1]), (x[0], x[1])))


def last_product(middle, packed, mine, sums, x):
    _, core = chip_core()

    @pl.when(core == 1)
    def _():
        spread(packed[LOW], root_corner(packed), x)
        mine[...] = dot3((middle[0, LOW], middle[1, LOW]), (x[0], x[1]))

    @pl.when(core == 0)
    def _():
        mine[...] = dot3(split(packed[LOW]), (middle[0], middle[1]))

    sums[...] = jnp.broadcast_to(lanes(mine[...] * mine[...])[None], sums.shape)


def unpack_stat(packed, out):
    sa, sc = unpack(packed[LOW, LOW], packed[HALF : HALF + 1, LOW])
    off = packed[LOW, TOP]
    out[LOW, LOW] = sa
    out[LOW, TOP] = off
    out[TOP, LOW] = off.T
    out[TOP, TOP] = sc


def write_pieces(pieces, scale, out, scaled, sems):
    copies = []
    for n, (base, src) in enumerate(pieces):
        for r in range(0, HALF, CHUNK):
            scaled[n, pl.ds(r, CHUNK)] = src[pl.ds(r, CHUNK)] * scale
            start = pl.multiple_of(base + r, CHUNK)
            copies.append(
                pltpu.make_async_copy(scaled.at[n, pl.ds(r, CHUNK)], out.at[pl.ds(start, CHUNK)], sems.at[len(copies)])
            )
            copies[-1].start()
    for copy in copies:
        copy.wait()


def place_near(pairs, direct, across, sums, totals, owners, out, facts, scaled, sems):
    chip, core = chip_core()
    prec_sq = jnp.sum(jnp.sum(sums[...], axis=0), axis=1, keepdims=True)
    scale = jnp.sqrt(totals[0:1, 0:1] / (prec_sq + epsilon))
    facts[0:1, :] = jnp.broadcast_to(scale, (1, 128))
    rows = [
        [owners[0, lax.bitwise_xor(chip, jnp.int32(j))] * BLOCK + half * HALF for j in range(pairs)]
        for half in (core, 1 - core)
    ]
    for n, row in enumerate(rows[0][1:] + rows[1][1:]):
        facts[n + 1 : n + 2, :] = jnp.full((1, 128), row.astype(f32))
    write_pieces(((rows[0][0], direct), (rows[1][0], across)), scale, out, scaled, sems)


def place_more(swapped, count, *refs):
    facts, _, out, scaled, sems = refs[count:]
    pieces = [
        (jnp.max(facts[n : n + 1, :]).astype(jnp.int32), x) for n, x in enumerate(refs[:count], 1 + swapped * count)
    ]
    write_pieces(pieces, facts[0:1, 0:1], out, scaled, sems)


def per_device(activations, out_grads, statistics, owner_blocks):
    rep_count = lax.axis_size("rep")
    pairs = rep_count // 2
    devices = rep_count * lax.axis_size("stripe")
    tokens = activations.shape[0]
    piece, square = (HALF, BLOCK), (BLOCK, BLOCK)
    unit = 6 * BLOCK**3

    whole = jax.ShapeDtypeStruct((2,) + square, bf16)
    split_square = pltpu.VMEM((2,) + square, bf16)
    m = pairs // 2

    def terms(*plan):
        return call(
            functools.partial(grad_terms, plan),
            [(len(chips),) + piece for chips, _ in plan],
            [HBM] * 3,
            [
                pltpu.VMEM(activations.shape, bf16),
                pltpu.VMEM(out_grads.shape, bf16),
                pltpu.SMEM(owner_blocks.shape, jnp.int32),
                pltpu.SemaphoreType.DMA((3,)),
            ],
            flops=2 * tokens * HALF * BLOCK * sum(len(chips) for chips, _ in plan),
        )(*(in_hbm(x) for x in (activations, out_grads, owner_blocks)))

    above, below = range(m, pairs), range(m)
    (send_far,) = terms((above, True))
    got_far = flip(send_far, 1)
    keep_far, send_near, keep_near = terms((above, False), (below, True), (below, False))
    got_near = flip(send_near, 1)
    arrived = [flip(keep_far[j] + got_far[j], 2 * m) for j in range(m)]
    while m > 1:
        m //= 2
        held = [keep_near[j] + got_near[j] + arrived[j] for j in range(m, 2 * m)]
        arrived = [x + flip(y, 2 * m) for x, y in zip(arrived, held)]
    shuffle = [(s * pairs + p, 2 * p + 1 - s) for s in range(2) for p in range(pairs)]
    packed, trace = call(pack_stat, [(PACKED, BLOCK), (1, 128)], [VMEM])(statistics[0, 0])
    old = lax.ppermute(packed, "rep", shuffle)
    half, sums = call(
        functools.partial(finish_half, devices), [piece, (devices, 2, 128)], [VMEM] * 4
    )(keep_near, got_near, arrived[0], trace)
    other = flip(half, 1)
    sums = lax.all_to_all(sums, AXES, 0, 0)
    facts, out_packed, g_split = call(
        update_stat,
        [(2, 128), (PACKED, BLOCK), pltpu.HBM((2,) + square, bf16)],
        [VMEM] * 3,
        [pltpu.VMEM((2, 2) + square, bf16), pltpu.SemaphoreType.DMA],
        flops=unit,
        out_specs=[VMEM] * 2 + [HBM],
    )(half, other, old)
    new_packed = lax.ppermute(out_packed, "rep", [(t, s) for s, t in shuffle])
    mine_root, totals = call(
        functools.partial(root, devices),
        [(HALF + HALF // 2, BLOCK), (1, 128)],
        [VMEM] * 3,
        [split_square] * 3,
        flops=3 * unit,
    )(out_packed, facts, sums)
    other_root = flip(mine_root, 1)
    (middle,) = call(half_way, [whole], [VMEM] * 2, [split_square], flops=unit)(g_split, mine_root)
    mine, prec = call(last_product, [piece, (lax.axis_size("stripe"), 1, 128)], [VMEM] * 2, [split_square], flops=unit)(middle, other_root)

    bit = 1
    while bit < rep_count:
        masks = [x for x in (3 * bit, 2 * bit, bit) if x < rep_count]
        prec = sum((flip(prec, x) for x in masks), prec)
        bit *= 4
    direct, m = [mine], 1
    while m < pairs:
        direct = direct + [flip(x, 2 * m) for x in direct]
        m *= 2
    across = [flip(mine, 1)]
    prec = lax.all_to_all(prec, "stripe", 0, 0)
    (new_stat,) = call(unpack_stat, [square], [VMEM])(new_packed)
    slab = (pairs * BLOCK, out_grads.shape[1])

    def landing(count):
        return [pltpu.VMEM((count,) + piece, f32), pltpu.SemaphoreType.DMA((count * HALF // CHUNK,))]

    placed, facts = call(
        functools.partial(place_near, pairs),
        [slab, (2 * pairs - 1, 128)],
        [VMEM] * 4 + [SMEM],
        landing(2),
        out_specs=[HBM, VMEM],
    )(mine, across[0], prec, totals, owner_blocks)
    across = [flip(x, 1) for x in direct[1:]]
    count = pairs - 1
    for swapped, found in ((0, direct[1:]), (1, across)):
        (placed,) = call(
            functools.partial(place_more, swapped, count),
            [slab],
            [VMEM] * (count + 1) + [HBM],
            landing(count),
            out_specs=[HBM],
            input_output_aliases={count + 1: 0},
        )(*found, facts, placed)
    return placed, new_stat[None, None]


def solution(mesh):
    in_specs = (
        P("rep", None),
        P("rep", "stripe"),
        P("rep", "stripe", None, None),
        P("stripe", None),
    )
    out_specs = (P(None, "stripe"), P("rep", "stripe", None, None))
    return jax.shard_map(per_device, mesh=mesh, in_specs=in_specs, out_specs=out_specs, check_vma=False)
```

```python
import functools
import math

import jax
import jax.numpy as jnp
from jax import lax
from jax.experimental import pallas as pl
from jax.experimental.pallas import tpu as pltpu
from jax.sharding import PartitionSpec as P


BLOCK = 512
HALF = BLOCK // 2
PACKED = HALF + 8
CHUNK = 64

decay_rate = 0.95
damping = 0.25
epsilon = 1e-06
AXES = ("rep", "stripe")
f32 = jnp.float32
bf16 = jnp.bfloat16

ROOT_COEFFS = (
    25 / 16,
    -5 / 16 - 3125 / 4096,
    3125 / 4096,
    -1250 / 4096,
    250 / 4096,
    -25 / 4096,
    1 / 4096,
)

VMEM = pl.BlockSpec(memory_space=pltpu.VMEM)
SMEM = pl.BlockSpec(memory_space=pltpu.SMEM)
HBM = pl.BlockSpec(memory_space=pltpu.HBM)
LOW = pl.ds(0, HALF)
TOP = pl.ds(HALF, HALF)


def call(body, out_shapes, in_specs, scratch=(), limit=16, flops=0, out_specs=None, **kwargs):
    return pl.pallas_call(
        body,
        out_shape=[jax.ShapeDtypeStruct(s, f32) if isinstance(s, tuple) else s for s in out_shapes],
        in_specs=in_specs,
        out_specs=out_specs or [VMEM] * len(out_shapes),
        scratch_shapes=list(scratch),
        compiler_params=pltpu.CompilerParams(vmem_limit_bytes=limit << 20),
        cost_estimate=pl.CostEstimate(flops=flops, bytes_accessed=1 << 20, transcendentals=0),
        **kwargs,
    )


def flip(x, mask):
    return lax.ppermute(x, "rep", [(i, i ^ mask) for i in range(lax.axis_size("rep"))])


def in_hbm(x):
    return pltpu.with_memory_space_constraint(x, pltpu.HBM)


def chip_core():
    me = lax.axis_index("rep")
    return lax.shift_right_logical(me, 1), lax.bitwise_and(me, 1)


def split(x):
    hi = x.astype(bf16)
    return hi, (x - hi.astype(f32)).astype(bf16)


def mm(a, b):
    return jnp.dot(a, b, preferred_element_type=f32)


def dot3(a, b):
    return mm(a[0], b[0]) + (mm(a[0], b[1]) + mm(a[1], b[0]))


def triangle():
    i = lax.broadcasted_iota(jnp.int32, (HALF, HALF), 0)
    j = lax.broadcasted_iota(jnp.int32, (HALF, HALF), 1)
    return i, j


def lanes(x):
    rows = jnp.sum(x, axis=0, keepdims=True)
    return sum(rows[:, k : k + 128] for k in range(0, x.shape[1], 128))


def pack_into(out, a, b, c):
    i, j = triangle()
    out[LOW, LOW] = jnp.where(i <= j, a, c)
    out[LOW, TOP] = b
    out[HALF:, LOW] = jnp.broadcast_to(jnp.sum(jnp.where(i == j, c, 0.0), axis=0, keepdims=True), (8, HALF))


def unpack(u, diag):
    i, j = triangle()
    ut = u.T
    return jnp.where(i <= j, u, ut), jnp.where(i > j, u, jnp.where(i < j, ut, diag))


def pack_stat(pairs, stat, owners, out, trace, rows):
    chip, core = chip_core()
    for n in range(2 * pairs):
        half = core if n < pairs else 1 - core
        row = owners[0, lax.bitwise_xor(chip, jnp.int32(n % pairs))] * BLOCK + half * HALF
        rows[n : n + 1, :] = jnp.full((1, 128), row.astype(f32))
    i, j = triangle()
    a, c = stat[LOW, LOW], stat[TOP, TOP]
    pack_into(out, a, stat[LOW, TOP], c)
    trace[...] = lanes(jnp.where(i == j, a + c, 0.0))


def grad_terms(plan, acts, grads, owners, *refs):
    outs, (av, gv, ov, sems) = refs[: len(plan)], refs[len(plan) :]
    chip, core = chip_core()
    copies = [
        pltpu.make_async_copy(src, dst, sems.at[k]) for k, (src, dst) in enumerate(((owners, ov), (acts, av), (grads, gv)))
    ]
    for copy in copies:
        copy.start()
    for copy in copies:
        copy.wait()
    cotangent = gv[...]
    for out, (chips, swapped) in zip(outs, plan):
        half = 1 - core if swapped else core
        for n, j in enumerate(chips):
            start = ov[0, chip ^ j] * BLOCK + half * HALF
            cols = av[:, pl.ds(pl.multiple_of(start, HALF), HALF)]
            out[n] = lax.dot_general(cols, cotangent, (((0,), (0,)), ((), ())), preferred_element_type=f32)


def finish_half(devices, keep, got, rest, trace, half, sums):
    value = keep[0] + got[0] + rest[...]
    half[...] = value
    both = jnp.concatenate([lanes(value * value), trace[...]], axis=0)
    sums[...] = jnp.broadcast_to(both[None], (devices, 2, 128))


def spread(top, corner, out):
    out[0, LOW], out[1, LOW] = split(top)
    out[0, TOP, TOP], out[1, TOP, TOP] = split(corner)
    for k in range(2):
        out[k, TOP, LOW] = out[k, LOW, TOP].T


def upper_product(a, b):
    top = dot3((a[0, LOW], a[1, LOW]), (b[0], b[1]))
    return top, dot3((a[0, TOP], a[1, TOP]), (b[0, :, TOP], b[1, :, TOP]))


def total(x):
    return jnp.sum(jnp.sum(x, axis=0, keepdims=True), axis=1, keepdims=True)


def load_gradient(core, half, other, g):
    mine = pl.ds(pl.multiple_of(core * HALF, HALF), HALF)
    theirs = pl.ds(pl.multiple_of(HALF - core * HALF, HALF), HALF)
    for rows, src in ((mine, half), (theirs, other)):
        g[0, rows], g[1, rows] = split(src[...])


def unpack_upper(packed):
    s00, s11 = unpack(packed[LOW, LOW], packed[HALF : HALF + 1, LOW])
    return jnp.concatenate([s00, packed[LOW, TOP]], axis=1), s11


def update_stat(half, other, old, facts, square_out, cube_out, out, g_out, g, s1, s2, stage, sems):
    _, core = chip_core()
    load_gradient(core, half, other, g.at[0])
    copies = [pltpu.make_async_copy(g.at[0], g_out, sems.at[0]), pltpu.make_async_copy(stage, out, sems.at[1])]
    copies[0].start()
    for k in range(2):
        g[1, k] = g[0, k].T
    top, corner = upper_product(g.at[1 - core], g.at[core])
    was_top, was_corner = unpack_upper(old)
    top = decay_rate * was_top + top
    corner = decay_rate * was_corner + corner
    s00, s01 = top[:, :HALF], top[:, HALF:]
    pack_into(stage, s00, s01, corner)
    copies[1].start()
    i, j = triangle()
    trace = total(jnp.where(i == j, s00 + corner, 0.0))
    norm_sq = total(s00 * s00 + corner * corner + 2.0 * (s01 * s01))
    inv = 1.0 / jnp.sqrt(norm_sq + epsilon)
    spread(top * inv, corner * inv, s1)
    top, corner = upper_product(s1, s1)
    pack_into(square_out, top[:, :HALF], top[:, HALF:], corner)
    spread(top, corner, s2)
    top, corner = upper_product(s1, s2)
    pack_into(cube_out, top[:, :HALF], top[:, HALF:], corner)
    facts[...] = jnp.concatenate([jnp.broadcast_to(x, (1, 128)) for x in (norm_sq, trace)], axis=0)
    for copy in copies:
        copy.wait()


def coefficients(devices, facts, sums):
    both = jnp.sum(jnp.sum(sums[...], axis=0), axis=1, keepdims=True)
    grad_sq, trace_all = both[0:1], both[1:2]
    shift = (decay_rate * trace_all + 2.0 * grad_sq) * (damping / (devices * BLOCK))
    shift = jnp.broadcast_to(shift, (1, 128))
    norm_sq, trace = facts[0:1, :], facts[1:2, :]
    frob = jnp.sqrt(norm_sq + 2.0 * shift * trace + BLOCK * shift * shift + epsilon)
    a = jnp.sqrt(norm_sq + epsilon) / frob
    e = shift / frob
    outer = 1.0 / jnp.sqrt(jnp.sqrt(frob))
    k = []
    for i in range(7):
        value = jnp.full_like(e, ROOT_COEFFS[6] * math.comb(6, i))
        for j in range(5, i - 1, -1):
            value = value * e + math.comb(j, i) * ROOT_COEFFS[j]
        k.append((outer * value)[:, 0:1])
        outer = outer * a
    return k, grad_sq


def root(devices, stat_in, g_in, square, cubed, facts, sums, out, totals, g, stat, inner, cube, sems):
    copy = pltpu.make_async_copy(stat_in, stat, sems.at[0])
    fetch = pltpu.make_async_copy(g_in, g, sems.at[1])
    copy.start()
    fetch.start()
    k, grad_sq = coefficients(devices, facts, sums)
    inv = 1.0 / jnp.sqrt(facts[0:1, 0:1] + epsilon)
    third = unpack_upper(cubed)
    spread(*third, cube)
    second = unpack_upper(square)
    copy.wait()
    first = [x * inv for x in unpack_upper(stat)]
    tops, corners = zip(first, second, third)
    spread(*(k[4] * t[0] + k[5] * t[1] + k[6] * t[2] for t in (tops, corners)), inner)
    top, corner = upper_product(cube, inner)
    i, j = triangle()
    diag = jnp.where(i == j, k[0], 0.0)
    low = k[1] * tops[0] + k[2] * tops[1] + k[3] * tops[2] + top
    out[LOW, LOW] = low[:, :HALF] + diag
    out[LOW, TOP] = low[:, HALF:]
    corner = k[1] * corners[0] + k[2] * corners[1] + k[3] * corners[2] + corner + diag
    out[HALF:, LOW] = corner[: HALF // 2]
    out[HALF:, TOP] = corner[HALF // 2 :]
    totals[...] = jnp.broadcast_to(grad_sq, (1, 128))
    fetch.wait()


def root_corner(packed):
    return jnp.concatenate([packed[HALF:, LOW], packed[HALF:, TOP]], axis=0)


def half_way(g, packed, out, x):
    _, core = chip_core()
    spread(packed[LOW], root_corner(packed), x)

    @pl.when(core == 1)
    def _():
        y = dot3((x[0, TOP], x[1, TOP]), (g[0], g[1]))
        out[0, LOW], out[1, LOW] = split(y)

    @pl.when(core == 0)
    def _():
        out[0], out[1] = split(dot3((g[0], g[1]), (x[0], x[1])))


def last_product(middle, packed, mine, sums, x):
    _, core = chip_core()

    @pl.when(core == 1)
    def _():
        spread(packed[LOW], root_corner(packed), x)
        mine[...] = dot3((middle[0, LOW], middle[1, LOW]), (x[0], x[1]))

    @pl.when(core == 0)
    def _():
        mine[...] = dot3(split(packed[LOW]), (middle[0], middle[1]))

    sums[...] = jnp.broadcast_to(lanes(mine[...] * mine[...])[None], sums.shape)


def unpack_stat(packed, out):
    sa, sc = unpack(packed[LOW, LOW], packed[HALF : HALF + 1, LOW])
    off = packed[LOW, TOP]
    out[LOW, LOW] = sa
    out[LOW, TOP] = off
    out[TOP, LOW] = off.T
    out[TOP, TOP] = sc


def write_pieces(pieces, scale, out, scaled, sems):
    copies = []
    for n, (base, src) in enumerate(pieces):
        for r in range(0, HALF, CHUNK):
            scaled[n, pl.ds(r, CHUNK)] = src[pl.ds(r, CHUNK)] * scale
            start = pl.multiple_of(base + r, CHUNK)
            copies.append(
                pltpu.make_async_copy(scaled.at[n, pl.ds(r, CHUNK)], out.at[pl.ds(start, CHUNK)], sems.at[len(copies)])
            )
            copies[-1].start()
    for copy in copies:
        copy.wait()


def first_row(rows, n):
    return jnp.max(rows[n : n + 1, :]).astype(jnp.int32)


def place_most(pairs, *refs):
    direct, (across, sums, totals, rows, out, scale, scaled, sems) = refs[:pairs], refs[pairs:]
    prec_sq = jnp.sum(jnp.sum(sums[...], axis=0), axis=1, keepdims=True)
    factor = jnp.sqrt(totals[0:1, 0:1] / (prec_sq + epsilon))
    scale[...] = jnp.broadcast_to(factor, (1, 128))
    pieces = [(first_row(rows, pairs), across)] + [(first_row(rows, n), x) for n, x in enumerate(direct)]
    write_pieces(pieces, factor, out, scaled, sems)


def place_rest(pairs, *refs):
    across, (scale, rows, _, out, scaled, sems) = refs[: pairs - 1], refs[pairs - 1 :]
    pieces = [(first_row(rows, pairs + n), x) for n, x in enumerate(across, 1)]
    write_pieces(pieces, scale[0:1, 0:1], out, scaled, sems)


def per_device(activations, out_grads, statistics, owner_blocks):
    rep_count = lax.axis_size("rep")
    pairs = rep_count // 2
    devices = rep_count * lax.axis_size("stripe")
    tokens = activations.shape[0]
    piece, square = (HALF, BLOCK), (BLOCK, BLOCK)
    unit = 6 * BLOCK**3

    whole = jax.ShapeDtypeStruct((2,) + square, bf16)
    split_square = pltpu.VMEM((2,) + square, bf16)
    packed_buffer = pltpu.VMEM((PACKED, BLOCK), f32)
    m = pairs // 2

    def terms(*plan):
        return call(
            functools.partial(grad_terms, plan),
            [(len(chips),) + piece for chips, _ in plan],
            [HBM] * 3,
            [
                pltpu.VMEM(activations.shape, bf16),
                pltpu.VMEM(out_grads.shape, bf16),
                pltpu.SMEM(owner_blocks.shape, jnp.int32),
                pltpu.SemaphoreType.DMA((3,)),
            ],
            flops=2 * tokens * HALF * BLOCK * sum(len(chips) for chips, _ in plan),
        )(*(in_hbm(x) for x in (activations, out_grads, owner_blocks)))

    above, below = range(m, pairs), range(m)
    (send_far,) = terms((above, True))
    got_far = flip(send_far, 1)
    keep_far, send_near, keep_near = terms((above, False), (below, True), (below, False))
    got_near = flip(send_near, 1)
    arrived = [flip(keep_far[j] + got_far[j], 2 * m) for j in range(m)]
    while m > 1:
        m //= 2
        held = [keep_near[j] + got_near[j] + arrived[j] for j in range(m, 2 * m)]
        arrived = [x + flip(y, 2 * m) for x, y in zip(arrived, held)]
    shuffle = [(s * pairs + p, 2 * p + 1 - s) for s in range(2) for p in range(pairs)]
    packed, trace, rows = call(
        functools.partial(pack_stat, pairs), [(PACKED, BLOCK), (1, 128), (2 * pairs, 128)], [VMEM, SMEM]
    )(statistics[0, 0], owner_blocks)
    old = lax.ppermute(packed, "rep", shuffle)
    half, sums = call(
        functools.partial(finish_half, devices), [piece, (devices, 2, 128)], [VMEM] * 4
    )(keep_near, got_near, arrived[0], trace)
    other = flip(half, 1)
    sums = lax.all_to_all(sums, AXES, 0, 0)
    facts, square_p, cube_p, out_packed, g_split = call(
        update_stat,
        [(2, 128), (PACKED, BLOCK), (PACKED, BLOCK)]
        + [pltpu.HBM((PACKED, BLOCK), f32), pltpu.HBM((2,) + square, bf16)],
        [VMEM] * 3,
        [pltpu.VMEM((2, 2) + square, bf16), split_square, split_square, packed_buffer, pltpu.SemaphoreType.DMA((2,))],
        flops=3 * unit,
        out_specs=[VMEM] * 3 + [HBM] * 2,
    )(half, other, old)
    new_packed = lax.ppermute(out_packed, "rep", [(t, s) for s, t in shuffle])
    mine_root, totals, g_split = call(
        functools.partial(root, devices),
        [(HALF + HALF // 2, BLOCK), (1, 128), whole],
        [HBM] * 2 + [VMEM] * 4,
        [packed_buffer, split_square, split_square, pltpu.SemaphoreType.DMA((2,))],
        flops=unit,
    )(in_hbm(out_packed), in_hbm(g_split), square_p, cube_p, facts, sums)
    other_root = flip(mine_root, 1)
    (middle,) = call(half_way, [whole], [VMEM] * 2, [split_square], flops=unit)(g_split, mine_root)
    mine, prec = call(last_product, [piece, (lax.axis_size("stripe"), 1, 128)], [VMEM] * 2, [split_square], flops=unit)(middle, other_root)

    bit = 2
    while bit < rep_count:
        prec = prec + flip(prec, bit)
        bit *= 2
    prec = prec + flip(prec, 1)
    direct, m = [mine], 1
    while m < pairs:
        direct = direct + [flip(x, 2 * m) for x in direct]
        m *= 2
    across = [flip(mine, 1)]
    prec = lax.all_to_all(prec, "stripe", 0, 0)
    (new_stat,) = call(unpack_stat, [square], [VMEM])(new_packed)
    slab = (pairs * BLOCK, out_grads.shape[1])

    def landing(count):
        return [pltpu.VMEM((count,) + piece, f32), pltpu.SemaphoreType.DMA((count * HALF // CHUNK,))]

    forwarded = [flip(x, 1) for x in direct[1:]]
    placed, scale = call(
        functools.partial(place_most, pairs),
        [slab, (1, 128)],
        [VMEM] * (pairs + 4),
        landing(pairs + 1),
        out_specs=[HBM, VMEM],
    )(*direct, across[0], prec, totals, rows)
    (placed,) = call(
        functools.partial(place_rest, pairs),
        [slab],
        [VMEM] * (pairs + 1) + [HBM],
        landing(pairs - 1),
        out_specs=[HBM],
        input_output_aliases={pairs + 1: 0},
    )(*forwarded, scale, rows, placed)
    return placed, new_stat[None, None]


def solution(mesh):
    in_specs = (
        P("rep", None),
        P("rep", "stripe"),
        P("rep", "stripe", None, None),
        P("stripe", None),
    )
    out_specs = (P(None, "stripe"), P("rep", "stripe", None, None))
    return jax.shard_map(per_device, mesh=mesh, in_specs=in_specs, out_specs=out_specs, check_vma=False)
```

```python
import functools
import math

import jax
import jax.numpy as jnp
from jax import lax
from jax.experimental import pallas as pl
from jax.experimental.pallas import tpu as pltpu
from jax.sharding import PartitionSpec as P


BLOCK = 512
HALF = BLOCK // 2
PACKED = HALF + 8
CHUNK = 64

decay_rate = 0.95
damping = 0.25
epsilon = 1e-06
AXES = ("rep", "stripe")
f32 = jnp.float32
bf16 = jnp.bfloat16

ROOT_COEFFS = (
    25 / 16,
    -5 / 16 - 3125 / 4096,
    3125 / 4096,
    -1250 / 4096,
    250 / 4096,
    -25 / 4096,
    1 / 4096,
)

VMEM = pl.BlockSpec(memory_space=pltpu.VMEM)
SMEM = pl.BlockSpec(memory_space=pltpu.SMEM)
HBM = pl.BlockSpec(memory_space=pltpu.HBM)
LOW = pl.ds(0, HALF)
TOP = pl.ds(HALF, HALF)


def call(body, out_shapes, in_specs, scratch=(), limit=16, flops=0, out_specs=None, **kwargs):
    return pl.pallas_call(
        body,
        out_shape=[jax.ShapeDtypeStruct(s, f32) if isinstance(s, tuple) else s for s in out_shapes],
        in_specs=in_specs,
        out_specs=out_specs or [VMEM] * len(out_shapes),
        scratch_shapes=list(scratch),
        compiler_params=pltpu.CompilerParams(vmem_limit_bytes=limit << 20),
        cost_estimate=pl.CostEstimate(flops=flops, bytes_accessed=1 << 20, transcendentals=0),
        **kwargs,
    )


def flip(x, mask):
    return lax.ppermute(x, "rep", [(i, i ^ mask) for i in range(lax.axis_size("rep"))])


def in_hbm(x):
    return pltpu.with_memory_space_constraint(x, pltpu.HBM)


def chip_core():
    me = lax.axis_index("rep")
    return lax.shift_right_logical(me, 1), lax.bitwise_and(me, 1)


def split(x):
    hi = x.astype(bf16)
    return hi, (x - hi.astype(f32)).astype(bf16)


def mm(a, b):
    return jnp.dot(a, b, preferred_element_type=f32)


def dot3(a, b):
    return mm(a[0], b[0]) + (mm(a[0], b[1]) + mm(a[1], b[0]))


def triangle():
    i = lax.broadcasted_iota(jnp.int32, (HALF, HALF), 0)
    j = lax.broadcasted_iota(jnp.int32, (HALF, HALF), 1)
    return i, j


def lanes(x):
    rows = jnp.sum(x, axis=0, keepdims=True)
    return sum(rows[:, k : k + 128] for k in range(0, x.shape[1], 128))


def pack_into(out, a, b, c):
    i, j = triangle()
    out[LOW, LOW] = jnp.where(i <= j, a, c)
    out[LOW, TOP] = b
    out[HALF:, LOW] = jnp.broadcast_to(jnp.sum(jnp.where(i == j, c, 0.0), axis=0, keepdims=True), (8, HALF))


def unpack(u, diag):
    i, j = triangle()
    ut = u.T
    return jnp.where(i <= j, u, ut), jnp.where(i > j, u, jnp.where(i < j, ut, diag))


def pack_stat(pairs, stat, owners, out, trace, rows):
    chip, core = chip_core()
    for n in range(2 * pairs):
        half = core if n < pairs else 1 - core
        row = owners[0, lax.bitwise_xor(chip, jnp.int32(n % pairs))] * BLOCK + half * HALF
        rows[n : n + 1, :] = jnp.full((1, 128), row.astype(f32))
    i, j = triangle()
    a, c = stat[LOW, LOW], stat[TOP, TOP]
    pack_into(out, a, stat[LOW, TOP], c)
    trace[...] = lanes(jnp.where(i == j, a + c, 0.0))


def grad_terms(plan, acts, grads, owners, *refs):
    outs, (av, gv, ov, sems) = refs[: len(plan)], refs[len(plan) :]
    chip, core = chip_core()
    copies = [
        pltpu.make_async_copy(src, dst, sems.at[k]) for k, (src, dst) in enumerate(((owners, ov), (acts, av), (grads, gv)))
    ]
    for copy in copies:
        copy.start()
    for copy in copies:
        copy.wait()
    cotangent = gv[...]
    for out, (chips, swapped) in zip(outs, plan):
        half = 1 - core if swapped else core
        for n, j in enumerate(chips):
            start = ov[0, chip ^ j] * BLOCK + half * HALF
            cols = av[:, pl.ds(pl.multiple_of(start, HALF), HALF)]
            out[n] = lax.dot_general(cols, cotangent, (((0,), (0,)), ((), ())), preferred_element_type=f32)


def finish_half(devices, keep, got, rest, trace, half, sums):
    value = keep[0] + got[0] + rest[...]
    half[...] = value
    both = jnp.concatenate([lanes(value * value), trace[...]], axis=0)
    sums[...] = jnp.broadcast_to(both[None], (devices, 2, 128))


def spread(top, corner, out):
    out[0, LOW], out[1, LOW] = split(top)
    out[0, TOP, TOP], out[1, TOP, TOP] = split(corner)
    for k in range(2):
        out[k, TOP, LOW] = out[k, LOW, TOP].T


def upper_product(a, b):
    top = dot3((a[0, LOW], a[1, LOW]), (b[0], b[1]))
    return top, dot3((a[0, TOP], a[1, TOP]), (b[0, :, TOP], b[1, :, TOP]))


def total(x):
    return jnp.sum(jnp.sum(x, axis=0, keepdims=True), axis=1, keepdims=True)


def load_gradient(core, half, other, g):
    mine = pl.ds(pl.multiple_of(core * HALF, HALF), HALF)
    theirs = pl.ds(pl.multiple_of(HALF - core * HALF, HALF), HALF)
    for rows, src in ((mine, half), (theirs, other)):
        g[0, rows], g[1, rows] = split(src[...])


def unpack_upper(packed):
    s00, s11 = unpack(packed[LOW, LOW], packed[HALF : HALF + 1, LOW])
    return jnp.concatenate([s00, packed[LOW, TOP]], axis=1), s11


def update_stat(half, other, old, facts, square_out, cube_out, out, g_out, g, s1, s2, stage, sems):
    _, core = chip_core()
    load_gradient(core, half, other, g.at[0])
    copies = [pltpu.make_async_copy(g.at[0], g_out, sems.at[0]), pltpu.make_async_copy(stage, out, sems.at[1])]
    copies[0].start()
    for k in range(2):
        g[1, k] = g[0, k].T
    top, corner = upper_product(g.at[1 - core], g.at[core])
    was_top, was_corner = unpack_upper(old)
    top = decay_rate * was_top + top
    corner = decay_rate * was_corner + corner
    s00, s01 = top[:, :HALF], top[:, HALF:]
    pack_into(stage, s00, s01, corner)
    copies[1].start()
    i, j = triangle()
    trace = total(jnp.where(i == j, s00 + corner, 0.0))
    norm_sq = total(s00 * s00 + corner * corner + 2.0 * (s01 * s01))
    inv = 1.0 / jnp.sqrt(norm_sq + epsilon)
    spread(top * inv, corner * inv, s1)
    top, corner = upper_product(s1, s1)
    pack_into(square_out, top[:, :HALF], top[:, HALF:], corner)
    spread(top, corner, s2)
    top, corner = upper_product(s1, s2)
    pack_into(cube_out, top[:, :HALF], top[:, HALF:], corner)
    facts[...] = jnp.concatenate([jnp.broadcast_to(x, (1, 128)) for x in (norm_sq, trace)], axis=0)
    for copy in copies:
        copy.wait()


def coefficients(devices, facts, sums):
    both = jnp.sum(jnp.sum(sums[...], axis=0), axis=1, keepdims=True)
    grad_sq, trace_all = both[0:1], both[1:2]
    shift = (decay_rate * trace_all + 2.0 * grad_sq) * (damping / (devices * BLOCK))
    shift = jnp.broadcast_to(shift, (1, 128))
    norm_sq, trace = facts[0:1, :], facts[1:2, :]
    frob = jnp.sqrt(norm_sq + 2.0 * shift * trace + BLOCK * shift * shift + epsilon)
    a = jnp.sqrt(norm_sq + epsilon) / frob
    e = shift / frob
    outer = 1.0 / jnp.sqrt(jnp.sqrt(frob))
    k = []
    for i in range(7):
        value = jnp.full_like(e, ROOT_COEFFS[6] * math.comb(6, i))
        for j in range(5, i - 1, -1):
            value = value * e + math.comb(j, i) * ROOT_COEFFS[j]
        k.append((outer * value)[:, 0:1])
        outer = outer * a
    return k, grad_sq


def root(devices, stat_in, g_in, square, cubed, facts, sums, out, totals, g, stat, inner, cube, sems):
    copy = pltpu.make_async_copy(stat_in, stat, sems.at[0])
    fetch = pltpu.make_async_copy(g_in, g, sems.at[1])
    copy.start()
    fetch.start()
    k, grad_sq = coefficients(devices, facts, sums)
    inv = 1.0 / jnp.sqrt(facts[0:1, 0:1] + epsilon)
    third = unpack_upper(cubed)
    spread(*third, cube)
    second = unpack_upper(square)
    copy.wait()
    first = [x * inv for x in unpack_upper(stat)]
    tops, corners = zip(first, second, third)
    spread(*(k[4] * t[0] + k[5] * t[1] + k[6] * t[2] for t in (tops, corners)), inner)
    top, corner = upper_product(cube, inner)
    i, j = triangle()
    diag = jnp.where(i == j, k[0], 0.0)
    low = k[1] * tops[0] + k[2] * tops[1] + k[3] * tops[2] + top
    out[LOW, LOW] = low[:, :HALF] + diag
    out[LOW, TOP] = low[:, HALF:]
    corner = k[1] * corners[0] + k[2] * corners[1] + k[3] * corners[2] + corner + diag
    out[HALF:, LOW] = corner[: HALF // 2]
    out[HALF:, TOP] = corner[HALF // 2 :]
    totals[...] = jnp.broadcast_to(grad_sq, (1, 128))
    fetch.wait()


def root_corner(packed):
    return jnp.concatenate([packed[HALF:, LOW], packed[HALF:, TOP]], axis=0)


def half_way(g, packed, out, x):
    _, core = chip_core()
    spread(packed[LOW], root_corner(packed), x)

    @pl.when(core == 1)
    def _():
        y = dot3((x[0, TOP], x[1, TOP]), (g[0], g[1]))
        out[0, LOW], out[1, LOW] = split(y)

    @pl.when(core == 0)
    def _():
        out[0], out[1] = split(dot3((g[0], g[1]), (x[0], x[1])))


def last_product(middle, packed, mine, sums, x):
    _, core = chip_core()

    @pl.when(core == 1)
    def _():
        spread(packed[LOW], root_corner(packed), x)
        mine[...] = dot3((middle[0, LOW], middle[1, LOW]), (x[0], x[1]))

    @pl.when(core == 0)
    def _():
        mine[...] = dot3(split(packed[LOW]), (middle[0], middle[1]))

    sums[...] = jnp.broadcast_to(lanes(mine[...] * mine[...])[None], sums.shape)


def unpack_stat(packed, out):
    sa, sc = unpack(packed[LOW, LOW], packed[HALF : HALF + 1, LOW])
    off = packed[LOW, TOP]
    out[LOW, LOW] = sa
    out[LOW, TOP] = off
    out[TOP, LOW] = off.T
    out[TOP, TOP] = sc


def write_pieces(pieces, scale, out, scaled, sems):
    copies = []
    for n, (base, src) in enumerate(pieces):
        for r in range(0, HALF, CHUNK):
            scaled[n, pl.ds(r, CHUNK)] = src[pl.ds(r, CHUNK)] * scale
            start = pl.multiple_of(base + r, CHUNK)
            copies.append(
                pltpu.make_async_copy(scaled.at[n, pl.ds(r, CHUNK)], out.at[pl.ds(start, CHUNK)], sems.at[len(copies)])
            )
            copies[-1].start()
    for copy in copies:
        copy.wait()


def first_row(rows, n):
    return jnp.max(rows[n : n + 1, :]).astype(jnp.int32)


def place_most(pairs, *refs):
    direct, (across, sums, totals, rows, out, scale, scaled, sems) = refs[:pairs], refs[pairs:]
    prec_sq = jnp.sum(jnp.sum(sums[...], axis=0), axis=1, keepdims=True)
    factor = jnp.sqrt(totals[0:1, 0:1] / (prec_sq + epsilon))
    scale[...] = jnp.broadcast_to(factor, (1, 128))
    pieces = [(first_row(rows, pairs), across)] + [(first_row(rows, n), x) for n, x in enumerate(direct)]
    write_pieces(pieces, factor, out, scaled, sems)


def place_rest(pairs, *refs):
    across, (scale, rows, _, out, scaled, sems) = refs[: pairs - 1], refs[pairs - 1 :]
    pieces = [(first_row(rows, pairs + n), x) for n, x in enumerate(across, 1)]
    write_pieces(pieces, scale[0:1, 0:1], out, scaled, sems)


def per_device(activations, out_grads, statistics, owner_blocks):
    rep_count = lax.axis_size("rep")
    pairs = rep_count // 2
    devices = rep_count * lax.axis_size("stripe")
    stripes = lax.axis_size("stripe")
    tokens = activations.shape[0]
    piece, square = (HALF, BLOCK), (BLOCK, BLOCK)
    unit = 6 * BLOCK**3

    whole = jax.ShapeDtypeStruct((2,) + square, bf16)
    split_square = pltpu.VMEM((2,) + square, bf16)
    packed_buffer = pltpu.VMEM((PACKED, BLOCK), f32)
    m = pairs // 2

    def terms(*plan):
        return call(
            functools.partial(grad_terms, plan),
            [(len(chips),) + piece for chips, _ in plan],
            [HBM] * 3,
            [
                pltpu.VMEM(activations.shape, bf16),
                pltpu.VMEM(out_grads.shape, bf16),
                pltpu.SMEM(owner_blocks.shape, jnp.int32),
                pltpu.SemaphoreType.DMA((3,)),
            ],
            flops=2 * tokens * HALF * BLOCK * sum(len(chips) for chips, _ in plan),
        )(*(in_hbm(x) for x in (activations, out_grads, owner_blocks)))

    above, below = range(m, pairs), range(m)
    (send_far,) = terms((above, True))
    got_far = flip(send_far, 1)
    keep_far, send_near, keep_near = terms((above, False), (below, True), (below, False))
    got_near = flip(send_near, 1)
    arrived = [flip(keep_far[j] + got_far[j], 2 * m) for j in range(m)]
    while m > 1:
        m //= 2
        held = [keep_near[j] + got_near[j] + arrived[j] for j in range(m, 2 * m)]
        arrived = [x + flip(y, 2 * m) for x, y in zip(arrived, held)]
    shuffle = [(s * pairs + p, 2 * p + 1 - s) for s in range(2) for p in range(pairs)]
    packed, trace, rows = call(
        functools.partial(pack_stat, pairs), [(PACKED, BLOCK), (1, 128), (2 * pairs, 128)], [VMEM, SMEM]
    )(statistics[0, 0], owner_blocks)
    old = lax.ppermute(packed, "rep", shuffle)
    half, sums = call(
        functools.partial(finish_half, devices), [piece, (devices, 2, 128)], [VMEM] * 4
    )(keep_near, got_near, arrived[0], trace)
    other = flip(half, 1)
    sums = lax.all_to_all(sums, AXES, 0, 0)
    facts, square_p, cube_p, out_packed, g_split = call(
        update_stat,
        [(2, 128), (PACKED, BLOCK), (PACKED, BLOCK)]
        + [pltpu.HBM((PACKED, BLOCK), f32), pltpu.HBM((2,) + square, bf16)],
        [VMEM] * 3,
        [pltpu.VMEM((2, 2) + square, bf16), split_square, split_square, packed_buffer, pltpu.SemaphoreType.DMA((2,))],
        flops=3 * unit,
        out_specs=[VMEM] * 3 + [HBM] * 2,
        input_output_aliases={2: 1},
    )(half, other, old)
    new_packed = lax.ppermute(out_packed, "rep", [(t, s) for s, t in shuffle])
    mine_root, totals, g_split = call(
        functools.partial(root, devices),
        [(HALF + HALF // 2, BLOCK), (1, 128), whole],
        [HBM] * 2 + [VMEM] * 4,
        [packed_buffer, split_square, split_square, pltpu.SemaphoreType.DMA((2,))],
        flops=unit,
    )(in_hbm(out_packed), in_hbm(g_split), square_p, cube_p, facts, sums)
    other_root = flip(mine_root, 1)
    (middle,) = call(half_way, [whole], [VMEM] * 2, [split_square], flops=unit)(g_split, mine_root)
    mine, prec = call(last_product, [piece, (2 * stripes, 1, 128)], [VMEM] * 2, [split_square], flops=unit)(middle, other_root)

    bit = 2
    while bit < rep_count:
        prec = prec + flip(prec, bit)
        bit *= 2
    direct, m = [mine], 1
    while m < pairs:
        direct = direct + [flip(x, 2 * m) for x in direct]
        m *= 2
    across = [flip(mine, 1)]
    near = [(s + stripes // 4) % stripes for s in range(stripes)]
    groups = [[(2 * q + c) * stripes + s for s in near for c in range(2)] for q in range(pairs)]
    prec = lax.all_to_all(prec, AXES, 0, 0, axis_index_groups=groups)
    (new_stat,) = call(unpack_stat, [square], [VMEM])(new_packed)
    slab = (pairs * BLOCK, out_grads.shape[1])

    def landing(count):
        return [pltpu.VMEM((count,) + piece, f32), pltpu.SemaphoreType.DMA((count * HALF // CHUNK,))]

    forwarded = [flip(x, 1) for x in direct[1:]]
    placed, scale = call(
        functools.partial(place_most, pairs),
        [slab, (1, 128)],
        [VMEM] * (pairs + 4),
        landing(pairs + 1),
        out_specs=[HBM, VMEM],
    )(*direct, across[0], prec, totals, rows)
    (placed,) = call(
        functools.partial(place_rest, pairs),
        [slab],
        [VMEM] * (pairs + 1) + [HBM],
        landing(pairs - 1),
        out_specs=[HBM],
        input_output_aliases={pairs + 1: 0},
    )(*forwarded, scale, rows, placed)
    return placed, new_stat[None, None]


def solution(mesh):
    in_specs = (
        P("rep", None),
        P("rep", "stripe"),
        P("rep", "stripe", None, None),
        P("stripe", None),
    )
    out_specs = (P(None, "stripe"), P("rep", "stripe", None, None))
    return jax.shard_map(per_device, mesh=mesh, in_specs=in_specs, out_specs=out_specs, check_vma=False)
```

```python
import functools
import math

import jax
import jax.numpy as jnp
from jax import lax
from jax.experimental import pallas as pl
from jax.experimental.pallas import tpu as pltpu
from jax.sharding import PartitionSpec as P


BLOCK = 512
HALF = BLOCK // 2
PACKED = HALF + 8
CHUNK = 64
MOST = HALF - 64

decay_rate = 0.95
damping = 0.25
epsilon = 1e-06
AXES = ("rep", "stripe")
f32 = jnp.float32
bf16 = jnp.bfloat16

ROOT_COEFFS = (
    25 / 16,
    -5 / 16 - 3125 / 4096,
    3125 / 4096,
    -1250 / 4096,
    250 / 4096,
    -25 / 4096,
    1 / 4096,
)
SMALL_CUBIC = (-1 / 32, 9 / 16, -3 / 2, 1.0)


def quotient(poly, divisor):
    rest, out = list(poly), []
    for i in range(len(poly) - len(divisor), -1, -1):
        out.insert(0, rest[i + len(divisor) - 1])
        for n, d in enumerate(divisor):
            rest[i + n] -= out[0] * d
    return out, rest[: len(divisor) - 1]


ROOT_FACTOR, ROOT_REST = quotient(ROOT_COEFFS, SMALL_CUBIC)

VMEM = pl.BlockSpec(memory_space=pltpu.VMEM)
SMEM = pl.BlockSpec(memory_space=pltpu.SMEM)
HBM = pl.BlockSpec(memory_space=pltpu.HBM)
LOW = pl.ds(0, HALF)
TOP = pl.ds(HALF, HALF)


def call(body, out_shapes, in_specs, scratch=(), limit=16, flops=0, out_specs=None, **kwargs):
    return pl.pallas_call(
        body,
        out_shape=[jax.ShapeDtypeStruct(s, f32) if isinstance(s, tuple) else s for s in out_shapes],
        in_specs=in_specs,
        out_specs=out_specs or [VMEM] * len(out_shapes),
        scratch_shapes=list(scratch),
        compiler_params=pltpu.CompilerParams(vmem_limit_bytes=limit << 20),
        cost_estimate=pl.CostEstimate(flops=flops, bytes_accessed=1 << 20, transcendentals=0),
        **kwargs,
    )


def flip(x, mask):
    return lax.ppermute(x, "rep", [(i, i ^ mask) for i in range(lax.axis_size("rep"))])


def in_hbm(x):
    return pltpu.with_memory_space_constraint(x, pltpu.HBM)


def chip_core():
    me = lax.axis_index("rep")
    return lax.shift_right_logical(me, 1), lax.bitwise_and(me, 1)


def split(x):
    hi = x.astype(bf16)
    return hi, (x - hi.astype(f32)).astype(bf16)


def mm(a, b):
    return jnp.dot(a, b, preferred_element_type=f32)


def dot3(a, b):
    return mm(a[0], b[0]) + (mm(a[0], b[1]) + mm(a[1], b[0]))


def triangle():
    i = lax.broadcasted_iota(jnp.int32, (HALF, HALF), 0)
    j = lax.broadcasted_iota(jnp.int32, (HALF, HALF), 1)
    return i, j


def lanes(x):
    rows = jnp.sum(x, axis=0, keepdims=True)
    return sum(rows[:, k : k + 128] for k in range(0, x.shape[1], 128))


def pack_into(out, a, b, c):
    i, j = triangle()
    out[LOW, LOW] = jnp.where(i <= j, a, c)
    out[LOW, TOP] = b
    out[HALF:, LOW] = jnp.broadcast_to(jnp.sum(jnp.where(i == j, c, 0.0), axis=0, keepdims=True), (8, HALF))


def unpack(u, diag):
    i, j = triangle()
    ut = u.T
    return jnp.where(i <= j, u, ut), jnp.where(i > j, u, jnp.where(i < j, ut, diag))


def pack_stat(pairs, stat, owners, out, trace, rows):
    chip, core = chip_core()
    for n in range(2 * pairs):
        half = core if n < pairs else 1 - core
        row = owners[0, lax.bitwise_xor(chip, jnp.int32(n % pairs))] * BLOCK + half * HALF
        rows[n : n + 1, :] = jnp.full((1, 128), row.astype(f32))
    i, j = triangle()
    a, c = stat[LOW, LOW], stat[TOP, TOP]
    pack_into(out, a, stat[LOW, TOP], c)
    trace[...] = lanes(jnp.where(i == j, a + c, 0.0))


def grad_terms(plan, acts, grads, owners, *refs):
    outs, (av, gv, ov, sems) = refs[: len(plan)], refs[len(plan) :]
    chip, core = chip_core()
    parts = [(owners, ov)]
    for src, dst in ((grads, gv), (acts, av)):
        parts += [(src.at[pl.ds(r, CHUNK)], dst.at[pl.ds(r, CHUNK)]) for r in range(0, src.shape[0], CHUNK)]
    copies = [pltpu.make_async_copy(src, dst, sems.at[k]) for k, (src, dst) in enumerate(parts)]
    for copy in copies:
        copy.start()
    for copy in copies:
        copy.wait()
    cotangent = gv[...]
    for out, (chips, swapped) in zip(outs, plan):
        half = 1 - core if swapped else core
        for n, j in enumerate(chips):
            start = ov[0, chip ^ j] * BLOCK + half * HALF
            cols = av[:, pl.ds(pl.multiple_of(start, HALF), HALF)]
            out[n] = lax.dot_general(cols, cotangent, (((0,), (0,)), ((), ())), preferred_element_type=f32)


def finish_half(devices, keep, got, rest, trace, half, sums):
    value = keep[0] + got[0] + rest[...]
    half[LOW] = value
    half[HALF:] = jnp.zeros((PACKED - HALF, BLOCK), f32)
    both = jnp.concatenate([lanes(value * value), trace[...]], axis=0)
    sums[...] = jnp.broadcast_to(both[None], (devices, 2, 128))


def spread(top, corner, out):
    out[0, LOW], out[1, LOW] = split(top)
    out[0, TOP, TOP], out[1, TOP, TOP] = split(corner)
    for k in range(2):
        out[k, TOP, LOW] = out[k, LOW, TOP].T


def upper_product(a, b):
    top = dot3((a[0, LOW], a[1, LOW]), (b[0], b[1]))
    return top, dot3((a[0, TOP], a[1, TOP]), (b[0, :, TOP], b[1, :, TOP]))


def total(x):
    return jnp.sum(jnp.sum(x, axis=0, keepdims=True), axis=1, keepdims=True)


def load_gradient(core, half, other, g):
    mine = pl.ds(pl.multiple_of(core * HALF, HALF), HALF)
    theirs = pl.ds(pl.multiple_of(HALF - core * HALF, HALF), HALF)
    for rows, src in ((mine, half), (theirs, other)):
        g[0, rows], g[1, rows] = split(src[LOW])


def unpack_upper(packed):
    s00, s11 = unpack(packed[LOW, LOW], packed[HALF : HALF + 1, LOW])
    return jnp.concatenate([s00, packed[LOW, TOP]], axis=1), s11


def update_stat(half, other, old, facts, square_out, cube_out, out, g_out, g, s1, s2, sem):
    _, core = chip_core()
    load_gradient(core, half, other, g.at[0])
    copy = pltpu.make_async_copy(g.at[0], g_out, sem)
    copy.start()
    for k in range(2):
        g[1, k] = g[0, k].T
    top, corner = upper_product(g.at[1 - core], g.at[core])
    was_top, was_corner = unpack_upper(old)
    top = decay_rate * was_top + top
    corner = decay_rate * was_corner + corner
    s00, s01 = top[:, :HALF], top[:, HALF:]
    pack_into(out, s00, s01, corner)
    i, j = triangle()
    trace = total(jnp.where(i == j, s00 + corner, 0.0))
    norm_sq = total(s00 * s00 + corner * corner + 2.0 * (s01 * s01))
    inv = 1.0 / jnp.sqrt(norm_sq + epsilon)
    spread(top * inv, corner * inv, s1)
    top, corner = upper_product(s1, s1)
    pack_into(square_out, top[:, :HALF], top[:, HALF:], corner)
    spread(top, corner, s2)
    top, corner = upper_product(s1, s2)
    pack_into(cube_out, top[:, :HALF], top[:, HALF:], corner)
    facts[...] = jnp.concatenate([jnp.broadcast_to(x, (1, 128)) for x in (norm_sq, trace)], axis=0)
    copy.wait()


def coefficients(devices, facts, sums):
    both = jnp.sum(jnp.sum(sums[...], axis=0), axis=1, keepdims=True)
    grad_sq, trace_all = both[0:1], both[1:2]
    shift = (decay_rate * trace_all + 2.0 * grad_sq) * (damping / (devices * BLOCK))
    shift = jnp.broadcast_to(shift, (1, 128))
    norm_sq, trace = facts[0:1, :], facts[1:2, :]
    frob = jnp.sqrt(norm_sq + 2.0 * shift * trace + BLOCK * shift * shift + epsilon)
    a = jnp.sqrt(norm_sq + epsilon) / frob
    e = shift / frob

    def taken(poly, outer):
        out = []
        for i in range(len(poly)):
            value = jnp.full_like(e, poly[-1] * math.comb(len(poly) - 1, i))
            for j in range(len(poly) - 2, i - 1, -1):
                value = value * e + math.comb(j, i) * poly[j]
            out.append((outer * value)[:, 0:1])
            outer = outer * a
        return out

    outer = 1.0 / jnp.sqrt(jnp.sqrt(frob))
    return taken(SMALL_CUBIC, jnp.ones_like(e)), taken(ROOT_FACTOR, outer), taken(ROOT_REST, outer), grad_sq


def root(devices, stat, g_in, square, cubed, facts, sums, out, totals, g, left, right, sem):
    fetch = pltpu.make_async_copy(g_in, g, sem)
    fetch.start()
    small, factor, rest, grad_sq = coefficients(devices, facts, sums)
    inv = 1.0 / jnp.sqrt(facts[0:1, 0:1] + epsilon)
    i, j = triangle()
    on_diagonal = i == j

    def polynomial(k, powers, part):
        value = sum(k[n] * powers[n - 1][part] for n in range(1, len(k)))
        if part == 1:
            return value + jnp.where(on_diagonal, k[0], 0.0)
        return jnp.concatenate([value[:, :HALF] + jnp.where(on_diagonal, k[0], 0.0), value[:, HALF:]], axis=1)

    powers = [[x * inv for x in unpack_upper(stat)], unpack_upper(square), unpack_upper(cubed)]
    for dst, k in ((left, small), (right, factor)):
        dst[LOW] = polynomial(k, powers, 0).astype(bf16)
        dst[TOP, TOP] = polynomial(k, powers, 1).astype(bf16)
        dst[TOP, LOW] = dst[LOW, TOP].T
    out[LOW] = mm(left[LOW], right[...]) + polynomial(rest, powers, 0)
    corner = mm(left[TOP], right[:, TOP]) + polynomial(rest, powers, 1)
    out[HALF:, LOW] = corner[: HALF // 2]
    out[HALF:, TOP] = corner[HALF // 2 :]
    totals[...] = jnp.broadcast_to(grad_sq, (1, 128))
    fetch.wait()


def root_corner(packed):
    return jnp.concatenate([packed[HALF:, LOW], packed[HALF:, TOP]], axis=0)


def half_way(g, packed, out, x):
    _, core = chip_core()
    spread(packed[LOW], root_corner(packed), x)

    @pl.when(core == 1)
    def _():
        y = dot3((x[0, TOP], x[1, TOP]), (g[0], g[1]))
        out[0, LOW], out[1, LOW] = split(y)

    @pl.when(core == 0)
    def _():
        out[0], out[1] = split(dot3((g[0], g[1]), (x[0], x[1])))


def last_product(middle, packed, mine, most, rest, sums, x):
    _, core = chip_core()

    @pl.when(core == 1)
    def _():
        spread(packed[LOW], root_corner(packed), x)
        mine[...] = dot3((middle[0, LOW], middle[1, LOW]), (x[0], x[1]))

    @pl.when(core == 0)
    def _():
        mine[...] = dot3(split(packed[LOW]), (middle[0], middle[1]))

    most[...], rest[...] = mine[:MOST], mine[MOST:]
    sums[...] = jnp.broadcast_to(lanes(mine[...] * mine[...])[None], sums.shape)


def unpack_stat(packed, out):
    sa, sc = unpack(packed[LOW, LOW], packed[HALF : HALF + 1, LOW])
    off = packed[LOW, TOP]
    out[LOW, LOW] = sa
    out[LOW, TOP] = off
    out[TOP, LOW] = off.T
    out[TOP, TOP] = sc


def write_pieces(pieces, scale, out, scaled, sems):
    copies, base = [], 0
    for first, src in pieces:
        for r in range(0, src.shape[0], CHUNK):
            here = pl.ds(base + r, CHUNK)
            scaled[here] = src[pl.ds(r, CHUNK)] * scale
            start = pl.multiple_of(first + r, CHUNK)
            copies.append(pltpu.make_async_copy(scaled.at[here], out.at[pl.ds(start, CHUNK)], sems.at[len(copies)]))
            copies[-1].start()
        base += src.shape[0]
    for copy in copies:
        copy.wait()


def first_row(rows, n):
    return jnp.max(rows[n : n + 1, :]).astype(jnp.int32)


def place_first(plan, *refs):
    found, (sums, totals, rows, out, scale, scaled, sems) = refs[: len(plan)], refs[len(plan) :]
    prec_sq = jnp.sum(jnp.sum(sums[...], axis=0), axis=1, keepdims=True)
    factor = jnp.sqrt(totals[0:1, 0:1] / (prec_sq + epsilon))
    scale[...] = jnp.broadcast_to(factor, (1, 128))
    write_pieces([(first_row(rows, n) + r, x) for (n, r), x in zip(plan, found)], factor, out, scaled, sems)


def place_next(plan, *refs):
    found, (scale, rows, _, out, scaled, sems) = refs[: len(plan)], refs[len(plan) :]
    write_pieces(
        [(first_row(rows, n) + r, x) for (n, r), x in zip(plan, found)], scale[0:1, 0:1], out, scaled, sems
    )


def per_device(activations, out_grads, statistics, owner_blocks):
    rep_count = lax.axis_size("rep")
    pairs = rep_count // 2
    devices = rep_count * lax.axis_size("stripe")
    stripes = lax.axis_size("stripe")
    tokens = activations.shape[0]
    piece, square = (HALF, BLOCK), (BLOCK, BLOCK)
    unit = 6 * BLOCK**3

    whole = jax.ShapeDtypeStruct((2,) + square, bf16)
    split_square = pltpu.VMEM((2,) + square, bf16)
    m = pairs // 2

    def terms(*plan):
        return call(
            functools.partial(grad_terms, plan),
            [(len(chips),) + piece for chips, _ in plan],
            [HBM] * 3,
            [
                pltpu.VMEM(activations.shape, bf16),
                pltpu.VMEM(out_grads.shape, bf16),
                pltpu.SMEM(owner_blocks.shape, jnp.int32),
                pltpu.SemaphoreType.DMA((1 + 2 * (tokens // CHUNK),)),
            ],
            flops=2 * tokens * HALF * BLOCK * sum(len(chips) for chips, _ in plan),
        )(*(in_hbm(x) for x in (activations, out_grads, owner_blocks)))

    above, below = range(m, pairs), range(m)
    (send_far,) = terms((above, True))
    got_far = flip(send_far, 1)
    keep_far, send_near, keep_near = terms((above, False), (below, True), (below, False))
    got_near = flip(send_near, 1)
    arrived = [flip(keep_far[j] + got_far[j], 2 * m) for j in range(m)]
    while m > 1:
        m //= 2
        held = [keep_near[j] + got_near[j] + arrived[j] for j in range(m, 2 * m)]
        arrived = [x + flip(y, 2 * m) for x, y in zip(arrived, held)]
    shuffle = [(s * pairs + p, 2 * p + 1 - s) for s in range(2) for p in range(pairs)]
    packed, trace, rows = call(
        functools.partial(pack_stat, pairs), [(PACKED, BLOCK), (1, 128), (2 * pairs, 128)], [VMEM, SMEM]
    )(statistics[0, 0], owner_blocks)
    old = lax.ppermute(packed, "rep", shuffle)
    half, sums = call(
        functools.partial(finish_half, devices), [(PACKED, BLOCK), (devices, 2, 128)], [VMEM] * 4
    )(keep_near, got_near, arrived[0], trace)
    other = flip(half, 1)
    sums = lax.all_to_all(sums, AXES, 0, 0)
    facts, square_p, cube_p, out_packed, g_split = call(
        update_stat,
        [(2, 128)] + [(PACKED, BLOCK)] * 3 + [pltpu.HBM((2,) + square, bf16)],
        [VMEM] * 3,
        [pltpu.VMEM((2, 2) + square, bf16), split_square, split_square, pltpu.SemaphoreType.DMA],
        flops=3 * unit,
        out_specs=[VMEM] * 4 + [HBM],
        input_output_aliases={0: 3, 1: 2, 2: 1},
    )(half, other, old)
    new_packed = lax.ppermute(out_packed, "rep", [(t, s) for s, t in shuffle])
    mine_root, totals, g_split = call(
        functools.partial(root, devices),
        [(HALF + HALF // 2, BLOCK), (1, 128), whole],
        [VMEM, HBM] + [VMEM] * 4,
        [pltpu.VMEM(square, bf16)] * 2 + [pltpu.SemaphoreType.DMA],
        flops=unit,
    )(out_packed, in_hbm(g_split), square_p, cube_p, facts, sums)
    other_root = flip(mine_root, 1)
    (middle,) = call(half_way, [whole], [VMEM] * 2, [split_square], flops=unit)(g_split, mine_root)
    mine, most, rest, prec = call(last_product, [piece, (MOST, BLOCK), (HALF - MOST, BLOCK), (2 * stripes, 1, 128)], [VMEM] * 2, [split_square], flops=unit)(middle, other_root)

    bit = 2
    while bit < rep_count:
        prec = prec + flip(prec, bit)
        bit *= 2

    def spread_over_chips(x):
        found, bit = [x], 2
        while bit < rep_count:
            found = found + [flip(y, bit) for y in found]
            bit *= 2
        return found[1:]

    most = spread_over_chips(most)
    rest = spread_over_chips(rest)
    across = flip(mine, 1)
    near = [(s + stripes // 4) % stripes for s in range(stripes)]
    groups = [[(2 * q + c) * stripes + s for s in near for c in range(2)] for q in range(pairs)]
    prec = lax.all_to_all(prec, AXES, 0, 0, axis_index_groups=groups)
    (new_stat,) = call(unpack_stat, [square], [VMEM])(new_packed)
    slab = (pairs * BLOCK, out_grads.shape[1])

    def landing(found):
        count = sum(x.shape[0] for x in found)
        return [pltpu.VMEM((count, BLOCK), f32), pltpu.SemaphoreType.DMA((count // CHUNK,))]

    def place(placed, plan, *found):
        (placed,) = call(
            functools.partial(place_next, plan),
            [slab],
            [VMEM] * (len(plan) + 2) + [HBM],
            landing(found),
            out_specs=[HBM],
            input_output_aliases={len(plan) + 2: 0},
        )(*found, scale, rows, placed)
        return placed

    far = range(1, pairs)
    plan, found = [(0, 0), (pairs, 0)], (mine, across)
    placed, scale = call(
        functools.partial(place_first, plan), [slab, (1, 128)], [VMEM] * 5, landing(found), out_specs=[HBM, VMEM]
    )(*found, prec, totals, rows)
    most_across = [flip(x, 1) for x in most]
    rest_across = [flip(x, 1) for x in rest]
    plan = [(j, 0) for j in far] + [(pairs + j, 0) for j in far] + [(j, MOST) for j in far]
    placed = place(placed, plan, *most, *most_across, *rest)
    placed = place(placed, [(pairs + j, MOST) for j in far], *rest_across)
    return placed, new_stat[None, None]


def solution(mesh):
    in_specs = (
        P("rep", None),
        P("rep", "stripe"),
        P("rep", "stripe", None, None),
        P("stripe", None),
    )
    out_specs = (P(None, "stripe"), P("rep", "stripe", None, None))
    return jax.shard_map(per_device, mesh=mesh, in_specs=in_specs, out_specs=out_specs, check_vma=False)
```

```python
import functools
import math

import jax
import jax.numpy as jnp
from jax import lax
from jax.experimental import pallas as pl
from jax.experimental.pallas import tpu as pltpu
from jax.sharding import PartitionSpec as P


BLOCK = 512
HALF = BLOCK // 2
PACKED = HALF + 8
CHUNK = 64
MOST = HALF - 64

decay_rate = 0.95
damping = 0.25
epsilon = 1e-06
AXES = ("rep", "stripe")
f32 = jnp.float32
bf16 = jnp.bfloat16

ROOT_COEFFS = (
    25 / 16,
    -5 / 16 - 3125 / 4096,
    3125 / 4096,
    -1250 / 4096,
    250 / 4096,
    -25 / 4096,
    1 / 4096,
)
SMALL_CUBIC = (-1 / 32, 9 / 16, -3 / 2, 1.0)


def quotient(poly, divisor):
    rest, out = list(poly), []
    for i in range(len(poly) - len(divisor), -1, -1):
        out.insert(0, rest[i + len(divisor) - 1])
        for n, d in enumerate(divisor):
            rest[i + n] -= out[0] * d
    return out, rest[: len(divisor) - 1]


ROOT_FACTOR, ROOT_REST = quotient(ROOT_COEFFS, SMALL_CUBIC)

VMEM = pl.BlockSpec(memory_space=pltpu.VMEM)
SMEM = pl.BlockSpec(memory_space=pltpu.SMEM)
HBM = pl.BlockSpec(memory_space=pltpu.HBM)
LOW = pl.ds(0, HALF)
TOP = pl.ds(HALF, HALF)


def call(body, out_shapes, in_specs, scratch=(), limit=16, flops=0, out_specs=None, **kwargs):
    return pl.pallas_call(
        body,
        out_shape=[jax.ShapeDtypeStruct(s, f32) if isinstance(s, tuple) else s for s in out_shapes],
        in_specs=in_specs,
        out_specs=out_specs or [VMEM] * len(out_shapes),
        scratch_shapes=list(scratch),
        compiler_params=pltpu.CompilerParams(vmem_limit_bytes=limit << 20),
        cost_estimate=pl.CostEstimate(flops=flops, bytes_accessed=1 << 20, transcendentals=0),
        **kwargs,
    )


def flip(x, mask):
    return lax.ppermute(x, "rep", [(i, i ^ mask) for i in range(lax.axis_size("rep"))])


def in_hbm(x):
    return pltpu.with_memory_space_constraint(x, pltpu.HBM)


def chip_core():
    me = lax.axis_index("rep")
    return lax.shift_right_logical(me, 1), lax.bitwise_and(me, 1)


def split(x):
    hi = x.astype(bf16)
    return hi, (x - hi.astype(f32)).astype(bf16)


def mm(a, b):
    return jnp.dot(a, b, preferred_element_type=f32)


def dot3(a, b):
    return mm(a[0], b[0]) + (mm(a[0], b[1]) + mm(a[1], b[0]))


def triangle():
    i = lax.broadcasted_iota(jnp.int32, (HALF, HALF), 0)
    j = lax.broadcasted_iota(jnp.int32, (HALF, HALF), 1)
    return i, j


def lanes(x):
    rows = jnp.sum(x, axis=0, keepdims=True)
    return sum(rows[:, k : k + 128] for k in range(0, x.shape[1], 128))


def pack_into(out, a, b, c):
    i, j = triangle()
    out[LOW, LOW] = jnp.where(i <= j, a, c)
    out[LOW, TOP] = b
    out[HALF:, LOW] = jnp.broadcast_to(jnp.sum(jnp.where(i == j, c, 0.0), axis=0, keepdims=True), (8, HALF))


def unpack(u, diag):
    i, j = triangle()
    ut = u.T
    return jnp.where(i <= j, u, ut), jnp.where(i > j, u, jnp.where(i < j, ut, diag))


def pack_stat(pairs, stat, owners, out, trace, rows):
    chip, core = chip_core()
    for n in range(2 * pairs):
        half = core if n < pairs else 1 - core
        row = owners[0, lax.bitwise_xor(chip, jnp.int32(n % pairs))] * BLOCK + half * HALF
        rows[n : n + 1, :] = jnp.full((1, 128), row.astype(f32))
    i, j = triangle()
    a, c = stat[LOW, LOW], stat[TOP, TOP]
    pack_into(out, a, stat[LOW, TOP], c)
    trace[...] = lanes(jnp.where(i == j, a + c, 0.0))


def grad_terms(plan, acts, grads, owners, *refs):
    outs, (av, gv, ov, sems) = refs[: len(plan)], refs[len(plan) :]
    chip, core = chip_core()
    copies = [
        pltpu.make_async_copy(src, dst, sems.at[k]) for k, (src, dst) in enumerate(((owners, ov), (acts, av), (grads, gv)))
    ]
    for copy in copies:
        copy.start()
    for copy in copies:
        copy.wait()
    cotangent = gv[...]
    for out, (chips, swapped) in zip(outs, plan):
        half = 1 - core if swapped else core
        for n, j in enumerate(chips):
            start = ov[0, chip ^ j] * BLOCK + half * HALF
            cols = av[:, pl.ds(pl.multiple_of(start, HALF), HALF)]
            out[n] = lax.dot_general(cols, cotangent, (((0,), (0,)), ((), ())), preferred_element_type=f32)


def finish_half(devices, keep, got, rest, trace, half, sums):
    value = keep[0] + got[0] + rest[...]
    half[LOW] = value
    half[HALF:] = jnp.zeros((PACKED - HALF, BLOCK), f32)
    both = jnp.concatenate([lanes(value * value), trace[...]], axis=0)
    sums[...] = jnp.broadcast_to(both[None], (devices, 2, 128))


def spread(top, corner, out):
    out[0, LOW], out[1, LOW] = split(top)
    out[0, TOP, TOP], out[1, TOP, TOP] = split(corner)
    for k in range(2):
        out[k, TOP, LOW] = out[k, LOW, TOP].T


def upper_product(a, b):
    top = dot3((a[0, LOW], a[1, LOW]), (b[0], b[1]))
    return top, dot3((a[0, TOP], a[1, TOP]), (b[0, :, TOP], b[1, :, TOP]))


def total(x):
    return jnp.sum(jnp.sum(x, axis=0, keepdims=True), axis=1, keepdims=True)


def load_gradient(core, half, other, g):
    mine = pl.ds(pl.multiple_of(core * HALF, HALF), HALF)
    theirs = pl.ds(pl.multiple_of(HALF - core * HALF, HALF), HALF)
    for rows, src in ((mine, half), (theirs, other)):
        g[0, rows], g[1, rows] = split(src[LOW])


def unpack_upper(packed):
    s00, s11 = unpack(packed[LOW, LOW], packed[HALF : HALF + 1, LOW])
    return jnp.concatenate([s00, packed[LOW, TOP]], axis=1), s11


def update_stat(half, other, old, facts, square_out, cube_out, out, g_out, g, s1, s2, sem):
    _, core = chip_core()
    load_gradient(core, half, other, g.at[0])
    copy = pltpu.make_async_copy(g.at[0], g_out, sem)
    copy.start()
    for k in range(2):
        g[1, k] = g[0, k].T
    top, corner = upper_product(g.at[1 - core], g.at[core])
    was_top, was_corner = unpack_upper(old)
    top = decay_rate * was_top + top
    corner = decay_rate * was_corner + corner
    s00, s01 = top[:, :HALF], top[:, HALF:]
    pack_into(out, s00, s01, corner)
    i, j = triangle()
    trace = total(jnp.where(i == j, s00 + corner, 0.0))
    norm_sq = total(s00 * s00 + corner * corner + 2.0 * (s01 * s01))
    inv = 1.0 / jnp.sqrt(norm_sq + epsilon)
    spread(top * inv, corner * inv, s1)
    top, corner = upper_product(s1, s1)
    pack_into(square_out, top[:, :HALF], top[:, HALF:], corner)
    spread(top, corner, s2)
    top, corner = upper_product(s1, s2)
    pack_into(cube_out, top[:, :HALF], top[:, HALF:], corner)
    facts[...] = jnp.concatenate([jnp.broadcast_to(x, (1, 128)) for x in (norm_sq, trace)], axis=0)
    copy.wait()


def coefficients(devices, facts, sums):
    both = jnp.sum(jnp.sum(sums[...], axis=0), axis=1, keepdims=True)
    grad_sq, trace_all = both[0:1], both[1:2]
    shift = (decay_rate * trace_all + 2.0 * grad_sq) * (damping / (devices * BLOCK))
    shift = jnp.broadcast_to(shift, (1, 128))
    norm_sq, trace = facts[0:1, :], facts[1:2, :]
    frob = jnp.sqrt(norm_sq + 2.0 * shift * trace + BLOCK * shift * shift + epsilon)
    a = jnp.sqrt(norm_sq + epsilon) / frob
    e = shift / frob

    def taken(poly, outer):
        out = []
        for i in range(len(poly)):
            value = jnp.full_like(e, poly[-1] * math.comb(len(poly) - 1, i))
            for j in range(len(poly) - 2, i - 1, -1):
                value = value * e + math.comb(j, i) * poly[j]
            out.append((outer * value)[:, 0:1])
            outer = outer * a
        return out

    outer = 1.0 / jnp.sqrt(jnp.sqrt(frob))
    return taken(SMALL_CUBIC, jnp.ones_like(e)), taken(ROOT_FACTOR, outer), taken(ROOT_REST, outer), grad_sq


def root(devices, stat, g_in, square, cubed, facts, sums, out, totals, g, left, right, sem):
    fetch = pltpu.make_async_copy(g_in, g, sem)
    fetch.start()
    small, factor, rest, grad_sq = coefficients(devices, facts, sums)
    inv = 1.0 / jnp.sqrt(facts[0:1, 0:1] + epsilon)
    i, j = triangle()
    on_diagonal = i == j

    def polynomial(k, powers, part):
        value = sum(k[n] * powers[n - 1][part] for n in range(1, len(k)))
        if part == 1:
            return value + jnp.where(on_diagonal, k[0], 0.0)
        return jnp.concatenate([value[:, :HALF] + jnp.where(on_diagonal, k[0], 0.0), value[:, HALF:]], axis=1)

    powers = [[x * inv for x in unpack_upper(stat)], unpack_upper(square), unpack_upper(cubed)]
    for dst, k in ((left, small), (right, factor)):
        dst[LOW] = polynomial(k, powers, 0).astype(bf16)
        dst[TOP, TOP] = polynomial(k, powers, 1).astype(bf16)
        dst[TOP, LOW] = dst[LOW, TOP].T
    out[LOW] = mm(left[LOW], right[...]) + polynomial(rest, powers, 0)
    corner = mm(left[TOP], right[:, TOP]) + polynomial(rest, powers, 1)
    out[HALF:, LOW] = corner[: HALF // 2]
    out[HALF:, TOP] = corner[HALF // 2 :]
    totals[...] = jnp.broadcast_to(grad_sq, (1, 128))
    fetch.wait()


def root_corner(packed):
    return jnp.concatenate([packed[HALF:, LOW], packed[HALF:, TOP]], axis=0)


def half_way(g, packed, out, x):
    _, core = chip_core()
    spread(packed[LOW], root_corner(packed), x)

    @pl.when(core == 1)
    def _():
        y = dot3((x[0, TOP], x[1, TOP]), (g[0], g[1]))
        out[0, LOW], out[1, LOW] = split(y)

    @pl.when(core == 0)
    def _():
        out[0], out[1] = split(dot3((g[0], g[1]), (x[0], x[1])))


def last_product(middle, packed, mine, most, rest, sums, x):
    _, core = chip_core()

    @pl.when(core == 1)
    def _():
        spread(packed[LOW], root_corner(packed), x)
        mine[...] = dot3((middle[0, LOW], middle[1, LOW]), (x[0], x[1]))

    @pl.when(core == 0)
    def _():
        mine[...] = dot3(split(packed[LOW]), (middle[0], middle[1]))

    most[...], rest[...] = mine[:MOST], mine[MOST:]
    sums[...] = jnp.broadcast_to(lanes(mine[...] * mine[...])[None], sums.shape)


def unpack_stat(packed, out):
    sa, sc = unpack(packed[LOW, LOW], packed[HALF : HALF + 1, LOW])
    off = packed[LOW, TOP]
    out[LOW, LOW] = sa
    out[LOW, TOP] = off
    out[TOP, LOW] = off.T
    out[TOP, TOP] = sc


def write_pieces(pieces, scale, out, scaled, sems):
    copies, base = [], 0
    for first, src in pieces:
        for r in range(0, src.shape[0], CHUNK):
            here = pl.ds(base + r, CHUNK)
            scaled[here] = src[pl.ds(r, CHUNK)] * scale
            start = pl.multiple_of(first + r, CHUNK)
            copies.append(pltpu.make_async_copy(scaled.at[here], out.at[pl.ds(start, CHUNK)], sems.at[len(copies)]))
            copies[-1].start()
        base += src.shape[0]
    for copy in copies:
        copy.wait()


def first_row(rows, n):
    return jnp.max(rows[n : n + 1, :]).astype(jnp.int32)


def place_first(plan, *refs):
    found, (sums, totals, rows, out, scale, scaled, sems) = refs[: len(plan)], refs[len(plan) :]
    prec_sq = jnp.sum(jnp.sum(sums[...], axis=0), axis=1, keepdims=True)
    factor = jnp.sqrt(totals[0:1, 0:1] / (prec_sq + epsilon))
    scale[...] = jnp.broadcast_to(factor, (1, 128))
    write_pieces([(first_row(rows, n) + r, x) for (n, r), x in zip(plan, found)], factor, out, scaled, sems)


def place_next(plan, *refs):
    found, (scale, rows, _, out, scaled, sems) = refs[: len(plan)], refs[len(plan) :]
    write_pieces(
        [(first_row(rows, n) + r, x) for (n, r), x in zip(plan, found)], scale[0:1, 0:1], out, scaled, sems
    )


def per_device(activations, out_grads, statistics, owner_blocks):
    rep_count = lax.axis_size("rep")
    pairs = rep_count // 2
    devices = rep_count * lax.axis_size("stripe")
    stripes = lax.axis_size("stripe")
    tokens = activations.shape[0]
    piece, square = (HALF, BLOCK), (BLOCK, BLOCK)
    unit = 6 * BLOCK**3

    whole = jax.ShapeDtypeStruct((2,) + square, bf16)
    split_square = pltpu.VMEM((2,) + square, bf16)
    m = pairs // 2

    def terms(*plan):
        return call(
            functools.partial(grad_terms, plan),
            [(len(chips),) + piece for chips, _ in plan],
            [HBM] * 3,
            [
                pltpu.VMEM(activations.shape, bf16),
                pltpu.VMEM(out_grads.shape, bf16),
                pltpu.SMEM(owner_blocks.shape, jnp.int32),
                pltpu.SemaphoreType.DMA((3,)),
            ],
            flops=2 * tokens * HALF * BLOCK * sum(len(chips) for chips, _ in plan),
        )(*(in_hbm(x) for x in (activations, out_grads, owner_blocks)))

    above, below = range(m, pairs), range(m)
    (send_far,) = terms((above, True))
    got_far = flip(send_far, 1)
    keep_far, send_near, keep_near = terms((above, False), (below, True), (below, False))
    got_near = flip(send_near, 1)
    arrived = [flip(keep_far[j] + got_far[j], 2 * m) for j in range(m)]
    while m > 1:
        m //= 2
        held = [keep_near[j] + got_near[j] + arrived[j] for j in range(m, 2 * m)]
        arrived = [x + flip(y, 2 * m) for x, y in zip(arrived, held)]
    shuffle = [(s * pairs + p, 2 * p + 1 - s) for s in range(2) for p in range(pairs)]
    packed, trace, rows = call(
        functools.partial(pack_stat, pairs), [(PACKED, BLOCK), (1, 128), (2 * pairs, 128)], [VMEM, SMEM]
    )(statistics[0, 0], owner_blocks)
    old = lax.ppermute(packed, "rep", shuffle)
    half, sums = call(
        functools.partial(finish_half, devices), [(PACKED, BLOCK), (devices, 2, 128)], [VMEM] * 4
    )(keep_near, got_near, arrived[0], trace)
    other = flip(half, 1)
    sums = lax.all_to_all(sums, AXES, 0, 0)
    facts, square_p, cube_p, out_packed, g_split = call(
        update_stat,
        [(2, 128)] + [(PACKED, BLOCK)] * 3 + [pltpu.HBM((2,) + square, bf16)],
        [VMEM] * 3,
        [pltpu.VMEM((2, 2) + square, bf16), split_square, split_square, pltpu.SemaphoreType.DMA],
        flops=3 * unit,
        out_specs=[VMEM] * 4 + [HBM],
        input_output_aliases={0: 3, 1: 2, 2: 1},
    )(half, other, old)
    new_packed = lax.ppermute(out_packed, "rep", [(t, s) for s, t in shuffle])
    mine_root, totals, g_split = call(
        functools.partial(root, devices),
        [(HALF + HALF // 2, BLOCK), (1, 128), whole],
        [VMEM, HBM] + [VMEM] * 4,
        [pltpu.VMEM(square, bf16)] * 2 + [pltpu.SemaphoreType.DMA],
        flops=unit,
    )(out_packed, in_hbm(g_split), square_p, cube_p, facts, sums)
    other_root = flip(mine_root, 1)
    (middle,) = call(half_way, [whole], [VMEM] * 2, [split_square], flops=unit)(g_split, mine_root)
    mine, most, rest, prec = call(last_product, [piece, (MOST, BLOCK), (HALF - MOST, BLOCK), (2 * stripes, 1, 128)], [VMEM] * 2, [split_square], flops=unit)(middle, other_root)

    bit = 2
    while bit < rep_count:
        prec = prec + flip(prec, bit)
        bit *= 2

    def spread_over_chips(x):
        found, bit = [x], 2
        while bit < rep_count:
            found = found + [flip(y, bit) for y in found]
            bit *= 2
        return found[1:]

    most = spread_over_chips(most)
    rest = spread_over_chips(rest)
    across = flip(mine, 1)
    near = [(s + stripes // 4) % stripes for s in range(stripes)]
    groups = [[(2 * q + c) * stripes + s for s in near for c in range(2)] for q in range(pairs)]
    prec = lax.all_to_all(prec, AXES, 0, 0, axis_index_groups=groups)
    (new_stat,) = call(unpack_stat, [square], [VMEM])(new_packed)
    slab = (pairs * BLOCK, out_grads.shape[1])

    def landing(found):
        count = sum(x.shape[0] for x in found)
        return [pltpu.VMEM((count, BLOCK), f32), pltpu.SemaphoreType.DMA((count // CHUNK,))]

    def place(placed, plan, *found):
        (placed,) = call(
            functools.partial(place_next, plan),
            [slab],
            [VMEM] * (len(plan) + 2) + [HBM],
            landing(found),
            out_specs=[HBM],
            input_output_aliases={len(plan) + 2: 0},
        )(*found, scale, rows, placed)
        return placed

    far = range(1, pairs)
    plan, found = [(0, 0), (pairs, 0)], (mine, across)
    placed, scale = call(
        functools.partial(place_first, plan), [slab, (1, 128)], [VMEM] * 5, landing(found), out_specs=[HBM, VMEM]
    )(*found, prec, totals, rows)
    most_across = [flip(x, 1) for x in most]
    rest_across = [flip(x, 1) for x in rest]
    plan = [(j, 0) for j in far] + [(pairs + j, 0) for j in far] + [(j, MOST) for j in far]
    placed = place(placed, plan, *most, *most_across, *rest)
    placed = place(placed, [(pairs + j, MOST) for j in far], *rest_across)
    return placed, new_stat[None, None]


def solution(mesh):
    in_specs = (
        P("rep", None),
        P("rep", "stripe"),
        P("rep", "stripe", None, None),
        P("stripe", None),
    )
    out_specs = (P(None, "stripe"), P("rep", "stripe", None, None))
    return jax.shard_map(per_device, mesh=mesh, in_specs=in_specs, out_specs=out_specs, check_vma=False)
```

```python
import functools
import math

import jax
import jax.numpy as jnp
from jax import lax
from jax.experimental import pallas as pl
from jax.experimental.pallas import tpu as pltpu
from jax.sharding import PartitionSpec as P


BLOCK = 512
HALF = BLOCK // 2
PACKED = HALF + 8
CHUNK = 64
MOST = HALF - 64

decay_rate = 0.95
damping = 0.25
epsilon = 1e-06
AXES = ("rep", "stripe")
f32 = jnp.float32
bf16 = jnp.bfloat16

ROOT_COEFFS = (
    25 / 16,
    -5 / 16 - 3125 / 4096,
    3125 / 4096,
    -1250 / 4096,
    250 / 4096,
    -25 / 4096,
    1 / 4096,
)
SMALL_CUBIC = (-1 / 32, 9 / 16, -3 / 2, 1.0)


def quotient(poly, divisor):
    rest, out = list(poly), []
    for i in range(len(poly) - len(divisor), -1, -1):
        out.insert(0, rest[i + len(divisor) - 1])
        for n, d in enumerate(divisor):
            rest[i + n] -= out[0] * d
    return out, rest[: len(divisor) - 1]


ROOT_FACTOR, ROOT_REST = quotient(ROOT_COEFFS, SMALL_CUBIC)

VMEM = pl.BlockSpec(memory_space=pltpu.VMEM)
SMEM = pl.BlockSpec(memory_space=pltpu.SMEM)
HBM = pl.BlockSpec(memory_space=pltpu.HBM)
LOW = pl.ds(0, HALF)
TOP = pl.ds(HALF, HALF)


def call(body, out_shapes, in_specs, scratch=(), limit=16, flops=0, out_specs=None, **kwargs):
    return pl.pallas_call(
        body,
        out_shape=[jax.ShapeDtypeStruct(s, f32) if isinstance(s, tuple) else s for s in out_shapes],
        in_specs=in_specs,
        out_specs=out_specs or [VMEM] * len(out_shapes),
        scratch_shapes=list(scratch),
        compiler_params=pltpu.CompilerParams(vmem_limit_bytes=limit << 20),
        cost_estimate=pl.CostEstimate(flops=flops, bytes_accessed=1 << 20, transcendentals=0),
        **kwargs,
    )


def flip(x, mask):
    return lax.ppermute(x, "rep", [(i, i ^ mask) for i in range(lax.axis_size("rep"))])


def in_hbm(x):
    return pltpu.with_memory_space_constraint(x, pltpu.HBM)


def chip_core():
    me = lax.axis_index("rep")
    return lax.shift_right_logical(me, 1), lax.bitwise_and(me, 1)


def split(x):
    hi = x.astype(bf16)
    return hi, (x - hi.astype(f32)).astype(bf16)


def mm(a, b):
    return jnp.dot(a, b, preferred_element_type=f32)


def dot3(a, b):
    return mm(a[0], b[0]) + (mm(a[0], b[1]) + mm(a[1], b[0]))


def triangle():
    i = lax.broadcasted_iota(jnp.int32, (HALF, HALF), 0)
    j = lax.broadcasted_iota(jnp.int32, (HALF, HALF), 1)
    return i, j


def lanes(x):
    rows = jnp.sum(x, axis=0, keepdims=True)
    return sum(rows[:, k : k + 128] for k in range(0, x.shape[1], 128))


def pack_into(out, a, b, c):
    i, j = triangle()
    out[LOW, LOW] = jnp.where(i <= j, a, c)
    out[LOW, TOP] = b
    out[HALF:, LOW] = jnp.broadcast_to(jnp.sum(jnp.where(i == j, c, 0.0), axis=0, keepdims=True), (8, HALF))


def unpack(u, diag):
    i, j = triangle()
    ut = u.T
    return jnp.where(i <= j, u, ut), jnp.where(i > j, u, jnp.where(i < j, ut, diag))


def pack_stat(pairs, stat, owners, out, trace, rows):
    chip, core = chip_core()
    for n in range(2 * pairs):
        half = core if n < pairs else 1 - core
        row = owners[0, lax.bitwise_xor(chip, jnp.int32(n % pairs))] * BLOCK + half * HALF
        rows[n : n + 1, :] = jnp.full((1, 128), row.astype(f32))
    i, j = triangle()
    a, c = stat[LOW, LOW], stat[TOP, TOP]
    pack_into(out, a, stat[LOW, TOP], c)
    trace[...] = lanes(jnp.where(i == j, a + c, 0.0))


def grad_terms(plan, acts, grads, owners, *refs):
    outs, (av, gv, ov, sems) = refs[: len(plan)], refs[len(plan) :]
    chip, core = chip_core()
    copies = [
        pltpu.make_async_copy(src, dst, sems.at[k]) for k, (src, dst) in enumerate(((owners, ov), (acts, av), (grads, gv)))
    ]
    for copy in copies:
        copy.start()
    for copy in copies:
        copy.wait()
    cotangent = gv[...]
    for out, (chips, swapped) in zip(outs, plan):
        half = 1 - core if swapped else core
        for n, j in enumerate(chips):
            start = ov[0, chip ^ j] * BLOCK + half * HALF
            cols = av[:, pl.ds(pl.multiple_of(start, HALF), HALF)]
            out[n] = lax.dot_general(cols, cotangent, (((0,), (0,)), ((), ())), preferred_element_type=f32)


def finish_half(devices, keep, got, rest, trace, half, sums):
    value = keep[0] + got[0] + rest[...]
    half[LOW] = value
    half[HALF:] = jnp.zeros((PACKED - HALF, BLOCK), f32)
    both = jnp.concatenate([lanes(value * value), trace[...]], axis=0)
    sums[...] = jnp.broadcast_to(both[None], (devices, 2, 128))


def spread(top, corner, out):
    out[0, LOW], out[1, LOW] = split(top)
    out[0, TOP, TOP], out[1, TOP, TOP] = split(corner)
    for k in range(2):
        out[k, TOP, LOW] = out[k, LOW, TOP].T


def upper_product(a, b):
    top = dot3((a[0, LOW], a[1, LOW]), (b[0], b[1]))
    return top, dot3((a[0, TOP], a[1, TOP]), (b[0, :, TOP], b[1, :, TOP]))


def total(x):
    return jnp.sum(jnp.sum(x, axis=0, keepdims=True), axis=1, keepdims=True)


def load_gradient(core, half, other, g):
    mine = pl.ds(pl.multiple_of(core * HALF, HALF), HALF)
    theirs = pl.ds(pl.multiple_of(HALF - core * HALF, HALF), HALF)
    for rows, src in ((mine, half), (theirs, other)):
        g[0, rows], g[1, rows] = split(src[LOW])


def unpack_upper(packed):
    s00, s11 = unpack(packed[LOW, LOW], packed[HALF : HALF + 1, LOW])
    return jnp.concatenate([s00, packed[LOW, TOP]], axis=1), s11


def update_stat(half, other, old, facts, square_out, cube_out, out, g_out, g, s1, s2, sem):
    _, core = chip_core()
    load_gradient(core, half, other, g.at[0])
    copy = pltpu.make_async_copy(g.at[0], g_out, sem)
    copy.start()
    for k in range(2):
        g[1, k] = g[0, k].T
    top, corner = upper_product(g.at[1 - core], g.at[core])
    was_top, was_corner = unpack_upper(old)
    top = decay_rate * was_top + top
    corner = decay_rate * was_corner + corner
    s00, s01 = top[:, :HALF], top[:, HALF:]
    pack_into(out, s00, s01, corner)
    i, j = triangle()
    trace = total(jnp.where(i == j, s00 + corner, 0.0))
    norm_sq = total(s00 * s00 + corner * corner + 2.0 * (s01 * s01))
    inv = 1.0 / jnp.sqrt(norm_sq + epsilon)
    spread(top * inv, corner * inv, s1)
    top, corner = upper_product(s1, s1)
    pack_into(square_out, top[:, :HALF], top[:, HALF:], corner)
    spread(top, corner, s2)
    top, corner = upper_product(s1, s2)
    pack_into(cube_out, top[:, :HALF], top[:, HALF:], corner)
    facts[...] = jnp.concatenate([jnp.broadcast_to(x, (1, 128)) for x in (norm_sq, trace)], axis=0)
    copy.wait()


def coefficients(devices, facts, sums):
    both = jnp.sum(jnp.sum(sums[...], axis=0), axis=1, keepdims=True)
    grad_sq, trace_all = both[0:1], both[1:2]
    shift = (decay_rate * trace_all + 2.0 * grad_sq) * (damping / (devices * BLOCK))
    shift = jnp.broadcast_to(shift, (1, 128))
    norm_sq, trace = facts[0:1, :], facts[1:2, :]
    frob = jnp.sqrt(norm_sq + 2.0 * shift * trace + BLOCK * shift * shift + epsilon)
    a = jnp.sqrt(norm_sq + epsilon) / frob
    e = shift / frob

    def taken(poly, outer):
        out = []
        for i in range(len(poly)):
            value = jnp.full_like(e, poly[-1] * math.comb(len(poly) - 1, i))
            for j in range(len(poly) - 2, i - 1, -1):
                value = value * e + math.comb(j, i) * poly[j]
            out.append((outer * value)[:, 0:1])
            outer = outer * a
        return out

    outer = 1.0 / jnp.sqrt(jnp.sqrt(frob))
    return taken(SMALL_CUBIC, jnp.ones_like(e)), taken(ROOT_FACTOR, outer), taken(ROOT_REST, outer), grad_sq


def root(devices, stat, g_in, square, cubed, facts, sums, out, totals, g, left, right, sem):
    fetch = pltpu.make_async_copy(g_in, g, sem)
    fetch.start()
    small, factor, rest, grad_sq = coefficients(devices, facts, sums)
    inv = 1.0 / jnp.sqrt(facts[0:1, 0:1] + epsilon)
    i, j = triangle()
    on_diagonal = i == j

    def polynomial(k, powers, part):
        value = sum(k[n] * powers[n - 1][part] for n in range(1, len(k)))
        if part == 1:
            return value + jnp.where(on_diagonal, k[0], 0.0)
        return jnp.concatenate([value[:, :HALF] + jnp.where(on_diagonal, k[0], 0.0), value[:, HALF:]], axis=1)

    powers = [[x * inv for x in unpack_upper(stat)], unpack_upper(square), unpack_upper(cubed)]
    for dst, k in ((left, small), (right, factor)):
        dst[LOW] = polynomial(k, powers, 0).astype(bf16)
        dst[TOP, TOP] = polynomial(k, powers, 1).astype(bf16)
        dst[TOP, LOW] = dst[LOW, TOP].T
    top = mm(left[LOW], right[...]) + polynomial(rest, powers, 0)
    corner = mm(left[TOP], right[:, TOP]) + polynomial(rest, powers, 1)
    pack_into(out, top[:, :HALF], top[:, HALF:], corner)
    totals[...] = jnp.broadcast_to(grad_sq, (1, 128))
    fetch.wait()


def half_way(g, packed, out, x):
    _, core = chip_core()
    spread(*unpack_upper(packed), x)

    @pl.when(core == 1)
    def _():
        y = dot3((x[0, TOP], x[1, TOP]), (g[0], g[1]))
        out[0, LOW], out[1, LOW] = split(y)

    @pl.when(core == 0)
    def _():
        out[0], out[1] = split(dot3((g[0], g[1]), (x[0], x[1])))


def last_product(middle, packed, mine, most, rest, sums, x):
    _, core = chip_core()

    @pl.when(core == 1)
    def _():
        spread(*unpack_upper(packed), x)
        mine[...] = dot3((middle[0, LOW], middle[1, LOW]), (x[0], x[1]))

    @pl.when(core == 0)
    def _():
        mine[...] = dot3(split(unpack_upper(packed)[0]), (middle[0], middle[1]))

    most[...], rest[...] = mine[:MOST], mine[MOST:]
    sums[...] = jnp.broadcast_to(lanes(mine[...] * mine[...])[None], sums.shape)


def unpack_stat(packed, out):
    sa, sc = unpack(packed[LOW, LOW], packed[HALF : HALF + 1, LOW])
    off = packed[LOW, TOP]
    out[LOW, LOW] = sa
    out[LOW, TOP] = off
    out[TOP, LOW] = off.T
    out[TOP, TOP] = sc


def write_pieces(pieces, scale, out, scaled, sems):
    copies, base = [], 0
    for first, src in pieces:
        for r in range(0, src.shape[0], CHUNK):
            here = pl.ds(base + r, CHUNK)
            scaled[here] = src[pl.ds(r, CHUNK)] * scale
            start = pl.multiple_of(first + r, CHUNK)
            copies.append(pltpu.make_async_copy(scaled.at[here], out.at[pl.ds(start, CHUNK)], sems.at[len(copies)]))
            copies[-1].start()
        base += src.shape[0]
    for copy in copies:
        copy.wait()


def first_row(rows, n):
    return jnp.max(rows[n : n + 1, :]).astype(jnp.int32)


def place_first(plan, *refs):
    found, (sums, totals, rows, out, scale, scaled, sems) = refs[: len(plan)], refs[len(plan) :]
    prec_sq = jnp.sum(jnp.sum(sums[...], axis=0), axis=1, keepdims=True)
    factor = jnp.sqrt(totals[0:1, 0:1] / (prec_sq + epsilon))
    scale[...] = jnp.broadcast_to(factor, (1, 128))
    write_pieces([(first_row(rows, n) + r, x) for (n, r), x in zip(plan, found)], factor, out, scaled, sems)


def place_next(plan, *refs):
    found, (scale, rows, _, out, scaled, sems) = refs[: len(plan)], refs[len(plan) :]
    write_pieces(
        [(first_row(rows, n) + r, x) for (n, r), x in zip(plan, found)], scale[0:1, 0:1], out, scaled, sems
    )


def per_device(activations, out_grads, statistics, owner_blocks):
    rep_count = lax.axis_size("rep")
    pairs = rep_count // 2
    devices = rep_count * lax.axis_size("stripe")
    stripes = lax.axis_size("stripe")
    tokens = activations.shape[0]
    piece, square = (HALF, BLOCK), (BLOCK, BLOCK)
    unit = 6 * BLOCK**3

    whole = jax.ShapeDtypeStruct((2,) + square, bf16)
    split_square = pltpu.VMEM((2,) + square, bf16)
    m = pairs // 2

    def terms(*plan):
        return call(
            functools.partial(grad_terms, plan),
            [(len(chips),) + piece for chips, _ in plan],
            [HBM] * 3,
            [
                pltpu.VMEM(activations.shape, bf16),
                pltpu.VMEM(out_grads.shape, bf16),
                pltpu.SMEM(owner_blocks.shape, jnp.int32),
                pltpu.SemaphoreType.DMA((3,)),
            ],
            flops=2 * tokens * HALF * BLOCK * sum(len(chips) for chips, _ in plan),
        )(*(in_hbm(x) for x in (activations, out_grads, owner_blocks)))

    above, below = range(m, pairs), range(m)
    (send_far,) = terms((above, True))
    got_far = flip(send_far, 1)
    keep_far, send_near, keep_near = terms((above, False), (below, True), (below, False))
    got_near = flip(send_near, 1)
    arrived = [flip(keep_far[j] + got_far[j], 2 * m) for j in range(m)]
    while m > 1:
        m //= 2
        held = [keep_near[j] + got_near[j] + arrived[j] for j in range(m, 2 * m)]
        arrived = [x + flip(y, 2 * m) for x, y in zip(arrived, held)]
    shuffle = [(s * pairs + p, 2 * p + 1 - s) for s in range(2) for p in range(pairs)]
    packed, trace, rows = call(
        functools.partial(pack_stat, pairs), [(PACKED, BLOCK), (1, 128), (2 * pairs, 128)], [VMEM, SMEM]
    )(statistics[0, 0], owner_blocks)
    old = lax.ppermute(packed, "rep", shuffle)
    half, sums = call(
        functools.partial(finish_half, devices), [(PACKED, BLOCK), (devices, 2, 128)], [VMEM] * 4
    )(keep_near, got_near, arrived[0], trace)
    other = flip(half, 1)
    sums = lax.all_to_all(sums, AXES, 0, 0)
    facts, square_p, cube_p, out_packed, g_split = call(
        update_stat,
        [(2, 128)] + [(PACKED, BLOCK)] * 3 + [pltpu.HBM((2,) + square, bf16)],
        [VMEM] * 3,
        [pltpu.VMEM((2, 2) + square, bf16), split_square, split_square, pltpu.SemaphoreType.DMA],
        flops=3 * unit,
        out_specs=[VMEM] * 4 + [HBM],
        input_output_aliases={0: 3, 1: 2, 2: 1},
    )(half, other, old)
    new_packed = lax.ppermute(out_packed, "rep", [(t, s) for s, t in shuffle])
    mine_root, totals, g_split = call(
        functools.partial(root, devices),
        [(PACKED, BLOCK), (1, 128), whole],
        [VMEM, HBM] + [VMEM] * 4,
        [pltpu.VMEM(square, bf16)] * 2 + [pltpu.SemaphoreType.DMA],
        flops=unit,
    )(out_packed, in_hbm(g_split), square_p, cube_p, facts, sums)
    other_root = flip(mine_root, 1)
    (middle,) = call(half_way, [whole], [VMEM] * 2, [split_square], flops=unit)(g_split, mine_root)
    mine, most, rest, prec = call(last_product, [piece, (MOST, BLOCK), (HALF - MOST, BLOCK), (2 * stripes, 1, 128)], [VMEM] * 2, [split_square], flops=unit)(middle, other_root)

    bit = 2
    while bit < rep_count:
        prec = prec + flip(prec, bit)
        bit *= 2

    def spread_over_chips(x):
        found, bit = [x], 2
        while bit < rep_count:
            found = found + [flip(y, bit) for y in found]
            bit *= 2
        return found[1:]

    most = spread_over_chips(most)
    rest = spread_over_chips(rest)
    across = flip(mine, 1)
    near = [(s + stripes // 4) % stripes for s in range(stripes)]
    groups = [[(2 * q + c) * stripes + s for s in near for c in range(2)] for q in range(pairs)]
    prec = lax.all_to_all(prec, AXES, 0, 0, axis_index_groups=groups)
    (new_stat,) = call(unpack_stat, [square], [VMEM])(new_packed)
    slab = (pairs * BLOCK, out_grads.shape[1])

    def landing(found):
        count = sum(x.shape[0] for x in found)
        return [pltpu.VMEM((count, BLOCK), f32), pltpu.SemaphoreType.DMA((count // CHUNK,))]

    def place(placed, plan, *found):
        (placed,) = call(
            functools.partial(place_next, plan),
            [slab],
            [VMEM] * (len(plan) + 2) + [HBM],
            landing(found),
            out_specs=[HBM],
            input_output_aliases={len(plan) + 2: 0},
        )(*found, scale, rows, placed)
        return placed

    far = range(1, pairs)
    plan, found = [(0, 0), (pairs, 0)], (mine, across)
    placed, scale = call(
        functools.partial(place_first, plan), [slab, (1, 128)], [VMEM] * 5, landing(found), out_specs=[HBM, VMEM]
    )(*found, prec, totals, rows)
    most_across = [flip(x, 1) for x in most]
    rest_across = [flip(x, 1) for x in rest]
    plan = [(j, 0) for j in far] + [(pairs + j, 0) for j in far] + [(j, MOST) for j in far]
    placed = place(placed, plan, *most, *most_across, *rest)
    placed = place(placed, [(pairs + j, MOST) for j in far], *rest_across)
    return placed, new_stat[None, None]


def solution(mesh):
    in_specs = (
        P("rep", None),
        P("rep", "stripe"),
        P("rep", "stripe", None, None),
        P("stripe", None),
    )
    out_specs = (P(None, "stripe"), P("rep", "stripe", None, None))
    return jax.shard_map(per_device, mesh=mesh, in_specs=in_specs, out_specs=out_specs, check_vma=False)
```

```python
import functools
import math

import jax
import jax.numpy as jnp
from jax import lax
from jax.experimental import pallas as pl
from jax.experimental.pallas import tpu as pltpu
from jax.sharding import PartitionSpec as P


BLOCK = 512
HALF = BLOCK // 2
PACKED = HALF + 8
CHUNK = 64
MOST = HALF - 64

decay_rate = 0.95
damping = 0.25
epsilon = 1e-06
AXES = ("rep", "stripe")
f32 = jnp.float32
bf16 = jnp.bfloat16

ROOT_COEFFS = (
    25 / 16,
    -5 / 16 - 3125 / 4096,
    3125 / 4096,
    -1250 / 4096,
    250 / 4096,
    -25 / 4096,
    1 / 4096,
)
SMALL_CUBIC = (-1 / 32, 9 / 16, -3 / 2, 1.0)


def quotient(poly, divisor):
    rest, out = list(poly), []
    for i in range(len(poly) - len(divisor), -1, -1):
        out.insert(0, rest[i + len(divisor) - 1])
        for n, d in enumerate(divisor):
            rest[i + n] -= out[0] * d
    return out, rest[: len(divisor) - 1]


ROOT_FACTOR, ROOT_REST = quotient(ROOT_COEFFS, SMALL_CUBIC)

VMEM = pl.BlockSpec(memory_space=pltpu.VMEM)
SMEM = pl.BlockSpec(memory_space=pltpu.SMEM)
HBM = pl.BlockSpec(memory_space=pltpu.HBM)
LOW = pl.ds(0, HALF)
TOP = pl.ds(HALF, HALF)


def call(body, out_shapes, in_specs, scratch=(), limit=16, flops=0, out_specs=None, **kwargs):
    return pl.pallas_call(
        body,
        out_shape=[jax.ShapeDtypeStruct(s, f32) if isinstance(s, tuple) else s for s in out_shapes],
        in_specs=in_specs,
        out_specs=out_specs or [VMEM] * len(out_shapes),
        scratch_shapes=list(scratch),
        compiler_params=pltpu.CompilerParams(vmem_limit_bytes=limit << 20),
        cost_estimate=pl.CostEstimate(flops=flops, bytes_accessed=1 << 20, transcendentals=0),
        **kwargs,
    )


def flip(x, mask):
    return lax.ppermute(x, "rep", [(i, i ^ mask) for i in range(lax.axis_size("rep"))])


def in_hbm(x):
    return pltpu.with_memory_space_constraint(x, pltpu.HBM)


def chip_core():
    me = lax.axis_index("rep")
    return lax.shift_right_logical(me, 1), lax.bitwise_and(me, 1)


def split(x):
    hi = x.astype(bf16)
    return hi, (x - hi.astype(f32)).astype(bf16)


def mm(a, b):
    return jnp.dot(a, b, preferred_element_type=f32)


def dot3(a, b):
    return mm(a[0], b[0]) + (mm(a[0], b[1]) + mm(a[1], b[0]))


def triangle():
    i = lax.broadcasted_iota(jnp.int32, (HALF, HALF), 0)
    j = lax.broadcasted_iota(jnp.int32, (HALF, HALF), 1)
    return i, j


def lanes(x):
    rows = jnp.sum(x, axis=0, keepdims=True)
    return sum(rows[:, k : k + 128] for k in range(0, x.shape[1], 128))


def pack_into(out, a, b, c):
    i, j = triangle()
    out[LOW, LOW] = jnp.where(i <= j, a, c)
    out[LOW, TOP] = b
    out[HALF:, LOW] = jnp.broadcast_to(jnp.sum(jnp.where(i == j, c, 0.0), axis=0, keepdims=True), (8, HALF))


def unpack(u, diag):
    i, j = triangle()
    ut = u.T
    return jnp.where(i <= j, u, ut), jnp.where(i > j, u, jnp.where(i < j, ut, diag))


def pack_stat(pairs, stat, owners, out, trace, rows):
    chip, core = chip_core()
    for n in range(2 * pairs):
        half = core if n < pairs else 1 - core
        row = owners[0, lax.bitwise_xor(chip, jnp.int32(n % pairs))] * BLOCK + half * HALF
        rows[n : n + 1, :] = jnp.full((1, 128), row.astype(f32))
    i, j = triangle()
    a, c = stat[LOW, LOW], stat[TOP, TOP]
    pack_into(out, a, stat[LOW, TOP], c)
    trace[...] = lanes(jnp.where(i == j, a + c, 0.0))


def grad_terms(plan, acts, grads, owners, *refs):
    outs, (av, gv, ov, sems) = refs[: len(plan)], refs[len(plan) :]
    chip, core = chip_core()
    copies = [
        pltpu.make_async_copy(src, dst, sems.at[k]) for k, (src, dst) in enumerate(((owners, ov), (acts, av), (grads, gv)))
    ]
    for copy in copies:
        copy.start()
    for copy in copies:
        copy.wait()
    cotangent = gv[...]
    for out, (chips, swapped, first, count) in zip(outs, plan):
        half = 1 - core if swapped else core
        for n, j in enumerate(chips):
            start = ov[0, chip ^ j] * BLOCK + half * HALF + first
            cols = av[:, pl.ds(pl.multiple_of(start, 128), count)]
            out[n] = lax.dot_general(cols, cotangent, (((0,), (0,)), ((), ())), preferred_element_type=f32)


def finish_half(devices, keep, got, rest_a, rest_b, trace, half, sums):
    value = keep[0] + got[0] + jnp.concatenate([rest_a[...], rest_b[...]], axis=0)
    half[LOW] = value
    half[HALF:] = jnp.zeros((PACKED - HALF, BLOCK), f32)
    both = jnp.concatenate([lanes(value * value), trace[...]], axis=0)
    sums[...] = jnp.broadcast_to(both[None], (devices, 2, 128))


def spread(top, corner, out):
    out[0, LOW], out[1, LOW] = split(top)
    out[0, TOP, TOP], out[1, TOP, TOP] = split(corner)
    for k in range(2):
        out[k, TOP, LOW] = out[k, LOW, TOP].T


def upper_product(a, b):
    top = dot3((a[0, LOW], a[1, LOW]), (b[0], b[1]))
    return top, dot3((a[0, TOP], a[1, TOP]), (b[0, :, TOP], b[1, :, TOP]))


def total(x):
    return jnp.sum(jnp.sum(x, axis=0, keepdims=True), axis=1, keepdims=True)


def load_gradient(core, half, other, g):
    mine = pl.ds(pl.multiple_of(core * HALF, HALF), HALF)
    theirs = pl.ds(pl.multiple_of(HALF - core * HALF, HALF), HALF)
    for rows, src in ((mine, half), (theirs, other)):
        g[0, rows], g[1, rows] = split(src[LOW])


def unpack_upper(packed):
    s00, s11 = unpack(packed[LOW, LOW], packed[HALF : HALF + 1, LOW])
    return jnp.concatenate([s00, packed[LOW, TOP]], axis=1), s11


def update_stat(half, other, old, facts, square_out, cube_out, out, g_out, g, s1, s2, sem):
    _, core = chip_core()
    load_gradient(core, half, other, g.at[0])
    copy = pltpu.make_async_copy(g.at[0], g_out, sem)
    copy.start()
    for k in range(2):
        g[1, k] = g[0, k].T
    top, corner = upper_product(g.at[1 - core], g.at[core])
    was_top, was_corner = unpack_upper(old)
    top = decay_rate * was_top + top
    corner = decay_rate * was_corner + corner
    s00, s01 = top[:, :HALF], top[:, HALF:]
    pack_into(out, s00, s01, corner)
    i, j = triangle()
    trace = total(jnp.where(i == j, s00 + corner, 0.0))
    norm_sq = total(s00 * s00 + corner * corner + 2.0 * (s01 * s01))
    inv = 1.0 / jnp.sqrt(norm_sq + epsilon)
    spread(top * inv, corner * inv, s1)
    top, corner = upper_product(s1, s1)
    pack_into(square_out, top[:, :HALF], top[:, HALF:], corner)
    spread(top, corner, s2)
    top, corner = upper_product(s1, s2)
    pack_into(cube_out, top[:, :HALF], top[:, HALF:], corner)
    facts[...] = jnp.concatenate([jnp.broadcast_to(x, (1, 128)) for x in (norm_sq, trace)], axis=0)
    copy.wait()


def coefficients(devices, facts, sums):
    both = jnp.sum(jnp.sum(sums[...], axis=0), axis=1, keepdims=True)
    grad_sq, trace_all = both[0:1], both[1:2]
    shift = (decay_rate * trace_all + 2.0 * grad_sq) * (damping / (devices * BLOCK))
    shift = jnp.broadcast_to(shift, (1, 128))
    norm_sq, trace = facts[0:1, :], facts[1:2, :]
    frob = jnp.sqrt(norm_sq + 2.0 * shift * trace + BLOCK * shift * shift + epsilon)
    a = jnp.sqrt(norm_sq + epsilon) / frob
    e = shift / frob

    def taken(poly, outer):
        out = []
        for i in range(len(poly)):
            value = jnp.full_like(e, poly[-1] * math.comb(len(poly) - 1, i))
            for j in range(len(poly) - 2, i - 1, -1):
                value = value * e + math.comb(j, i) * poly[j]
            out.append((outer * value)[:, 0:1])
            outer = outer * a
        return out

    outer = 1.0 / jnp.sqrt(jnp.sqrt(frob))
    return taken(SMALL_CUBIC, jnp.ones_like(e)), taken(ROOT_FACTOR, outer), taken(ROOT_REST, outer), grad_sq


def root(devices, stat, g_in, square, cubed, facts, sums, out, low, totals, g, left, right, sem):
    fetch = pltpu.make_async_copy(g_in, g, sem)
    fetch.start()
    small, factor, rest, grad_sq = coefficients(devices, facts, sums)
    inv = 1.0 / jnp.sqrt(facts[0:1, 0:1] + epsilon)
    i, j = triangle()
    on_diagonal = i == j

    def polynomial(k, powers, part):
        value = sum(k[n] * powers[n - 1][part] for n in range(1, len(k)))
        if part == 1:
            return value + jnp.where(on_diagonal, k[0], 0.0)
        return jnp.concatenate([value[:, :HALF] + jnp.where(on_diagonal, k[0], 0.0), value[:, HALF:]], axis=1)

    powers = [[x * inv for x in unpack_upper(stat)], unpack_upper(square), unpack_upper(cubed)]
    for dst, k in ((left, small), (right, factor)):
        dst[LOW] = polynomial(k, powers, 0).astype(bf16)
        dst[TOP, TOP] = polynomial(k, powers, 1).astype(bf16)
        dst[TOP, LOW] = dst[LOW, TOP].T
    out[...] = mm(left[LOW], right[...]) + polynomial(rest, powers, 0)
    low[...] = mm(left[TOP], right[:, TOP]) + polynomial(rest, powers, 1)
    totals[...] = jnp.broadcast_to(grad_sq, (1, 128))
    fetch.wait()


def half_way(g, upper, corner, out, x):
    _, core = chip_core()
    spread(upper[...], corner[...], x)

    @pl.when(core == 1)
    def _():
        y = dot3((x[0, TOP], x[1, TOP]), (g[0], g[1]))
        out[0, LOW], out[1, LOW] = split(y)

    @pl.when(core == 0)
    def _():
        out[0], out[1] = split(dot3((g[0], g[1]), (x[0], x[1])))


def last_product(middle, upper, corner, mine, most, rest, sums, x):
    _, core = chip_core()

    @pl.when(core == 1)
    def _():
        spread(upper[...], corner[...], x)
        mine[...] = dot3((middle[0, LOW], middle[1, LOW]), (x[0], x[1]))

    @pl.when(core == 0)
    def _():
        mine[...] = dot3(split(upper[...]), (middle[0], middle[1]))

    most[...], rest[...] = mine[:MOST], mine[MOST:]
    sums[...] = jnp.broadcast_to(lanes(mine[...] * mine[...])[None], sums.shape)


def unpack_stat(packed, out):
    sa, sc = unpack(packed[LOW, LOW], packed[HALF : HALF + 1, LOW])
    off = packed[LOW, TOP]
    out[LOW, LOW] = sa
    out[LOW, TOP] = off
    out[TOP, LOW] = off.T
    out[TOP, TOP] = sc


def write_pieces(pieces, scale, out, scaled, sems):
    copies, base = [], 0
    for first, src in pieces:
        for r in range(0, src.shape[0], CHUNK):
            here = pl.ds(base + r, CHUNK)
            scaled[here] = src[pl.ds(r, CHUNK)] * scale
            start = pl.multiple_of(first + r, CHUNK)
            copies.append(pltpu.make_async_copy(scaled.at[here], out.at[pl.ds(start, CHUNK)], sems.at[len(copies)]))
            copies[-1].start()
        base += src.shape[0]
    for copy in copies:
        copy.wait()


def first_row(rows, n):
    return jnp.max(rows[n : n + 1, :]).astype(jnp.int32)


def place_first(plan, *refs):
    found, (sums, totals, rows, out, scale, scaled, sems) = refs[: len(plan)], refs[len(plan) :]
    prec_sq = jnp.sum(jnp.sum(sums[...], axis=0), axis=1, keepdims=True)
    factor = jnp.sqrt(totals[0:1, 0:1] / (prec_sq + epsilon))
    scale[...] = jnp.broadcast_to(factor, (1, 128))
    write_pieces([(first_row(rows, n) + r, x) for (n, r), x in zip(plan, found)], factor, out, scaled, sems)


def place_next(plan, *refs):
    found, (scale, rows, _, out, scaled, sems) = refs[: len(plan)], refs[len(plan) :]
    write_pieces(
        [(first_row(rows, n) + r, x) for (n, r), x in zip(plan, found)], scale[0:1, 0:1], out, scaled, sems
    )


def per_device(activations, out_grads, statistics, owner_blocks):
    rep_count = lax.axis_size("rep")
    pairs = rep_count // 2
    devices = rep_count * lax.axis_size("stripe")
    stripes = lax.axis_size("stripe")
    tokens = activations.shape[0]
    piece, square = (HALF, BLOCK), (BLOCK, BLOCK)
    unit = 6 * BLOCK**3

    whole = jax.ShapeDtypeStruct((2,) + square, bf16)
    split_square = pltpu.VMEM((2,) + square, bf16)
    m = pairs // 2

    def terms(*plan):
        return call(
            functools.partial(grad_terms, plan),
            [(len(chips), count, BLOCK) for chips, _, _, count in plan],
            [HBM] * 3,
            [
                pltpu.VMEM(activations.shape, bf16),
                pltpu.VMEM(out_grads.shape, bf16),
                pltpu.SMEM(owner_blocks.shape, jnp.int32),
                pltpu.SemaphoreType.DMA((3,)),
            ],
            flops=2 * tokens * HALF * BLOCK * len(plan),
        )(*(in_hbm(x) for x in (activations, out_grads, owner_blocks)))

    above, below = range(m, pairs), range(m)
    quarter = HALF // 2
    send_a, send_b, keep_a, keep_b = terms(
        (above, True, 0, quarter), (above, True, quarter, quarter), (above, False, 0, quarter), (above, False, quarter, quarter)
    )
    got_a = flip(send_a, 1)
    got_b = flip(send_b, 1)
    arrived_a = [flip(keep_a[j] + got_a[j], 2 * m) for j in range(m)]
    arrived_b = [flip(keep_b[j] + got_b[j], 2 * m) for j in range(m)]
    send_near, keep_near = terms((below, True, 0, HALF), (below, False, 0, HALF))
    got_near = flip(send_near, 1)
    arrived = list(zip(arrived_a, arrived_b))
    while m > 1:
        m //= 2
        arrived = [jnp.concatenate(x) for x in arrived]
        held = [keep_near[j] + got_near[j] + arrived[j] for j in range(m, 2 * m)]
        arrived = [x + flip(y, 2 * m) for x, y in zip(arrived, held)]
        arrived = [(x[:quarter], x[quarter:]) for x in arrived]
    shuffle = [(s * pairs + p, 2 * p + 1 - s) for s in range(2) for p in range(pairs)]
    packed, trace, rows = call(
        functools.partial(pack_stat, pairs), [(PACKED, BLOCK), (1, 128), (2 * pairs, 128)], [VMEM, SMEM]
    )(statistics[0, 0], owner_blocks)
    old = lax.ppermute(packed, "rep", shuffle)
    half, sums = call(
        functools.partial(finish_half, devices), [(PACKED, BLOCK), (devices, 2, 128)], [VMEM] * 5
    )(keep_near, got_near, *arrived[0], trace)
    other = flip(half, 1)
    sums = lax.all_to_all(sums, AXES, 0, 0)
    facts, square_p, cube_p, out_packed, g_split = call(
        update_stat,
        [(2, 128)] + [(PACKED, BLOCK)] * 3 + [pltpu.HBM((2,) + square, bf16)],
        [VMEM] * 3,
        [pltpu.VMEM((2, 2) + square, bf16), split_square, split_square, pltpu.SemaphoreType.DMA],
        flops=3 * unit,
        out_specs=[VMEM] * 4 + [HBM],
        input_output_aliases={0: 3, 1: 2, 2: 1},
    )(half, other, old)
    new_packed = lax.ppermute(out_packed, "rep", [(t, s) for s, t in shuffle])
    upper, corner, totals, g_split = call(
        functools.partial(root, devices),
        [piece, (HALF, HALF), (1, 128), whole],
        [VMEM, HBM] + [VMEM] * 4,
        [pltpu.VMEM(square, bf16)] * 2 + [pltpu.SemaphoreType.DMA],
        flops=unit,
    )(out_packed, in_hbm(g_split), square_p, cube_p, facts, sums)
    other_upper = flip(upper, 1)
    other_corner = flip(corner, 1)
    (middle,) = call(half_way, [whole], [VMEM] * 3, [split_square], flops=unit)(g_split, upper, corner)
    mine, most, rest, prec = call(last_product, [piece, (MOST, BLOCK), (HALF - MOST, BLOCK), (2 * stripes, 1, 128)], [VMEM] * 3, [split_square], flops=unit)(middle, other_upper, other_corner)

    bit = 2
    while bit < rep_count:
        prec = prec + flip(prec, bit)
        bit *= 2

    def spread_over_chips(x):
        found, bit = [x], 2
        while bit < rep_count:
            found = found + [flip(y, bit) for y in found]
            bit *= 2
        return found[1:]

    most = spread_over_chips(most)
    rest = spread_over_chips(rest)
    across = flip(mine, 1)
    near = [(s + stripes // 4) % stripes for s in range(stripes)]
    groups = [[(2 * q + c) * stripes + s for s in near for c in range(2)] for q in range(pairs)]
    prec = lax.all_to_all(prec, AXES, 0, 0, axis_index_groups=groups)
    (new_stat,) = call(unpack_stat, [square], [VMEM])(new_packed)
    slab = (pairs * BLOCK, out_grads.shape[1])

    def landing(found):
        count = sum(x.shape[0] for x in found)
        return [pltpu.VMEM((count, BLOCK), f32), pltpu.SemaphoreType.DMA((count // CHUNK,))]

    def place(placed, plan, *found):
        (placed,) = call(
            functools.partial(place_next, plan),
            [slab],
            [VMEM] * (len(plan) + 2) + [HBM],
            landing(found),
            out_specs=[HBM],
            input_output_aliases={len(plan) + 2: 0},
        )(*found, scale, rows, placed)
        return placed

    far = range(1, pairs)
    plan, found = [(0, 0), (pairs, 0)], (mine, across)
    placed, scale = call(
        functools.partial(place_first, plan), [slab, (1, 128)], [VMEM] * 5, landing(found), out_specs=[HBM, VMEM]
    )(*found, prec, totals, rows)
    most_across = [flip(x, 1) for x in most]
    rest_across = [flip(x, 1) for x in rest]
    plan = [(j, 0) for j in far] + [(pairs + j, 0) for j in far] + [(j, MOST) for j in far]
    placed = place(placed, plan, *most, *most_across, *rest)
    placed = place(placed, [(pairs + j, MOST) for j in far], *rest_across)
    return placed, new_stat[None, None]


def solution(mesh):
    in_specs = (
        P("rep", None),
        P("rep", "stripe"),
        P("rep", "stripe", None, None),
        P("stripe", None),
    )
    out_specs = (P(None, "stripe"), P("rep", "stripe", None, None))
    return jax.shard_map(per_device, mesh=mesh, in_specs=in_specs, out_specs=out_specs, check_vma=False)
```

```python
import functools
import math

import jax
import jax.numpy as jnp
from jax import lax
from jax.experimental import pallas as pl
from jax.experimental.pallas import tpu as pltpu
from jax.sharding import PartitionSpec as P


BLOCK = 512
HALF = BLOCK // 2
PACKED = HALF + 8
CHUNK = 64
MOST = HALF - 64

decay_rate = 0.95
damping = 0.25
epsilon = 1e-06
AXES = ("rep", "stripe")
f32 = jnp.float32
bf16 = jnp.bfloat16

ROOT_COEFFS = (
    25 / 16,
    -5 / 16 - 3125 / 4096,
    3125 / 4096,
    -1250 / 4096,
    250 / 4096,
    -25 / 4096,
    1 / 4096,
)
SMALL_CUBIC = (-1 / 32, 9 / 16, -3 / 2, 1.0)


def quotient(poly, divisor):
    rest, out = list(poly), []
    for i in range(len(poly) - len(divisor), -1, -1):
        out.insert(0, rest[i + len(divisor) - 1])
        for n, d in enumerate(divisor):
            rest[i + n] -= out[0] * d
    return out, rest[: len(divisor) - 1]


ROOT_FACTOR, ROOT_REST = quotient(ROOT_COEFFS, SMALL_CUBIC)

VMEM = pl.BlockSpec(memory_space=pltpu.VMEM)
SMEM = pl.BlockSpec(memory_space=pltpu.SMEM)
HBM = pl.BlockSpec(memory_space=pltpu.HBM)
LOW = pl.ds(0, HALF)
TOP = pl.ds(HALF, HALF)


def call(body, out_shapes, in_specs, scratch=(), limit=16, flops=0, out_specs=None, **kwargs):
    return pl.pallas_call(
        body,
        out_shape=[jax.ShapeDtypeStruct(s, f32) if isinstance(s, tuple) else s for s in out_shapes],
        in_specs=in_specs,
        out_specs=out_specs or [VMEM] * len(out_shapes),
        scratch_shapes=list(scratch),
        compiler_params=pltpu.CompilerParams(vmem_limit_bytes=limit << 20),
        cost_estimate=pl.CostEstimate(flops=flops, bytes_accessed=1 << 20, transcendentals=0),
        **kwargs,
    )


def flip(x, mask):
    return lax.ppermute(x, "rep", [(i, i ^ mask) for i in range(lax.axis_size("rep"))])


def in_hbm(x):
    return pltpu.with_memory_space_constraint(x, pltpu.HBM)


def chip_core():
    me = lax.axis_index("rep")
    return lax.shift_right_logical(me, 1), lax.bitwise_and(me, 1)


def split(x):
    hi = x.astype(bf16)
    return hi, (x - hi.astype(f32)).astype(bf16)


def mm(a, b):
    return jnp.dot(a, b, preferred_element_type=f32)


def dot3(a, b):
    return mm(a[0], b[0]) + (mm(a[0], b[1]) + mm(a[1], b[0]))


def triangle():
    i = lax.broadcasted_iota(jnp.int32, (HALF, HALF), 0)
    j = lax.broadcasted_iota(jnp.int32, (HALF, HALF), 1)
    return i, j


def lanes(x):
    rows = jnp.sum(x, axis=0, keepdims=True)
    return sum(rows[:, k : k + 128] for k in range(0, x.shape[1], 128))


def pack_into(out, a, b, c):
    i, j = triangle()
    out[LOW, LOW] = jnp.where(i <= j, a, c)
    out[LOW, TOP] = b
    out[HALF:, LOW] = jnp.broadcast_to(jnp.sum(jnp.where(i == j, c, 0.0), axis=0, keepdims=True), (8, HALF))


def unpack(u, diag):
    i, j = triangle()
    ut = u.T
    return jnp.where(i <= j, u, ut), jnp.where(i > j, u, jnp.where(i < j, ut, diag))


def pack_stat(pairs, stat, owners, out, trace, rows):
    chip, core = chip_core()
    for n in range(2 * pairs):
        half = core if n < pairs else 1 - core
        row = owners[0, lax.bitwise_xor(chip, jnp.int32(n % pairs))] * BLOCK + half * HALF
        rows[n : n + 1, :] = jnp.full((1, 128), row.astype(f32))
    i, j = triangle()
    a, c = stat[LOW, LOW], stat[TOP, TOP]
    pack_into(out, a, stat[LOW, TOP], c)
    trace[...] = lanes(jnp.where(i == j, a + c, 0.0))


def grad_terms(plan, acts, grads, owners, *refs):
    outs, (av, gv, ov, sems) = refs[: len(plan)], refs[len(plan) :]
    chip, core = chip_core()
    copies = [
        pltpu.make_async_copy(src, dst, sems.at[k]) for k, (src, dst) in enumerate(((owners, ov), (acts, av), (grads, gv)))
    ]
    for copy in copies:
        copy.start()
    for copy in copies:
        copy.wait()
    cotangent = gv[...]
    for out, (chips, swapped, first, count) in zip(outs, plan):
        half = 1 - core if swapped else core
        for n, j in enumerate(chips):
            start = ov[0, chip ^ j] * BLOCK + half * HALF + first
            cols = av[:, pl.ds(pl.multiple_of(start, 128), count)]
            out[n] = lax.dot_general(cols, cotangent, (((0,), (0,)), ((), ())), preferred_element_type=f32)


def finish_half(devices, keep, got, rest_a, rest_b, trace, half, sums):
    value = keep[0] + got[0] + jnp.concatenate([rest_a[...], rest_b[...]], axis=0)
    half[LOW] = value
    half[HALF:] = jnp.zeros((PACKED - HALF, BLOCK), f32)
    both = jnp.concatenate([lanes(value * value), trace[...]], axis=0)
    sums[...] = jnp.broadcast_to(both[None], (devices, 2, 128))


def spread(top, corner, out):
    out[0, LOW], out[1, LOW] = split(top)
    out[0, TOP, TOP], out[1, TOP, TOP] = split(corner)
    for k in range(2):
        out[k, TOP, LOW] = out[k, LOW, TOP].T


def upper_product(a, b):
    top = dot3((a[0, LOW], a[1, LOW]), (b[0], b[1]))
    return top, dot3((a[0, TOP], a[1, TOP]), (b[0, :, TOP], b[1, :, TOP]))


def total(x):
    return jnp.sum(jnp.sum(x, axis=0, keepdims=True), axis=1, keepdims=True)


def load_gradient(core, half, other, g):
    mine = pl.ds(pl.multiple_of(core * HALF, HALF), HALF)
    theirs = pl.ds(pl.multiple_of(HALF - core * HALF, HALF), HALF)
    for rows, src in ((mine, half), (theirs, other)):
        g[0, rows], g[1, rows] = split(src[LOW])


def unpack_upper(packed):
    s00, s11 = unpack(packed[LOW, LOW], packed[HALF : HALF + 1, LOW])
    return jnp.concatenate([s00, packed[LOW, TOP]], axis=1), s11


def update_stat(half, other, old, facts, square_out, cube_out, out, g_out, g, s1, s2, sem):
    _, core = chip_core()
    load_gradient(core, half, other, g.at[0])
    copy = pltpu.make_async_copy(g.at[0], g_out, sem)
    copy.start()
    for k in range(2):
        g[1, k] = g[0, k].T
    top, corner = upper_product(g.at[1 - core], g.at[core])
    was_top, was_corner = unpack_upper(old)
    top = decay_rate * was_top + top
    corner = decay_rate * was_corner + corner
    s00, s01 = top[:, :HALF], top[:, HALF:]
    pack_into(out, s00, s01, corner)
    i, j = triangle()
    trace = total(jnp.where(i == j, s00 + corner, 0.0))
    norm_sq = total(s00 * s00 + corner * corner + 2.0 * (s01 * s01))
    inv = 1.0 / jnp.sqrt(norm_sq + epsilon)
    spread(top * inv, corner * inv, s1)
    top, corner = upper_product(s1, s1)
    pack_into(square_out, top[:, :HALF], top[:, HALF:], corner)
    spread(top, corner, s2)
    top, corner = upper_product(s1, s2)
    pack_into(cube_out, top[:, :HALF], top[:, HALF:], corner)
    facts[...] = jnp.concatenate([jnp.broadcast_to(x, (1, 128)) for x in (norm_sq, trace)], axis=0)
    copy.wait()


def coefficients(devices, facts, sums):
    both = jnp.sum(jnp.sum(sums[...], axis=0), axis=1, keepdims=True)
    grad_sq, trace_all = both[0:1], both[1:2]
    shift = (decay_rate * trace_all + 2.0 * grad_sq) * (damping / (devices * BLOCK))
    shift = jnp.broadcast_to(shift, (1, 128))
    norm_sq, trace = facts[0:1, :], facts[1:2, :]
    frob = jnp.sqrt(norm_sq + 2.0 * shift * trace + BLOCK * shift * shift + epsilon)
    a = jnp.sqrt(norm_sq + epsilon) / frob
    e = shift / frob

    def taken(poly, outer):
        out = []
        for i in range(len(poly)):
            value = jnp.full_like(e, poly[-1] * math.comb(len(poly) - 1, i))
            for j in range(len(poly) - 2, i - 1, -1):
                value = value * e + math.comb(j, i) * poly[j]
            out.append((outer * value)[:, 0:1])
            outer = outer * a
        return out

    outer = 1.0 / jnp.sqrt(jnp.sqrt(frob))
    return taken(SMALL_CUBIC, jnp.ones_like(e)), taken(ROOT_FACTOR, outer), taken(ROOT_REST, outer), grad_sq


def root(devices, stat, g_in, square, cubed, facts, sums, out, totals, g, left, right, sem):
    fetch = pltpu.make_async_copy(g_in, g, sem)
    fetch.start()
    small, factor, rest, grad_sq = coefficients(devices, facts, sums)
    inv = 1.0 / jnp.sqrt(facts[0:1, 0:1] + epsilon)
    i, j = triangle()
    on_diagonal = i == j

    def polynomial(k, powers, part):
        value = sum(k[n] * powers[n - 1][part] for n in range(1, len(k)))
        if part == 1:
            return value + jnp.where(on_diagonal, k[0], 0.0)
        return jnp.concatenate([value[:, :HALF] + jnp.where(on_diagonal, k[0], 0.0), value[:, HALF:]], axis=1)

    powers = [[x * inv for x in unpack_upper(stat)], unpack_upper(square), unpack_upper(cubed)]
    for dst, k in ((left, small), (right, factor)):
        dst[LOW] = polynomial(k, powers, 0).astype(bf16)
        dst[TOP, TOP] = polynomial(k, powers, 1).astype(bf16)
        dst[TOP, LOW] = dst[LOW, TOP].T
    out[LOW] = mm(left[LOW], right[...]) + polynomial(rest, powers, 0)
    corner = mm(left[TOP], right[:, TOP]) + polynomial(rest, powers, 1)
    out[HALF:, LOW] = corner[: HALF // 2]
    out[HALF:, TOP] = corner[HALF // 2 :]
    totals[...] = jnp.broadcast_to(grad_sq, (1, 128))
    fetch.wait()


def root_corner(packed):
    return jnp.concatenate([packed[HALF:, LOW], packed[HALF:, TOP]], axis=0)


def half_way(g, packed, out, x):
    _, core = chip_core()
    spread(packed[LOW], root_corner(packed), x)

    @pl.when(core == 1)
    def _():
        y = dot3((x[0, TOP], x[1, TOP]), (g[0], g[1]))
        out[0, LOW], out[1, LOW] = split(y)

    @pl.when(core == 0)
    def _():
        out[0], out[1] = split(dot3((g[0], g[1]), (x[0], x[1])))


def last_product(middle, packed, mine, most, rest, sums, x):
    _, core = chip_core()

    @pl.when(core == 1)
    def _():
        spread(packed[LOW], root_corner(packed), x)
        mine[...] = dot3((middle[0, LOW], middle[1, LOW]), (x[0], x[1]))

    @pl.when(core == 0)
    def _():
        mine[...] = dot3(split(packed[LOW]), (middle[0], middle[1]))

    most[...], rest[...] = mine[:MOST], mine[MOST:]
    sums[...] = jnp.broadcast_to(lanes(mine[...] * mine[...])[None], sums.shape)


def unpack_stat(packed, out):
    sa, sc = unpack(packed[LOW, LOW], packed[HALF : HALF + 1, LOW])
    off = packed[LOW, TOP]
    out[LOW, LOW] = sa
    out[LOW, TOP] = off
    out[TOP, LOW] = off.T
    out[TOP, TOP] = sc


def write_pieces(pieces, scale, out, scaled, sems):
    copies, base = [], 0
    for first, src in pieces:
        for r in range(0, src.shape[0], CHUNK):
            here = pl.ds(base + r, CHUNK)
            scaled[here] = src[pl.ds(r, CHUNK)] * scale
            start = pl.multiple_of(first + r, CHUNK)
            copies.append(pltpu.make_async_copy(scaled.at[here], out.at[pl.ds(start, CHUNK)], sems.at[len(copies)]))
            copies[-1].start()
        base += src.shape[0]
    for copy in copies:
        copy.wait()


def first_row(rows, n):
    return jnp.max(rows[n : n + 1, :]).astype(jnp.int32)


def place_first(plan, *refs):
    found, (sums, totals, rows, out, scale, scaled, sems) = refs[: len(plan)], refs[len(plan) :]
    prec_sq = jnp.sum(jnp.sum(sums[...], axis=0), axis=1, keepdims=True)
    factor = jnp.sqrt(totals[0:1, 0:1] / (prec_sq + epsilon))
    scale[...] = jnp.broadcast_to(factor, (1, 128))
    write_pieces([(first_row(rows, n) + r, x) for (n, r), x in zip(plan, found)], factor, out, scaled, sems)


def place_next(plan, *refs):
    found, (scale, rows, _, out, scaled, sems) = refs[: len(plan)], refs[len(plan) :]
    write_pieces(
        [(first_row(rows, n) + r, x) for (n, r), x in zip(plan, found)], scale[0:1, 0:1], out, scaled, sems
    )


def per_device(activations, out_grads, statistics, owner_blocks):
    rep_count = lax.axis_size("rep")
    pairs = rep_count // 2
    devices = rep_count * lax.axis_size("stripe")
    stripes = lax.axis_size("stripe")
    tokens = activations.shape[0]
    piece, square = (HALF, BLOCK), (BLOCK, BLOCK)
    unit = 6 * BLOCK**3

    whole = jax.ShapeDtypeStruct((2,) + square, bf16)
    split_square = pltpu.VMEM((2,) + square, bf16)
    m = pairs // 2

    def terms(*plan):
        return call(
            functools.partial(grad_terms, plan),
            [(len(chips), count, BLOCK) for chips, _, _, count in plan],
            [HBM] * 3,
            [
                pltpu.VMEM(activations.shape, bf16),
                pltpu.VMEM(out_grads.shape, bf16),
                pltpu.SMEM(owner_blocks.shape, jnp.int32),
                pltpu.SemaphoreType.DMA((3,)),
            ],
            flops=2 * tokens * HALF * BLOCK * len(plan),
        )(*(in_hbm(x) for x in (activations, out_grads, owner_blocks)))

    above, below = range(m, pairs), range(m)
    quarter = HALF // 2
    send_a, send_b, keep_a, keep_b = terms(
        (above, True, 0, quarter), (above, True, quarter, quarter), (above, False, 0, quarter), (above, False, quarter, quarter)
    )
    got_a = flip(send_a, 1)
    got_b = flip(send_b, 1)
    arrived_a = [flip(keep_a[j] + got_a[j], 2 * m) for j in range(m)]
    arrived_b = [flip(keep_b[j] + got_b[j], 2 * m) for j in range(m)]
    send_near, keep_near = terms((below, True, 0, HALF), (below, False, 0, HALF))
    got_near = flip(send_near, 1)
    arrived = list(zip(arrived_a, arrived_b))
    while m > 1:
        m //= 2
        arrived = [jnp.concatenate(x) for x in arrived]
        held = [keep_near[j] + got_near[j] + arrived[j] for j in range(m, 2 * m)]
        arrived = [x + flip(y, 2 * m) for x, y in zip(arrived, held)]
        arrived = [(x[:quarter], x[quarter:]) for x in arrived]
    shuffle = [(s * pairs + p, 2 * p + 1 - s) for s in range(2) for p in range(pairs)]
    packed, trace, rows = call(
        functools.partial(pack_stat, pairs), [(PACKED, BLOCK), (1, 128), (2 * pairs, 128)], [VMEM, SMEM]
    )(statistics[0, 0], owner_blocks)
    old = lax.ppermute(packed, "rep", shuffle)
    half, sums = call(
        functools.partial(finish_half, devices), [(PACKED, BLOCK), (devices, 2, 128)], [VMEM] * 5
    )(keep_near, got_near, *arrived[0], trace)
    other = flip(half, 1)
    sums = lax.all_to_all(sums, AXES, 0, 0)
    facts, square_p, cube_p, out_packed, g_split = call(
        update_stat,
        [(2, 128)] + [(PACKED, BLOCK)] * 3 + [pltpu.HBM((2,) + square, bf16)],
        [VMEM] * 3,
        [pltpu.VMEM((2, 2) + square, bf16), split_square, split_square, pltpu.SemaphoreType.DMA],
        flops=3 * unit,
        out_specs=[VMEM] * 4 + [HBM],
        input_output_aliases={0: 3, 1: 2, 2: 1},
    )(half, other, old)
    new_packed = lax.ppermute(out_packed, "rep", [(t, s) for s, t in shuffle])
    mine_root, totals, g_split = call(
        functools.partial(root, devices),
        [(HALF + HALF // 2, BLOCK), (1, 128), whole],
        [VMEM, HBM] + [VMEM] * 4,
        [pltpu.VMEM(square, bf16)] * 2 + [pltpu.SemaphoreType.DMA],
        flops=unit,
    )(out_packed, in_hbm(g_split), square_p, cube_p, facts, sums)
    other_root = flip(mine_root, 1)
    (middle,) = call(half_way, [whole], [VMEM] * 2, [split_square], flops=unit)(g_split, mine_root)
    mine, most, rest, prec = call(last_product, [piece, (MOST, BLOCK), (HALF - MOST, BLOCK), (2 * stripes, 1, 128)], [VMEM] * 2, [split_square], flops=unit)(middle, other_root)

    bit = 2
    while bit < rep_count:
        prec = prec + flip(prec, bit)
        bit *= 2

    def spread_over_chips(x):
        found, bit = [x], 2
        while bit < rep_count:
            found = found + [flip(y, bit) for y in found]
            bit *= 2
        return found[1:]

    most = spread_over_chips(most)
    rest = spread_over_chips(rest)
    across = flip(mine, 1)
    near = [(s + stripes // 4) % stripes for s in range(stripes)]
    groups = [[(2 * q + c) * stripes + s for s in near for c in range(2)] for q in range(pairs)]
    prec = lax.all_to_all(prec, AXES, 0, 0, axis_index_groups=groups)
    (new_stat,) = call(unpack_stat, [square], [VMEM])(new_packed)
    slab = (pairs * BLOCK, out_grads.shape[1])

    def landing(found):
        count = sum(x.shape[0] for x in found)
        return [pltpu.VMEM((count, BLOCK), f32), pltpu.SemaphoreType.DMA((count // CHUNK,))]

    def place(placed, plan, *found):
        (placed,) = call(
            functools.partial(place_next, plan),
            [slab],
            [VMEM] * (len(plan) + 2) + [HBM],
            landing(found),
            out_specs=[HBM],
            input_output_aliases={len(plan) + 2: 0},
        )(*found, scale, rows, placed)
        return placed

    far = range(1, pairs)
    plan, found = [(0, 0), (pairs, 0)], (mine, across)
    placed, scale = call(
        functools.partial(place_first, plan), [slab, (1, 128)], [VMEM] * 5, landing(found), out_specs=[HBM, VMEM]
    )(*found, prec, totals, rows)
    most_across = [flip(x, 1) for x in most]
    rest_across = [flip(x, 1) for x in rest]
    plan = [(j, 0) for j in far] + [(pairs + j, 0) for j in far] + [(j, MOST) for j in far]
    placed = place(placed, plan, *most, *most_across, *rest)
    placed = place(placed, [(pairs + j, MOST) for j in far], *rest_across)
    return placed, new_stat[None, None]


def solution(mesh):
    in_specs = (
        P("rep", None),
        P("rep", "stripe"),
        P("rep", "stripe", None, None),
        P("stripe", None),
    )
    out_specs = (P(None, "stripe"), P("rep", "stripe", None, None))
    return jax.shard_map(per_device, mesh=mesh, in_specs=in_specs, out_specs=out_specs, check_vma=False)
```

```python
import functools
import math

import jax
import jax.numpy as jnp
from jax import lax
from jax.experimental import pallas as pl
from jax.experimental.pallas import tpu as pltpu
from jax.sharding import PartitionSpec as P


BLOCK = 512
HALF = BLOCK // 2
PACKED = HALF + 8
CHUNK = 64
MOST = HALF - 64

decay_rate = 0.95
damping = 0.25
epsilon = 1e-06
AXES = ("rep", "stripe")
f32 = jnp.float32
bf16 = jnp.bfloat16

ROOT_COEFFS = (
    25 / 16,
    -5 / 16 - 3125 / 4096,
    3125 / 4096,
    -1250 / 4096,
    250 / 4096,
    -25 / 4096,
    1 / 4096,
)
SMALL_CUBIC = (-1 / 32, 9 / 16, -3 / 2, 1.0)


def quotient(poly, divisor):
    rest, out = list(poly), []
    for i in range(len(poly) - len(divisor), -1, -1):
        out.insert(0, rest[i + len(divisor) - 1])
        for n, d in enumerate(divisor):
            rest[i + n] -= out[0] * d
    return out, rest[: len(divisor) - 1]


ROOT_FACTOR, ROOT_REST = quotient(ROOT_COEFFS, SMALL_CUBIC)

VMEM = pl.BlockSpec(memory_space=pltpu.VMEM)
SMEM = pl.BlockSpec(memory_space=pltpu.SMEM)
HBM = pl.BlockSpec(memory_space=pltpu.HBM)
LOW = pl.ds(0, HALF)
TOP = pl.ds(HALF, HALF)


def call(body, out_shapes, in_specs, scratch=(), limit=16, flops=0, out_specs=None, **kwargs):
    return pl.pallas_call(
        body,
        out_shape=[jax.ShapeDtypeStruct(s, f32) if isinstance(s, tuple) else s for s in out_shapes],
        in_specs=in_specs,
        out_specs=out_specs or [VMEM] * len(out_shapes),
        scratch_shapes=list(scratch),
        compiler_params=pltpu.CompilerParams(vmem_limit_bytes=limit << 20),
        cost_estimate=pl.CostEstimate(flops=flops, bytes_accessed=1 << 20, transcendentals=0),
        **kwargs,
    )


def flip(x, mask):
    return lax.ppermute(x, "rep", [(i, i ^ mask) for i in range(lax.axis_size("rep"))])


def in_hbm(x):
    return pltpu.with_memory_space_constraint(x, pltpu.HBM)


def chip_core():
    me = lax.axis_index("rep")
    return lax.shift_right_logical(me, 1), lax.bitwise_and(me, 1)


def split(x):
    hi = x.astype(bf16)
    return hi, (x - hi.astype(f32)).astype(bf16)


def mm(a, b):
    return jnp.dot(a, b, preferred_element_type=f32)


def dot3(a, b):
    return mm(a[0], b[0]) + (mm(a[0], b[1]) + mm(a[1], b[0]))


def triangle():
    i = lax.broadcasted_iota(jnp.int32, (HALF, HALF), 0)
    j = lax.broadcasted_iota(jnp.int32, (HALF, HALF), 1)
    return i, j


def lanes(x):
    rows = jnp.sum(x, axis=0, keepdims=True)
    return sum(rows[:, k : k + 128] for k in range(0, x.shape[1], 128))


def pack_into(out, a, b, c):
    i, j = triangle()
    out[LOW, LOW] = jnp.where(i <= j, a, c)
    out[LOW, TOP] = b
    out[HALF:, LOW] = jnp.broadcast_to(jnp.sum(jnp.where(i == j, c, 0.0), axis=0, keepdims=True), (8, HALF))


def unpack(u, diag):
    i, j = triangle()
    ut = u.T
    return jnp.where(i <= j, u, ut), jnp.where(i > j, u, jnp.where(i < j, ut, diag))


def pack_stat(pairs, stat, owners, out, trace, rows):
    chip, core = chip_core()
    for n in range(2 * pairs):
        half = core if n < pairs else 1 - core
        row = owners[0, lax.bitwise_xor(chip, jnp.int32(n % pairs))] * BLOCK + half * HALF
        rows[n : n + 1, :] = jnp.full((1, 128), row.astype(f32))
    i, j = triangle()
    a, c = stat[LOW, LOW], stat[TOP, TOP]
    pack_into(out, a, stat[LOW, TOP], c)
    trace[...] = lanes(jnp.where(i == j, a + c, 0.0))


def grad_terms(plan, acts, grads, owners, *refs):
    outs, (av, gv, ov, sems) = refs[: len(plan)], refs[len(plan) :]
    chip, core = chip_core()
    copies = [
        pltpu.make_async_copy(src, dst, sems.at[k]) for k, (src, dst) in enumerate(((owners, ov), (acts, av), (grads, gv)))
    ]
    for copy in copies:
        copy.start()
    for copy in copies:
        copy.wait()
    cotangent = gv[...]
    for out, (chips, swapped, first, count) in zip(outs, plan):
        half = 1 - core if swapped else core
        for n, j in enumerate(chips):
            start = ov[0, chip ^ j] * BLOCK + half * HALF + first
            cols = av[:, pl.ds(pl.multiple_of(start, 128), count)]
            out[n] = lax.dot_general(cols, cotangent, (((0,), (0,)), ((), ())), preferred_element_type=f32)


def finish_half(devices, keep, got, rest_a, rest_b, trace, half, sums):
    value = keep[0] + got[0] + jnp.concatenate([rest_a[...], rest_b[...]], axis=0)
    half[LOW] = value
    half[HALF:] = jnp.zeros((PACKED - HALF, BLOCK), f32)
    both = jnp.concatenate([lanes(value * value), trace[...]], axis=0)
    sums[...] = jnp.broadcast_to(both[None], (devices, 2, 128))


def spread(top, corner, out):
    out[0, LOW], out[1, LOW] = split(top)
    out[0, TOP, TOP], out[1, TOP, TOP] = split(corner)
    for k in range(2):
        out[k, TOP, LOW] = out[k, LOW, TOP].T


def upper_product(a, b):
    top = dot3((a[0, LOW], a[1, LOW]), (b[0], b[1]))
    return top, dot3((a[0, TOP], a[1, TOP]), (b[0, :, TOP], b[1, :, TOP]))


def total(x):
    return jnp.sum(jnp.sum(x, axis=0, keepdims=True), axis=1, keepdims=True)


def load_gradient(core, half, other, g):
    mine = pl.ds(pl.multiple_of(core * HALF, HALF), HALF)
    theirs = pl.ds(pl.multiple_of(HALF - core * HALF, HALF), HALF)
    for rows, src in ((mine, half), (theirs, other)):
        g[0, rows], g[1, rows] = split(src[LOW])


def unpack_upper(packed):
    s00, s11 = unpack(packed[LOW, LOW], packed[HALF : HALF + 1, LOW])
    return jnp.concatenate([s00, packed[LOW, TOP]], axis=1), s11


def update_stat(half, other, old, facts, square_out, cube_out, out, g_out, g, s1, s2, sem):
    _, core = chip_core()
    load_gradient(core, half, other, g.at[0])
    copy = pltpu.make_async_copy(g.at[0], g_out, sem)
    copy.start()
    for k in range(2):
        g[1, k] = g[0, k].T
    top, corner = upper_product(g.at[1 - core], g.at[core])
    was_top, was_corner = unpack_upper(old)
    top = decay_rate * was_top + top
    corner = decay_rate * was_corner + corner
    s00, s01 = top[:, :HALF], top[:, HALF:]
    pack_into(out, s00, s01, corner)
    i, j = triangle()
    trace = total(jnp.where(i == j, s00 + corner, 0.0))
    norm_sq = total(s00 * s00 + corner * corner + 2.0 * (s01 * s01))
    inv = 1.0 / jnp.sqrt(norm_sq + epsilon)
    spread(top * inv, corner * inv, s1)
    top, corner = upper_product(s1, s1)
    pack_into(square_out, top[:, :HALF], top[:, HALF:], corner)
    spread(top, corner, s2)
    top, corner = upper_product(s1, s2)
    pack_into(cube_out, top[:, :HALF], top[:, HALF:], corner)
    facts[...] = jnp.concatenate([jnp.broadcast_to(x, (1, 128)) for x in (norm_sq, trace)], axis=0)
    copy.wait()


def coefficients(devices, facts, sums):
    both = jnp.sum(jnp.sum(sums[...], axis=0), axis=1, keepdims=True)
    grad_sq, trace_all = both[0:1], both[1:2]
    shift = (decay_rate * trace_all + 2.0 * grad_sq) * (damping / (devices * BLOCK))
    shift = jnp.broadcast_to(shift, (1, 128))
    norm_sq, trace = facts[0:1, :], facts[1:2, :]
    frob = jnp.sqrt(norm_sq + 2.0 * shift * trace + BLOCK * shift * shift + epsilon)
    a = jnp.sqrt(norm_sq + epsilon) / frob
    e = shift / frob

    def taken(poly, outer):
        out = []
        for i in range(len(poly)):
            value = jnp.full_like(e, poly[-1] * math.comb(len(poly) - 1, i))
            for j in range(len(poly) - 2, i - 1, -1):
                value = value * e + math.comb(j, i) * poly[j]
            out.append((outer * value)[:, 0:1])
            outer = outer * a
        return out

    outer = 1.0 / jnp.sqrt(jnp.sqrt(frob))
    return taken(SMALL_CUBIC, jnp.ones_like(e)), taken(ROOT_FACTOR, outer), taken(ROOT_REST, outer), grad_sq


def root(devices, stat, g_in, square, cubed, facts, sums, out, totals, g, left, right, sem):
    fetch = pltpu.make_async_copy(g_in, g, sem)
    fetch.start()
    small, factor, rest, grad_sq = coefficients(devices, facts, sums)
    inv = 1.0 / jnp.sqrt(facts[0:1, 0:1] + epsilon)
    i, j = triangle()
    on_diagonal = i == j

    def polynomial(k, powers, part):
        value = sum(k[n] * powers[n - 1][part] for n in range(1, len(k)))
        if part == 1:
            return value + jnp.where(on_diagonal, k[0], 0.0)
        return jnp.concatenate([value[:, :HALF] + jnp.where(on_diagonal, k[0], 0.0), value[:, HALF:]], axis=1)

    powers = [[x * inv for x in unpack_upper(stat)], unpack_upper(square), unpack_upper(cubed)]
    for dst, k in ((left, small), (right, factor)):
        dst[LOW] = polynomial(k, powers, 0).astype(bf16)
        dst[TOP, TOP] = polynomial(k, powers, 1).astype(bf16)
        dst[TOP, LOW] = dst[LOW, TOP].T
    out[LOW] = mm(left[LOW], right[...]) + polynomial(rest, powers, 0)
    corner = mm(left[TOP], right[:, TOP]) + polynomial(rest, powers, 1)
    out[HALF:, LOW] = corner[: HALF // 2]
    out[HALF:, TOP] = corner[HALF // 2 :]
    totals[...] = jnp.broadcast_to(grad_sq, (1, 128))
    fetch.wait()


def root_corner(packed):
    return jnp.concatenate([packed[HALF:, LOW], packed[HALF:, TOP]], axis=0)


def half_way(g, packed, out, x):
    _, core = chip_core()
    spread(packed[LOW], root_corner(packed), x)

    @pl.when(core == 1)
    def _():
        y = dot3((x[0, TOP], x[1, TOP]), (g[0], g[1]))
        out[0, LOW], out[1, LOW] = split(y)

    @pl.when(core == 0)
    def _():
        out[0], out[1] = split(dot3((g[0], g[1]), (x[0], x[1])))


def last_product(middle, packed, mine, most, rest, sums, x):
    _, core = chip_core()

    @pl.when(core == 1)
    def _():
        spread(packed[LOW], root_corner(packed), x)
        mine[...] = dot3((middle[0, LOW], middle[1, LOW]), (x[0], x[1]))

    @pl.when(core == 0)
    def _():
        mine[...] = dot3(split(packed[LOW]), (middle[0], middle[1]))

    most[...], rest[...] = mine[:MOST], mine[MOST:]
    sums[...] = jnp.broadcast_to(lanes(mine[...] * mine[...])[None], sums.shape)


def unpack_stat(packed, out):
    sa, sc = unpack(packed[LOW, LOW], packed[HALF : HALF + 1, LOW])
    off = packed[LOW, TOP]
    out[LOW, LOW] = sa
    out[LOW, TOP] = off
    out[TOP, LOW] = off.T
    out[TOP, TOP] = sc


def write_pieces(pieces, scale, out, scaled, sems):
    copies, base = [], 0
    for first, src in pieces:
        for r in range(0, src.shape[0], CHUNK):
            here = pl.ds(base + r, CHUNK)
            scaled[here] = src[pl.ds(r, CHUNK)] * scale
            start = pl.multiple_of(first + r, CHUNK)
            copies.append(pltpu.make_async_copy(scaled.at[here], out.at[pl.ds(start, CHUNK)], sems.at[len(copies)]))
            copies[-1].start()
        base += src.shape[0]
    for copy in copies:
        copy.wait()


def first_row(rows, n):
    return rows[n, 0].astype(jnp.int32)


def place_first(plan, *refs):
    found, (sums, totals, rows, out, scale, scaled, sems) = refs[: len(plan)], refs[len(plan) :]
    prec_sq = jnp.sum(jnp.sum(sums[...], axis=0), axis=1, keepdims=True)
    factor = jnp.sqrt(totals[0:1, 0:1] / (prec_sq + epsilon))
    scale[...] = jnp.broadcast_to(factor, (1, 128))
    write_pieces([(first_row(rows, n) + r, x) for (n, r), x in zip(plan, found)], factor, out, scaled, sems)


def place_next(plan, *refs):
    found, (scale, rows, _, out, scaled, sems) = refs[: len(plan)], refs[len(plan) :]
    write_pieces(
        [(first_row(rows, n) + r, x) for (n, r), x in zip(plan, found)], scale[0:1, 0:1], out, scaled, sems
    )


def per_device(activations, out_grads, statistics, owner_blocks):
    rep_count = lax.axis_size("rep")
    pairs = rep_count // 2
    devices = rep_count * lax.axis_size("stripe")
    stripes = lax.axis_size("stripe")
    tokens = activations.shape[0]
    piece, square = (HALF, BLOCK), (BLOCK, BLOCK)
    unit = 6 * BLOCK**3

    whole = jax.ShapeDtypeStruct((2,) + square, bf16)
    split_square = pltpu.VMEM((2,) + square, bf16)
    m = pairs // 2

    def terms(*plan):
        return call(
            functools.partial(grad_terms, plan),
            [(len(chips), count, BLOCK) for chips, _, _, count in plan],
            [HBM] * 3,
            [
                pltpu.VMEM(activations.shape, bf16),
                pltpu.VMEM(out_grads.shape, bf16),
                pltpu.SMEM(owner_blocks.shape, jnp.int32),
                pltpu.SemaphoreType.DMA((3,)),
            ],
            flops=2 * tokens * HALF * BLOCK * len(plan),
        )(*(in_hbm(x) for x in (activations, out_grads, owner_blocks)))

    above, below = range(m, pairs), range(m)
    quarter = HALF // 2
    send_a, send_b, keep_a, keep_b = terms(
        (above, True, 0, quarter), (above, True, quarter, quarter), (above, False, 0, quarter), (above, False, quarter, quarter)
    )
    got_a = flip(send_a, 1)
    got_b = flip(send_b, 1)
    arrived_a = [flip(keep_a[j] + got_a[j], 2 * m) for j in range(m)]
    arrived_b = [flip(keep_b[j] + got_b[j], 2 * m) for j in range(m)]
    send_near, keep_near = terms((below, True, 0, HALF), (below, False, 0, HALF))
    got_near = flip(send_near, 1)
    arrived = list(zip(arrived_a, arrived_b))
    while m > 1:
        m //= 2
        arrived = [jnp.concatenate(x) for x in arrived]
        held = [keep_near[j] + got_near[j] + arrived[j] for j in range(m, 2 * m)]
        arrived = [x + flip(y, 2 * m) for x, y in zip(arrived, held)]
        arrived = [(x[:quarter], x[quarter:]) for x in arrived]
    shuffle = [(s * pairs + p, 2 * p + 1 - s) for s in range(2) for p in range(pairs)]
    packed, trace, rows = call(
        functools.partial(pack_stat, pairs), [(PACKED, BLOCK), (1, 128), (2 * pairs, 128)], [VMEM, SMEM]
    )(statistics[0, 0], owner_blocks)
    old = lax.ppermute(packed, "rep", shuffle)
    half, sums = call(
        functools.partial(finish_half, devices), [(PACKED, BLOCK), (devices, 2, 128)], [VMEM] * 5
    )(keep_near, got_near, *arrived[0], trace)
    other = flip(half, 1)
    sums = lax.all_to_all(sums, AXES, 0, 0)
    facts, square_p, cube_p, out_packed, g_split = call(
        update_stat,
        [(2, 128)] + [(PACKED, BLOCK)] * 3 + [pltpu.HBM((2,) + square, bf16)],
        [VMEM] * 3,
        [pltpu.VMEM((2, 2) + square, bf16), split_square, split_square, pltpu.SemaphoreType.DMA],
        flops=3 * unit,
        out_specs=[VMEM] * 4 + [HBM],
        input_output_aliases={0: 3, 1: 2, 2: 1},
    )(half, other, old)
    new_packed = lax.ppermute(out_packed, "rep", [(t, s) for s, t in shuffle])
    mine_root, totals, g_split = call(
        functools.partial(root, devices),
        [(HALF + HALF // 2, BLOCK), (1, 128), whole],
        [VMEM, HBM] + [VMEM] * 4,
        [pltpu.VMEM(square, bf16)] * 2 + [pltpu.SemaphoreType.DMA],
        flops=unit,
    )(out_packed, in_hbm(g_split), square_p, cube_p, facts, sums)
    other_root = flip(mine_root, 1)
    (middle,) = call(half_way, [whole], [VMEM] * 2, [split_square], flops=unit)(g_split, mine_root)
    mine, most, rest, prec = call(last_product, [piece, (MOST, BLOCK), (HALF - MOST, BLOCK), (2 * stripes, 1, 128)], [VMEM] * 2, [split_square], flops=unit)(middle, other_root)

    bit = 2
    while bit < rep_count:
        prec = prec + flip(prec, bit)
        bit *= 2

    def spread_over_chips(x):
        found, bit = [x], 2
        while bit < rep_count:
            found = found + [flip(y, bit) for y in found]
            bit *= 2
        return found[1:]

    most = spread_over_chips(most)
    rest = spread_over_chips(rest)
    across = flip(mine, 1)
    groups = [[(2 * q + c) * stripes + s for s in range(stripes) for c in range(2)] for q in range(pairs)]
    prec = lax.all_to_all(prec, AXES, 0, 0, axis_index_groups=groups)
    (new_stat,) = call(unpack_stat, [square], [VMEM])(new_packed)
    slab = (pairs * BLOCK, out_grads.shape[1])

    def landing(found):
        count = sum(x.shape[0] for x in found)
        return [pltpu.VMEM((count, BLOCK), f32), pltpu.SemaphoreType.DMA((count // CHUNK,))]

    def place(placed, plan, *found):
        (placed,) = call(
            functools.partial(place_next, plan),
            [slab],
            [VMEM] * (len(plan) + 2) + [HBM],
            landing(found),
            out_specs=[HBM],
            input_output_aliases={len(plan) + 2: 0},
        )(*found, scale, rows, placed)
        return placed

    far = range(1, pairs)
    plan, found = [(0, 0), (pairs, 0)], (mine, across)
    placed, scale = call(
        functools.partial(place_first, plan), [slab, (1, 128)], [VMEM] * 5, landing(found), out_specs=[HBM, VMEM]
    )(*found, prec, totals, rows)
    most_across = [flip(x, 1) for x in most]
    rest_across = [flip(x, 1) for x in rest]
    plan = [(j, 0) for j in far] + [(pairs + j, 0) for j in far] + [(j, MOST) for j in far]
    placed = place(placed, plan, *most, *most_across, *rest)
    placed = place(placed, [(pairs + j, MOST) for j in far], *rest_across)
    return placed, new_stat[None, None]


def solution(mesh):
    in_specs = (
        P("rep", None),
        P("rep", "stripe"),
        P("rep", "stripe", None, None),
        P("stripe", None),
    )
    out_specs = (P(None, "stripe"), P("rep", "stripe", None, None))
    return jax.shard_map(per_device, mesh=mesh, in_specs=in_specs, out_specs=out_specs, check_vma=False)
```

```python
import functools
import math

import jax
import jax.numpy as jnp
from jax import lax
from jax.experimental import pallas as pl
from jax.experimental.pallas import tpu as pltpu
from jax.sharding import PartitionSpec as P


BLOCK = 512
HALF = BLOCK // 2
PACKED = HALF + 8
CHUNK = 64
MOST = HALF - 64

decay_rate = 0.95
damping = 0.25
epsilon = 1e-06
AXES = ("rep", "stripe")
f32 = jnp.float32
bf16 = jnp.bfloat16

ROOT_COEFFS = (
    25 / 16,
    -5 / 16 - 3125 / 4096,
    3125 / 4096,
    -1250 / 4096,
    250 / 4096,
    -25 / 4096,
    1 / 4096,
)
SMALL_CUBIC = (-1 / 32, 9 / 16, -3 / 2, 1.0)


def quotient(poly, divisor):
    rest, out = list(poly), []
    for i in range(len(poly) - len(divisor), -1, -1):
        out.insert(0, rest[i + len(divisor) - 1])
        for n, d in enumerate(divisor):
            rest[i + n] -= out[0] * d
    return out, rest[: len(divisor) - 1]


ROOT_FACTOR, ROOT_REST = quotient(ROOT_COEFFS, SMALL_CUBIC)

VMEM = pl.BlockSpec(memory_space=pltpu.VMEM)
SMEM = pl.BlockSpec(memory_space=pltpu.SMEM)
HBM = pl.BlockSpec(memory_space=pltpu.HBM)
LOW = pl.ds(0, HALF)
TOP = pl.ds(HALF, HALF)


def call(body, out_shapes, in_specs, scratch=(), limit=16, flops=0, out_specs=None, **kwargs):
    return pl.pallas_call(
        body,
        out_shape=[jax.ShapeDtypeStruct(s, f32) if isinstance(s, tuple) else s for s in out_shapes],
        in_specs=in_specs,
        out_specs=out_specs or [VMEM] * len(out_shapes),
        scratch_shapes=list(scratch),
        compiler_params=pltpu.CompilerParams(vmem_limit_bytes=limit << 20),
        cost_estimate=pl.CostEstimate(flops=flops, bytes_accessed=1 << 20, transcendentals=0),
        **kwargs,
    )


def flip(x, mask):
    return lax.ppermute(x, "rep", [(i, i ^ mask) for i in range(lax.axis_size("rep"))])


def in_hbm(x):
    return pltpu.with_memory_space_constraint(x, pltpu.HBM)


def chip_core():
    me = lax.axis_index("rep")
    return lax.shift_right_logical(me, 1), lax.bitwise_and(me, 1)


def split(x):
    hi = x.astype(bf16)
    return hi, (x - hi.astype(f32)).astype(bf16)


def mm(a, b):
    return jnp.dot(a, b, preferred_element_type=f32)


def dot3(a, b):
    return mm(a[0], b[0]) + (mm(a[0], b[1]) + mm(a[1], b[0]))


def triangle():
    i = lax.broadcasted_iota(jnp.int32, (HALF, HALF), 0)
    j = lax.broadcasted_iota(jnp.int32, (HALF, HALF), 1)
    return i, j


def lanes(x):
    rows = jnp.sum(x, axis=0, keepdims=True)
    return sum(rows[:, k : k + 128] for k in range(0, x.shape[1], 128))


def pack_into(out, a, b, c):
    i, j = triangle()
    out[LOW, LOW] = jnp.where(i <= j, a, c)
    out[LOW, TOP] = b
    out[HALF:, LOW] = jnp.broadcast_to(jnp.sum(jnp.where(i == j, c, 0.0), axis=0, keepdims=True), (8, HALF))


def unpack(u, diag):
    i, j = triangle()
    ut = u.T
    return jnp.where(i <= j, u, ut), jnp.where(i > j, u, jnp.where(i < j, ut, diag))


def pack_stat(pairs, stat, owners, out, trace, rows):
    chip, core = chip_core()
    for n in range(2 * pairs):
        half = core if n < pairs else 1 - core
        row = owners[0, lax.bitwise_xor(chip, jnp.int32(n % pairs))] * BLOCK + half * HALF
        rows[n : n + 1, :] = jnp.full((1, 128), row.astype(f32))
    i, j = triangle()
    a, c = stat[LOW, LOW], stat[TOP, TOP]
    pack_into(out, a, stat[LOW, TOP], c)
    trace[...] = lanes(jnp.where(i == j, a + c, 0.0))


def grad_terms(plan, acts, grads, owners, *refs):
    outs, (av, gv, ov, sems) = refs[: len(plan)], refs[len(plan) :]
    chip, core = chip_core()
    copies = [
        pltpu.make_async_copy(src, dst, sems.at[k]) for k, (src, dst) in enumerate(((owners, ov), (acts, av), (grads, gv)))
    ]
    for copy in copies:
        copy.start()
    for copy in copies:
        copy.wait()
    cotangent = gv[...]
    for out, (chips, swapped, first, count) in zip(outs, plan):
        half = 1 - core if swapped else core
        for n, j in enumerate(chips):
            start = ov[0, chip ^ j] * BLOCK + half * HALF + first
            cols = av[:, pl.ds(pl.multiple_of(start, 128), count)]
            out[n] = lax.dot_general(cols, cotangent, (((0,), (0,)), ((), ())), preferred_element_type=f32)


def finish_half(devices, keep, got, rest_a, rest_b, trace, half, sums):
    value = keep[0] + got[0] + jnp.concatenate([rest_a[...], rest_b[...]], axis=0)
    half[LOW] = value
    half[HALF:] = jnp.zeros((PACKED - HALF, BLOCK), f32)
    both = jnp.concatenate([lanes(value * value), trace[...]], axis=0)
    sums[...] = jnp.broadcast_to(both[None], (devices, 2, 128))


def spread(top, corner, out):
    out[0, LOW], out[1, LOW] = split(top)
    out[0, TOP, TOP], out[1, TOP, TOP] = split(corner)
    for k in range(2):
        out[k, TOP, LOW] = out[k, LOW, TOP].T


def upper_product(a, b):
    top = dot3((a[0, LOW], a[1, LOW]), (b[0], b[1]))
    return top, dot3((a[0, TOP], a[1, TOP]), (b[0, :, TOP], b[1, :, TOP]))


def total(x):
    return jnp.sum(jnp.sum(x, axis=0, keepdims=True), axis=1, keepdims=True)


def load_gradient(core, half, other, g):
    mine = pl.ds(pl.multiple_of(core * HALF, HALF), HALF)
    theirs = pl.ds(pl.multiple_of(HALF - core * HALF, HALF), HALF)
    for rows, src in ((mine, half), (theirs, other)):
        g[0, rows], g[1, rows] = split(src[LOW])


def unpack_upper(packed):
    s00, s11 = unpack(packed[LOW, LOW], packed[HALF : HALF + 1, LOW])
    return jnp.concatenate([s00, packed[LOW, TOP]], axis=1), s11


def update_stat(half, other, old, facts, square_out, cube_out, out, g_out, g, s1, s2, sem):
    _, core = chip_core()
    load_gradient(core, half, other, g.at[0])
    copy = pltpu.make_async_copy(g.at[0], g_out, sem)
    copy.start()
    for k in range(2):
        g[1, k] = g[0, k].T
    top, corner = upper_product(g.at[1 - core], g.at[core])
    was_top, was_corner = unpack_upper(old)
    top = decay_rate * was_top + top
    corner = decay_rate * was_corner + corner
    s00, s01 = top[:, :HALF], top[:, HALF:]
    pack_into(out, s00, s01, corner)
    i, j = triangle()
    trace = total(jnp.where(i == j, s00 + corner, 0.0))
    norm_sq = total(s00 * s00 + corner * corner + 2.0 * (s01 * s01))
    inv = 1.0 / jnp.sqrt(norm_sq + epsilon)
    spread(top * inv, corner * inv, s1)
    top, corner = upper_product(s1, s1)
    pack_into(square_out, top[:, :HALF], top[:, HALF:], corner)
    spread(top, corner, s2)
    top, corner = upper_product(s1, s2)
    pack_into(cube_out, top[:, :HALF], top[:, HALF:], corner)
    facts[...] = jnp.concatenate([jnp.broadcast_to(x, (1, 128)) for x in (norm_sq, trace)], axis=0)
    copy.wait()


def coefficients(devices, facts, sums):
    both = jnp.sum(jnp.sum(sums[...], axis=0), axis=1, keepdims=True)
    grad_sq, trace_all = both[0:1], both[1:2]
    shift = (decay_rate * trace_all + 2.0 * grad_sq) * (damping / (devices * BLOCK))
    shift = jnp.broadcast_to(shift, (1, 128))
    norm_sq, trace = facts[0:1, :], facts[1:2, :]
    frob = jnp.sqrt(norm_sq + 2.0 * shift * trace + BLOCK * shift * shift + epsilon)
    a = jnp.sqrt(norm_sq + epsilon) / frob
    e = shift / frob

    def taken(poly, outer):
        out = []
        for i in range(len(poly)):
            value = jnp.full_like(e, poly[-1] * math.comb(len(poly) - 1, i))
            for j in range(len(poly) - 2, i - 1, -1):
                value = value * e + math.comb(j, i) * poly[j]
            out.append((outer * value)[:, 0:1])
            outer = outer * a
        return out

    outer = 1.0 / jnp.sqrt(jnp.sqrt(frob))
    return taken(SMALL_CUBIC, jnp.ones_like(e)), taken(ROOT_FACTOR, outer), taken(ROOT_REST, outer), grad_sq


def root(devices, stat, g_in, square, cubed, facts, sums, out, totals, g, left, right, sem):
    fetch = pltpu.make_async_copy(g_in, g, sem)
    fetch.start()
    small, factor, rest, grad_sq = coefficients(devices, facts, sums)
    inv = 1.0 / jnp.sqrt(facts[0:1, 0:1] + epsilon)
    i, j = triangle()
    on_diagonal = i == j

    def polynomial(k, powers, part):
        value = sum(k[n] * powers[n - 1][part] for n in range(1, len(k)))
        if part == 1:
            return value + jnp.where(on_diagonal, k[0], 0.0)
        return jnp.concatenate([value[:, :HALF] + jnp.where(on_diagonal, k[0], 0.0), value[:, HALF:]], axis=1)

    powers = [[x * inv for x in unpack_upper(stat)], unpack_upper(square), unpack_upper(cubed)]
    for dst, k in ((left, small), (right, factor)):
        dst[LOW] = polynomial(k, powers, 0).astype(bf16)
        dst[TOP, TOP] = polynomial(k, powers, 1).astype(bf16)
        dst[TOP, LOW] = dst[LOW, TOP].T
    out[LOW] = mm(left[LOW], right[...]) + polynomial(rest, powers, 0)
    corner = mm(left[TOP], right[:, TOP]) + polynomial(rest, powers, 1)
    out[HALF:, LOW] = corner[: HALF // 2]
    out[HALF:, TOP] = corner[HALF // 2 :]
    totals[...] = jnp.broadcast_to(grad_sq, (1, 128))
    fetch.wait()


def root_corner(packed):
    return jnp.concatenate([packed[HALF:, LOW], packed[HALF:, TOP]], axis=0)


def half_way(g, packed, out, x):
    _, core = chip_core()
    spread(packed[LOW], root_corner(packed), x)

    @pl.when(core == 1)
    def _():
        y = dot3((x[0, TOP], x[1, TOP]), (g[0], g[1]))
        out[0, LOW], out[1, LOW] = split(y)

    @pl.when(core == 0)
    def _():
        out[0], out[1] = split(dot3((g[0], g[1]), (x[0], x[1])))


def last_product(middle, packed, mine, most, rest, sums, x):
    _, core = chip_core()

    @pl.when(core == 1)
    def _():
        spread(packed[LOW], root_corner(packed), x)
        mine[...] = dot3((middle[0, LOW], middle[1, LOW]), (x[0], x[1]))

    @pl.when(core == 0)
    def _():
        mine[...] = dot3(split(packed[LOW]), (middle[0], middle[1]))

    most[...], rest[...] = mine[:MOST], mine[MOST:]
    sums[...] = jnp.broadcast_to(lanes(mine[...] * mine[...])[None], sums.shape)


def unpack_stat(packed, out):
    sa, sc = unpack(packed[LOW, LOW], packed[HALF : HALF + 1, LOW])
    off = packed[LOW, TOP]
    out[LOW, LOW] = sa
    out[LOW, TOP] = off
    out[TOP, LOW] = off.T
    out[TOP, TOP] = sc


def write_pieces(pieces, scale, out, scaled, sems):
    copies, base = [], 0
    for first, src in pieces:
        for r in range(0, src.shape[0], CHUNK):
            here = pl.ds(base + r, CHUNK)
            scaled[here] = src[pl.ds(r, CHUNK)] * scale
            start = pl.multiple_of(first + r, CHUNK)
            copies.append(pltpu.make_async_copy(scaled.at[here], out.at[pl.ds(start, CHUNK)], sems.at[len(copies)]))
            copies[-1].start()
        base += src.shape[0]
    for copy in copies:
        copy.wait()


def first_row(rows, n):
    return rows[n, 0].astype(jnp.int32)


def place_first(plan, *refs):
    found, (sums, totals, rows, out, scale, scaled, sems) = refs[: len(plan)], refs[len(plan) :]
    prec_sq = jnp.sum(jnp.sum(sums[...], axis=0), axis=1, keepdims=True)
    factor = jnp.sqrt(totals[0:1, 0:1] / (prec_sq + epsilon))
    scale[...] = jnp.broadcast_to(factor, (1, 128))
    write_pieces([(first_row(rows, n) + r, x) for (n, r), x in zip(plan, found)], factor, out, scaled, sems)


def place_next(plan, *refs):
    found, (scale, rows, _, out, scaled, sems) = refs[: len(plan)], refs[len(plan) :]
    write_pieces(
        [(first_row(rows, n) + r, x) for (n, r), x in zip(plan, found)], scale[0:1, 0:1], out, scaled, sems
    )


def per_device(activations, out_grads, statistics, owner_blocks):
    rep_count = lax.axis_size("rep")
    pairs = rep_count // 2
    devices = rep_count * lax.axis_size("stripe")
    stripes = lax.axis_size("stripe")
    tokens = activations.shape[0]
    piece, square = (HALF, BLOCK), (BLOCK, BLOCK)
    unit = 6 * BLOCK**3

    whole = jax.ShapeDtypeStruct((2,) + square, bf16)
    split_square = pltpu.VMEM((2,) + square, bf16)
    m = pairs // 2

    def terms(*plan):
        return call(
            functools.partial(grad_terms, plan),
            [(len(chips), count, BLOCK) for chips, _, _, count in plan],
            [HBM] * 3,
            [
                pltpu.VMEM(activations.shape, bf16),
                pltpu.VMEM(out_grads.shape, bf16),
                pltpu.SMEM(owner_blocks.shape, jnp.int32),
                pltpu.SemaphoreType.DMA((3,)),
            ],
            flops=2 * tokens * HALF * BLOCK * len(plan),
        )(*(in_hbm(x) for x in (activations, out_grads, owner_blocks)))

    above, below = range(m, pairs), range(m)
    quarter = HALF // 2
    send_a, send_b, keep_a, keep_b = terms(
        (above, True, 0, quarter), (above, True, quarter, quarter), (above, False, 0, quarter), (above, False, quarter, quarter)
    )
    got_a = flip(send_a, 1)
    got_b = flip(send_b, 1)
    arrived_a = [flip(keep_a[j] + got_a[j], 2 * m) for j in range(m)]
    arrived_b = [flip(keep_b[j] + got_b[j], 2 * m) for j in range(m)]
    send_near, keep_near = terms((below, True, 0, HALF), (below, False, 0, HALF))
    got_near = flip(send_near, 1)
    arrived = list(zip(arrived_a, arrived_b))
    while m > 1:
        m //= 2
        arrived = [jnp.concatenate(x) for x in arrived]
        held = [keep_near[j] + got_near[j] + arrived[j] for j in range(m, 2 * m)]
        arrived = [x + flip(y, 2 * m) for x, y in zip(arrived, held)]
        arrived = [(x[:quarter], x[quarter:]) for x in arrived]
    shuffle = [(s * pairs + p, 2 * p + 1 - s) for s in range(2) for p in range(pairs)]
    packed, trace, rows = call(
        functools.partial(pack_stat, pairs), [(PACKED, BLOCK), (1, 128), (2 * pairs, 128)], [VMEM, SMEM]
    )(statistics[0, 0], owner_blocks)
    old = lax.ppermute(packed, "rep", shuffle)
    half, sums = call(
        functools.partial(finish_half, devices), [(PACKED, BLOCK), (devices, 2, 128)], [VMEM] * 5
    )(keep_near, got_near, *arrived[0], trace)
    other = flip(half, 1)
    sums = lax.all_to_all(sums, AXES, 0, 0)
    facts, square_p, cube_p, out_packed, g_split = call(
        update_stat,
        [(2, 128)] + [(PACKED, BLOCK)] * 3 + [pltpu.HBM((2,) + square, bf16)],
        [VMEM] * 3,
        [pltpu.VMEM((2, 2) + square, bf16), split_square, split_square, pltpu.SemaphoreType.DMA],
        flops=3 * unit,
        out_specs=[VMEM] * 4 + [HBM],
        input_output_aliases={0: 3, 1: 2, 2: 1},
    )(half, other, old)
    new_packed = lax.ppermute(out_packed, "rep", [(t, s) for s, t in shuffle])
    mine_root, totals, g_split = call(
        functools.partial(root, devices),
        [(HALF + HALF // 2, BLOCK), (1, 128), whole],
        [VMEM, HBM] + [VMEM] * 4,
        [pltpu.VMEM(square, bf16)] * 2 + [pltpu.SemaphoreType.DMA],
        flops=unit,
    )(out_packed, in_hbm(g_split), square_p, cube_p, facts, sums)
    other_root = flip(mine_root, 1)
    (middle,) = call(half_way, [whole], [VMEM] * 2, [split_square], flops=unit)(g_split, mine_root)
    mine, most, rest, prec = call(last_product, [piece, (MOST, BLOCK), (HALF - MOST, BLOCK), (2 * stripes, 1, 128)], [VMEM] * 2, [split_square], flops=unit)(middle, other_root)

    bit = 2
    while bit < rep_count:
        prec = prec + flip(prec, bit)
        bit *= 2

    def spread_over_chips(x):
        found, bit = [x], 2
        while bit < rep_count:
            found = found + [flip(y, bit) for y in found]
            bit *= 2
        return found[1:]

    most = spread_over_chips(most)
    rest = spread_over_chips(rest)
    across = flip(mine, 1)
    near = [(s + stripes // 4) % stripes for s in range(stripes)]
    groups = [[(2 * q + c) * stripes + s for s in near for c in range(2)] for q in range(pairs)]
    prec = lax.all_to_all(prec, AXES, 0, 0, axis_index_groups=groups)
    (new_stat,) = call(unpack_stat, [square], [VMEM])(new_packed)
    slab = (pairs * BLOCK, out_grads.shape[1])

    def landing(found):
        count = sum(x.shape[0] for x in found)
        return [pltpu.VMEM((count, BLOCK), f32), pltpu.SemaphoreType.DMA((count // CHUNK,))]

    def place(placed, plan, *found):
        (placed,) = call(
            functools.partial(place_next, plan),
            [slab],
            [VMEM] * (len(plan) + 2) + [HBM],
            landing(found),
            out_specs=[HBM],
            input_output_aliases={len(plan) + 2: 0},
        )(*found, scale, rows, placed)
        return placed

    far = range(1, pairs)
    plan, found = [(0, 0)], (mine,)
    placed, scale = call(
        functools.partial(place_first, plan), [slab, (1, 128)], [VMEM] * 4, landing(found), out_specs=[HBM, VMEM]
    )(*found, prec, totals, rows)
    most_across = [flip(x, 1) for x in most]
    rest_across = [flip(x, 1) for x in rest]
    plan = [(pairs, 0)] + [(j, 0) for j in far] + [(pairs + j, 0) for j in far] + [(j, MOST) for j in far]
    placed = place(placed, plan, across, *most, *most_across, *rest)
    placed = place(placed, [(pairs + j, MOST) for j in far], *rest_across)
    return placed, new_stat[None, None]


def solution(mesh):
    in_specs = (
        P("rep", None),
        P("rep", "stripe"),
        P("rep", "stripe", None, None),
        P("stripe", None),
    )
    out_specs = (P(None, "stripe"), P("rep", "stripe", None, None))
    return jax.shard_map(per_device, mesh=mesh, in_specs=in_specs, out_specs=out_specs, check_vma=False)
```

```python
import functools
import math

import jax
import jax.numpy as jnp
from jax import lax
from jax.experimental import pallas as pl
from jax.experimental.pallas import tpu as pltpu
from jax.sharding import PartitionSpec as P


BLOCK = 512
HALF = BLOCK // 2
PACKED = HALF + 8
MOST = HALF - 64

decay_rate = 0.95
damping = 0.25
epsilon = 1e-06
AXES = ("rep", "stripe")
f32 = jnp.float32
bf16 = jnp.bfloat16

ROOT_COEFFS = (
    25 / 16,
    -5 / 16 - 3125 / 4096,
    3125 / 4096,
    -1250 / 4096,
    250 / 4096,
    -25 / 4096,
    1 / 4096,
)
SMALL_CUBIC = (-1 / 32, 9 / 16, -3 / 2, 1.0)


def quotient(poly, divisor):
    rest, out = list(poly), []
    for i in range(len(poly) - len(divisor), -1, -1):
        out.insert(0, rest[i + len(divisor) - 1])
        for n, d in enumerate(divisor):
            rest[i + n] -= out[0] * d
    return out, rest[: len(divisor) - 1]


ROOT_FACTOR, ROOT_REST = quotient(ROOT_COEFFS, SMALL_CUBIC)

VMEM = pl.BlockSpec(memory_space=pltpu.VMEM)
SMEM = pl.BlockSpec(memory_space=pltpu.SMEM)
HBM = pl.BlockSpec(memory_space=pltpu.HBM)
LOW = pl.ds(0, HALF)
TOP = pl.ds(HALF, HALF)


def call(body, out_shapes, in_specs, scratch=(), limit=16, flops=0, out_specs=None, **kwargs):
    return pl.pallas_call(
        body,
        out_shape=[jax.ShapeDtypeStruct(s, f32) if isinstance(s, tuple) else s for s in out_shapes],
        in_specs=in_specs,
        out_specs=out_specs or [VMEM] * len(out_shapes),
        scratch_shapes=list(scratch),
        compiler_params=pltpu.CompilerParams(vmem_limit_bytes=limit << 20),
        cost_estimate=pl.CostEstimate(flops=flops, bytes_accessed=1 << 20, transcendentals=0),
        **kwargs,
    )


def flip(x, mask):
    return lax.ppermute(x, "rep", [(i, i ^ mask) for i in range(lax.axis_size("rep"))])


def in_hbm(x):
    return pltpu.with_memory_space_constraint(x, pltpu.HBM)


def chip_core():
    me = lax.axis_index("rep")
    return lax.shift_right_logical(me, 1), lax.bitwise_and(me, 1)


def split(x):
    hi = x.astype(bf16)
    return hi, (x - hi.astype(f32)).astype(bf16)


def mm(a, b):
    return jnp.dot(a, b, preferred_element_type=f32)


def dot3(a, b):
    return mm(a[0], b[0]) + (mm(a[0], b[1]) + mm(a[1], b[0]))


def triangle():
    i = lax.broadcasted_iota(jnp.int32, (HALF, HALF), 0)
    j = lax.broadcasted_iota(jnp.int32, (HALF, HALF), 1)
    return i, j


def lanes(x):
    rows = jnp.sum(x, axis=0, keepdims=True)
    return sum(rows[:, k : k + 128] for k in range(0, x.shape[1], 128))


def pack_into(out, a, b, c):
    i, j = triangle()
    out[LOW, LOW] = jnp.where(i <= j, a, c)
    out[LOW, TOP] = b
    out[HALF:, LOW] = jnp.broadcast_to(jnp.sum(jnp.where(i == j, c, 0.0), axis=0, keepdims=True), (8, HALF))


def unpack(u, diag):
    i, j = triangle()
    ut = u.T
    return jnp.where(i <= j, u, ut), jnp.where(i > j, u, jnp.where(i < j, ut, diag))


def pack_stat(pairs, stat, owners, out, trace, rows):
    chip, core = chip_core()
    for n in range(2 * pairs):
        half = core if n < pairs else 1 - core
        row = owners[0, lax.bitwise_xor(chip, jnp.int32(n % pairs))] * BLOCK + half * HALF
        rows[n : n + 1, :] = jnp.full((1, 128), row.astype(f32))
    i, j = triangle()
    a, c = stat[LOW, LOW], stat[TOP, TOP]
    pack_into(out, a, stat[LOW, TOP], c)
    trace[...] = lanes(jnp.where(i == j, a + c, 0.0))


def grad_terms(plan, acts, grads, owners, *refs):
    outs, (av, gv, ov, sems) = refs[: len(plan)], refs[len(plan) :]
    chip, core = chip_core()
    copies = [
        pltpu.make_async_copy(src, dst, sems.at[k]) for k, (src, dst) in enumerate(((owners, ov), (acts, av), (grads, gv)))
    ]
    for copy in copies:
        copy.start()
    for copy in copies:
        copy.wait()
    cotangent = gv[...]
    for out, (chips, swapped, first, count) in zip(outs, plan):
        half = 1 - core if swapped else core
        for n, j in enumerate(chips):
            start = ov[0, chip ^ j] * BLOCK + half * HALF + first
            cols = av[:, pl.ds(pl.multiple_of(start, 128), count)]
            out[n] = lax.dot_general(cols, cotangent, (((0,), (0,)), ((), ())), preferred_element_type=f32)


def finish_half(devices, keep, got, rest_a, rest_b, trace, half, sums):
    value = keep[0] + got[0] + jnp.concatenate([rest_a[...], rest_b[...]], axis=0)
    half[LOW] = value
    half[HALF:] = jnp.zeros((PACKED - HALF, BLOCK), f32)
    both = jnp.concatenate([lanes(value * value), trace[...]], axis=0)
    sums[...] = jnp.broadcast_to(both[None], (devices, 2, 128))


def spread(top, corner, out):
    out[0, LOW], out[1, LOW] = split(top)
    out[0, TOP, TOP], out[1, TOP, TOP] = split(corner)
    for k in range(2):
        out[k, TOP, LOW] = out[k, LOW, TOP].T


def upper_product(a, b):
    top = dot3((a[0, LOW], a[1, LOW]), (b[0], b[1]))
    return top, dot3((a[0, TOP], a[1, TOP]), (b[0, :, TOP], b[1, :, TOP]))


def total(x):
    return jnp.sum(jnp.sum(x, axis=0, keepdims=True), axis=1, keepdims=True)


def load_gradient(core, half, other, g):
    mine = pl.ds(pl.multiple_of(core * HALF, HALF), HALF)
    theirs = pl.ds(pl.multiple_of(HALF - core * HALF, HALF), HALF)
    for rows, src in ((mine, half), (theirs, other)):
        g[0, rows], g[1, rows] = split(src[LOW])


def unpack_upper(packed):
    s00, s11 = unpack(packed[LOW, LOW], packed[HALF : HALF + 1, LOW])
    return jnp.concatenate([s00, packed[LOW, TOP]], axis=1), s11


def update_stat(half, other, old, facts, square_out, cube_out, out, g_out, g, s1, s2, sem):
    _, core = chip_core()
    load_gradient(core, half, other, g.at[0])
    copy = pltpu.make_async_copy(g.at[0], g_out, sem)
    copy.start()
    for k in range(2):
        g[1, k] = g[0, k].T
    top, corner = upper_product(g.at[1 - core], g.at[core])
    was_top, was_corner = unpack_upper(old)
    top = decay_rate * was_top + top
    corner = decay_rate * was_corner + corner
    s00, s01 = top[:, :HALF], top[:, HALF:]
    pack_into(out, s00, s01, corner)
    i, j = triangle()
    trace = total(jnp.where(i == j, s00 + corner, 0.0))
    norm_sq = total(s00 * s00 + corner * corner + 2.0 * (s01 * s01))
    inv = 1.0 / jnp.sqrt(norm_sq + epsilon)
    spread(top * inv, corner * inv, s1)
    top, corner = upper_product(s1, s1)
    pack_into(square_out, top[:, :HALF], top[:, HALF:], corner)
    spread(top, corner, s2)
    top, corner = upper_product(s1, s2)
    pack_into(cube_out, top[:, :HALF], top[:, HALF:], corner)
    facts[...] = jnp.concatenate([jnp.broadcast_to(x, (1, 128)) for x in (norm_sq, trace)], axis=0)
    copy.wait()


def coefficients(devices, facts, sums):
    both = jnp.sum(jnp.sum(sums[...], axis=0), axis=1, keepdims=True)
    grad_sq, trace_all = both[0:1], both[1:2]
    shift = (decay_rate * trace_all + 2.0 * grad_sq) * (damping / (devices * BLOCK))
    shift = jnp.broadcast_to(shift, (1, 128))
    norm_sq, trace = facts[0:1, :], facts[1:2, :]
    frob = jnp.sqrt(norm_sq + 2.0 * shift * trace + BLOCK * shift * shift + epsilon)
    a = jnp.sqrt(norm_sq + epsilon) / frob
    e = shift / frob

    def taken(poly, outer):
        out = []
        for i in range(len(poly)):
            value = jnp.full_like(e, poly[-1] * math.comb(len(poly) - 1, i))
            for j in range(len(poly) - 2, i - 1, -1):
                value = value * e + math.comb(j, i) * poly[j]
            out.append((outer * value)[:, 0:1])
            outer = outer * a
        return out

    outer = 1.0 / jnp.sqrt(jnp.sqrt(frob))
    return taken(SMALL_CUBIC, jnp.ones_like(e)), taken(ROOT_FACTOR, outer), taken(ROOT_REST, outer), grad_sq


def root(devices, stat, g_in, square, cubed, facts, sums, out, totals, g, left, right, sem):
    fetch = pltpu.make_async_copy(g_in, g, sem)
    fetch.start()
    small, factor, rest, grad_sq = coefficients(devices, facts, sums)
    inv = 1.0 / jnp.sqrt(facts[0:1, 0:1] + epsilon)
    i, j = triangle()
    on_diagonal = i == j

    def polynomial(k, powers, part):
        value = sum(k[n] * powers[n - 1][part] for n in range(1, len(k)))
        if part == 1:
            return value + jnp.where(on_diagonal, k[0], 0.0)
        return jnp.concatenate([value[:, :HALF] + jnp.where(on_diagonal, k[0], 0.0), value[:, HALF:]], axis=1)

    powers = [[x * inv for x in unpack_upper(stat)], unpack_upper(square), unpack_upper(cubed)]
    for dst, k in ((left, small), (right, factor)):
        dst[LOW] = polynomial(k, powers, 0).astype(bf16)
        dst[TOP, TOP] = polynomial(k, powers, 1).astype(bf16)
        dst[TOP, LOW] = dst[LOW, TOP].T
    out[LOW] = mm(left[LOW], right[...]) + polynomial(rest, powers, 0)
    corner = mm(left[TOP], right[:, TOP]) + polynomial(rest, powers, 1)
    out[HALF:, LOW] = corner[: HALF // 2]
    out[HALF:, TOP] = corner[HALF // 2 :]
    totals[...] = jnp.broadcast_to(grad_sq, (1, 128))
    fetch.wait()


def root_corner(packed):
    return jnp.concatenate([packed[HALF:, LOW], packed[HALF:, TOP]], axis=0)


def half_way(g, packed, out, x):
    _, core = chip_core()
    spread(packed[LOW], root_corner(packed), x)

    @pl.when(core == 1)
    def _():
        y = dot3((x[0, TOP], x[1, TOP]), (g[0], g[1]))
        out[0, LOW], out[1, LOW] = split(y)

    @pl.when(core == 0)
    def _():
        out[0], out[1] = split(dot3((g[0], g[1]), (x[0], x[1])))


def last_product(middle, packed, mine, most, rest, sums, x):
    _, core = chip_core()

    @pl.when(core == 1)
    def _():
        spread(packed[LOW], root_corner(packed), x)
        mine[...] = dot3((middle[0, LOW], middle[1, LOW]), (x[0], x[1]))

    @pl.when(core == 0)
    def _():
        mine[...] = dot3(split(packed[LOW]), (middle[0], middle[1]))

    most[...], rest[...] = mine[:MOST], mine[MOST:]
    sums[...] = jnp.broadcast_to(lanes(mine[...] * mine[...])[None], sums.shape)


def unpack_stat(packed, out):
    sa, sc = unpack(packed[LOW, LOW], packed[HALF : HALF + 1, LOW])
    off = packed[LOW, TOP]
    out[LOW, LOW] = sa
    out[LOW, TOP] = off
    out[TOP, LOW] = off.T
    out[TOP, TOP] = sc


def write_pieces(pieces, scale, out, scaled, sems):
    copies, base = [], 0
    for first, src in pieces:
        here = pl.ds(base, src.shape[0])
        scaled[here] = src[...] * scale
        start = pl.multiple_of(first, 64)
        copies.append(pltpu.make_async_copy(scaled.at[here], out.at[pl.ds(start, src.shape[0])], sems.at[len(copies)]))
        copies[-1].start()
        base += src.shape[0]
    for copy in copies:
        copy.wait()


def first_row(rows, n):
    return rows[n, 0].astype(jnp.int32)


def place_first(plan, *refs):
    found, (sums, totals, rows, out, scale, scaled, sems) = refs[: len(plan)], refs[len(plan) :]
    prec_sq = jnp.sum(jnp.sum(sums[...], axis=0), axis=1, keepdims=True)
    factor = jnp.sqrt(totals[0:1, 0:1] / (prec_sq + epsilon))
    scale[...] = jnp.broadcast_to(factor, (1, 128))
    write_pieces([(first_row(rows, n) + r, x) for (n, r), x in zip(plan, found)], factor, out, scaled, sems)


def place_next(plan, *refs):
    found, (scale, rows, _, out, scaled, sems) = refs[: len(plan)], refs[len(plan) :]
    write_pieces(
        [(first_row(rows, n) + r, x) for (n, r), x in zip(plan, found)], scale[0:1, 0:1], out, scaled, sems
    )


def per_device(activations, out_grads, statistics, owner_blocks):
    rep_count = lax.axis_size("rep")
    pairs = rep_count // 2
    devices = rep_count * lax.axis_size("stripe")
    stripes = lax.axis_size("stripe")
    tokens = activations.shape[0]
    piece, square = (HALF, BLOCK), (BLOCK, BLOCK)
    unit = 6 * BLOCK**3

    whole = jax.ShapeDtypeStruct((2,) + square, bf16)
    split_square = pltpu.VMEM((2,) + square, bf16)
    m = pairs // 2

    def terms(*plan):
        return call(
            functools.partial(grad_terms, plan),
            [(len(chips), count, BLOCK) for chips, _, _, count in plan],
            [HBM] * 3,
            [
                pltpu.VMEM(activations.shape, bf16),
                pltpu.VMEM(out_grads.shape, bf16),
                pltpu.SMEM(owner_blocks.shape, jnp.int32),
                pltpu.SemaphoreType.DMA((3,)),
            ],
            flops=2 * tokens * HALF * BLOCK * len(plan),
        )(*(in_hbm(x) for x in (activations, out_grads, owner_blocks)))

    above, below = range(m, pairs), range(m)
    quarter = HALF // 2
    send_a, send_b, keep_a, keep_b = terms(
        (above, True, 0, quarter), (above, True, quarter, quarter), (above, False, 0, quarter), (above, False, quarter, quarter)
    )
    got_a = flip(send_a, 1)
    got_b = flip(send_b, 1)
    arrived_a = [flip(keep_a[j] + got_a[j], 2 * m) for j in range(m)]
    arrived_b = [flip(keep_b[j] + got_b[j], 2 * m) for j in range(m)]
    send_near, keep_near = terms((below, True, 0, HALF), (below, False, 0, HALF))
    got_near = flip(send_near, 1)
    arrived = list(zip(arrived_a, arrived_b))
    while m > 1:
        m //= 2
        arrived = [jnp.concatenate(x) for x in arrived]
        held = [keep_near[j] + got_near[j] + arrived[j] for j in range(m, 2 * m)]
        arrived = [x + flip(y, 2 * m) for x, y in zip(arrived, held)]
        arrived = [(x[:quarter], x[quarter:]) for x in arrived]
    shuffle = [(s * pairs + p, 2 * p + 1 - s) for s in range(2) for p in range(pairs)]
    packed, trace, rows = call(
        functools.partial(pack_stat, pairs), [(PACKED, BLOCK), (1, 128), (2 * pairs, 128)], [VMEM, SMEM]
    )(statistics[0, 0], owner_blocks)
    old = lax.ppermute(packed, "rep", shuffle)
    half, sums = call(
        functools.partial(finish_half, devices), [(PACKED, BLOCK), (devices, 2, 128)], [VMEM] * 5
    )(keep_near, got_near, *arrived[0], trace)
    other = flip(half, 1)
    sums = lax.all_to_all(sums, AXES, 0, 0)
    facts, square_p, cube_p, out_packed, g_split = call(
        update_stat,
        [(2, 128)] + [(PACKED, BLOCK)] * 3 + [pltpu.HBM((2,) + square, bf16)],
        [VMEM] * 3,
        [pltpu.VMEM((2, 2) + square, bf16), split_square, split_square, pltpu.SemaphoreType.DMA],
        flops=3 * unit,
        out_specs=[VMEM] * 4 + [HBM],
        input_output_aliases={0: 3, 1: 2, 2: 1},
    )(half, other, old)
    new_packed = lax.ppermute(out_packed, "rep", [(t, s) for s, t in shuffle])
    mine_root, totals, g_split = call(
        functools.partial(root, devices),
        [(HALF + HALF // 2, BLOCK), (1, 128), whole],
        [VMEM, HBM] + [VMEM] * 4,
        [pltpu.VMEM(square, bf16)] * 2 + [pltpu.SemaphoreType.DMA],
        flops=unit,
    )(out_packed, in_hbm(g_split), square_p, cube_p, facts, sums)
    other_root = flip(mine_root, 1)
    (middle,) = call(half_way, [whole], [VMEM] * 2, [split_square], flops=unit)(g_split, mine_root)
    mine, most, rest, prec = call(last_product, [piece, (MOST, BLOCK), (HALF - MOST, BLOCK), (2 * stripes, 1, 128)], [VMEM] * 2, [split_square], flops=unit)(middle, other_root)

    bit = 2
    while bit < rep_count:
        prec = prec + flip(prec, bit)
        bit *= 2

    def spread_over_chips(x):
        found, bit = [x], 2
        while bit < rep_count:
            found = found + [flip(y, bit) for y in found]
            bit *= 2
        return found[1:]

    most = spread_over_chips(most)
    rest = spread_over_chips(rest)
    across = flip(mine, 1)
    near = [(s + stripes // 4) % stripes for s in range(stripes)]
    groups = [[(2 * q + c) * stripes + s for s in near for c in range(2)] for q in range(pairs)]
    prec = lax.all_to_all(prec, AXES, 0, 0, axis_index_groups=groups)
    (new_stat,) = call(unpack_stat, [square], [VMEM])(new_packed)
    slab = (pairs * BLOCK, out_grads.shape[1])

    def landing(found):
        count = sum(x.shape[0] for x in found)
        return [pltpu.VMEM((count, BLOCK), f32), pltpu.SemaphoreType.DMA((len(found),))]

    def place(placed, plan, *found):
        (placed,) = call(
            functools.partial(place_next, plan),
            [slab],
            [VMEM] * (len(plan) + 2) + [HBM],
            landing(found),
            out_specs=[HBM],
            input_output_aliases={len(plan) + 2: 0},
        )(*found, scale, rows, placed)
        return placed

    far = range(1, pairs)
    plan, found = [(0, 0)], (mine,)
    placed, scale = call(
        functools.partial(place_first, plan), [slab, (1, 128)], [VMEM] * 4, landing(found), out_specs=[HBM, VMEM]
    )(*found, prec, totals, rows)
    most_across = [flip(x, 1) for x in most]
    rest_across = [flip(x, 1) for x in rest]
    plan = [(pairs, 0)] + [(j, 0) for j in far] + [(pairs + j, 0) for j in far] + [(j, MOST) for j in far]
    placed = place(placed, plan, across, *most, *most_across, *rest)
    placed = place(placed, [(pairs + j, MOST) for j in far], *rest_across)
    return placed, new_stat[None, None]


def solution(mesh):
    in_specs = (
        P("rep", None),
        P("rep", "stripe"),
        P("rep", "stripe", None, None),
        P("stripe", None),
    )
    out_specs = (P(None, "stripe"), P("rep", "stripe", None, None))
    return jax.shard_map(per_device, mesh=mesh, in_specs=in_specs, out_specs=out_specs, check_vma=False)
```

```python
import functools
import math

import jax
import jax.numpy as jnp
from jax import lax
from jax.experimental import pallas as pl
from jax.experimental.pallas import tpu as pltpu
from jax.sharding import PartitionSpec as P


BLOCK = 512
HALF = BLOCK // 2
PACKED = HALF + 8
CHUNK = 64
MOST = HALF - 64

decay_rate = 0.95
damping = 0.25
epsilon = 1e-06
AXES = ("rep", "stripe")
f32 = jnp.float32
bf16 = jnp.bfloat16

ROOT_COEFFS = (
    25 / 16,
    -5 / 16 - 3125 / 4096,
    3125 / 4096,
    -1250 / 4096,
    250 / 4096,
    -25 / 4096,
    1 / 4096,
)
SMALL_CUBIC = (-1 / 32, 9 / 16, -3 / 2, 1.0)


def quotient(poly, divisor):
    rest, out = list(poly), []
    for i in range(len(poly) - len(divisor), -1, -1):
        out.insert(0, rest[i + len(divisor) - 1])
        for n, d in enumerate(divisor):
            rest[i + n] -= out[0] * d
    return out, rest[: len(divisor) - 1]


ROOT_FACTOR, ROOT_REST = quotient(ROOT_COEFFS, SMALL_CUBIC)

VMEM = pl.BlockSpec(memory_space=pltpu.VMEM)
SMEM = pl.BlockSpec(memory_space=pltpu.SMEM)
HBM = pl.BlockSpec(memory_space=pltpu.HBM)
LOW = pl.ds(0, HALF)
TOP = pl.ds(HALF, HALF)


def call(body, out_shapes, in_specs, scratch=(), limit=16, flops=0, out_specs=None, **kwargs):
    return pl.pallas_call(
        body,
        out_shape=[jax.ShapeDtypeStruct(s, f32) if isinstance(s, tuple) else s for s in out_shapes],
        in_specs=in_specs,
        out_specs=out_specs or [VMEM] * len(out_shapes),
        scratch_shapes=list(scratch),
        compiler_params=pltpu.CompilerParams(vmem_limit_bytes=limit << 20),
        cost_estimate=pl.CostEstimate(flops=flops, bytes_accessed=1 << 20, transcendentals=0),
        **kwargs,
    )


def flip(x, mask):
    return lax.ppermute(x, "rep", [(i, i ^ mask) for i in range(lax.axis_size("rep"))])


def in_hbm(x):
    return pltpu.with_memory_space_constraint(x, pltpu.HBM)


def chip_core():
    me = lax.axis_index("rep")
    return lax.shift_right_logical(me, 1), lax.bitwise_and(me, 1)


def split(x):
    hi = x.astype(bf16)
    return hi, (x - hi.astype(f32)).astype(bf16)


def mm(a, b):
    return jnp.dot(a, b, preferred_element_type=f32)


def dot3(a, b):
    return mm(a[0], b[0]) + (mm(a[0], b[1]) + mm(a[1], b[0]))


def triangle():
    i = lax.broadcasted_iota(jnp.int32, (HALF, HALF), 0)
    j = lax.broadcasted_iota(jnp.int32, (HALF, HALF), 1)
    return i, j


def lanes(x):
    rows = jnp.sum(x, axis=0, keepdims=True)
    return sum(rows[:, k : k + 128] for k in range(0, x.shape[1], 128))


def pack_into(out, a, b, c):
    i, j = triangle()
    out[LOW, LOW] = jnp.where(i <= j, a, c)
    out[LOW, TOP] = b
    out[HALF:, LOW] = jnp.broadcast_to(jnp.sum(jnp.where(i == j, c, 0.0), axis=0, keepdims=True), (8, HALF))


def unpack(u, diag):
    i, j = triangle()
    ut = u.T
    return jnp.where(i <= j, u, ut), jnp.where(i > j, u, jnp.where(i < j, ut, diag))


def pack_stat(pairs, source, owners, out, trace, rows, stat, sem):
    copy = pltpu.make_async_copy(source, stat, sem)
    copy.start()
    chip, core = chip_core()
    for n in range(2 * pairs):
        half = core if n < pairs else 1 - core
        row = owners[0, lax.bitwise_xor(chip, jnp.int32(n % pairs))] * BLOCK + half * HALF
        rows[n : n + 1, :] = jnp.full((1, 128), row.astype(f32))
    copy.wait()
    i, j = triangle()
    a, c = stat[LOW, LOW], stat[TOP, TOP]
    pack_into(out, a, stat[LOW, TOP], c)
    trace[...] = lanes(jnp.where(i == j, a + c, 0.0))


def grad_terms(plan, acts, grads, owners, *refs):
    outs, (av, gv, ov, sems) = refs[: len(plan)], refs[len(plan) :]
    chip, core = chip_core()
    copies = [
        pltpu.make_async_copy(src, dst, sems.at[k]) for k, (src, dst) in enumerate(((acts, av), (grads, gv), (owners, ov)))
    ]
    for copy in copies:
        copy.start()
    for copy in copies:
        copy.wait()
    cotangent = gv[...]
    for out, (chips, swapped, first, count) in zip(outs, plan):
        half = 1 - core if swapped else core
        for n, j in enumerate(chips):
            start = ov[0, chip ^ j] * BLOCK + half * HALF + first
            cols = av[:, pl.ds(pl.multiple_of(start, 128), count)]
            out[n] = lax.dot_general(cols, cotangent, (((0,), (0,)), ((), ())), preferred_element_type=f32)


def finish_half(devices, keep, got, rest_a, rest_b, trace, half, sums):
    value = keep[0] + got[0] + jnp.concatenate([rest_a[...], rest_b[...]], axis=0)
    half[LOW] = value
    half[HALF:] = jnp.zeros((PACKED - HALF, BLOCK), f32)
    both = jnp.concatenate([lanes(value * value), trace[...]], axis=0)
    sums[...] = jnp.broadcast_to(both[None], (devices, 2, 128))


def spread(top, corner, out):
    out[0, LOW], out[1, LOW] = split(top)
    out[0, TOP, TOP], out[1, TOP, TOP] = split(corner)
    for k in range(2):
        out[k, TOP, LOW] = out[k, LOW, TOP].T


def upper_product(a, b):
    top = dot3((a[0, LOW], a[1, LOW]), (b[0], b[1]))
    return top, dot3((a[0, TOP], a[1, TOP]), (b[0, :, TOP], b[1, :, TOP]))


def total(x):
    return jnp.sum(jnp.sum(x, axis=0, keepdims=True), axis=1, keepdims=True)


def load_gradient(core, half, other, g):
    mine = pl.ds(pl.multiple_of(core * HALF, HALF), HALF)
    theirs = pl.ds(pl.multiple_of(HALF - core * HALF, HALF), HALF)
    for rows, src in ((mine, half), (theirs, other)):
        g[0, rows], g[1, rows] = split(src[LOW])


def unpack_upper(packed):
    s00, s11 = unpack(packed[LOW, LOW], packed[HALF : HALF + 1, LOW])
    return jnp.concatenate([s00, packed[LOW, TOP]], axis=1), s11


def update_stat(half, other, old, facts, square_out, cube_out, out, g_out, g, s1, s2, sem):
    _, core = chip_core()
    load_gradient(core, half, other, g.at[0])
    copy = pltpu.make_async_copy(g.at[0], g_out, sem)
    copy.start()
    for k in range(2):
        g[1, k] = g[0, k].T
    top, corner = upper_product(g.at[1 - core], g.at[core])
    was_top, was_corner = unpack_upper(old)
    top = decay_rate * was_top + top
    corner = decay_rate * was_corner + corner
    s00, s01 = top[:, :HALF], top[:, HALF:]
    pack_into(out, s00, s01, corner)
    i, j = triangle()
    trace = total(jnp.where(i == j, s00 + corner, 0.0))
    norm_sq = total(s00 * s00 + corner * corner + 2.0 * (s01 * s01))
    inv = 1.0 / jnp.sqrt(norm_sq + epsilon)
    spread(top * inv, corner * inv, s1)
    top, corner = upper_product(s1, s1)
    pack_into(square_out, top[:, :HALF], top[:, HALF:], corner)
    spread(top, corner, s2)
    top, corner = upper_product(s1, s2)
    pack_into(cube_out, top[:, :HALF], top[:, HALF:], corner)
    facts[...] = jnp.concatenate([jnp.broadcast_to(x, (1, 128)) for x in (norm_sq, trace)], axis=0)
    copy.wait()


def coefficients(devices, facts, sums):
    both = jnp.sum(jnp.sum(sums[...], axis=0), axis=1, keepdims=True)
    grad_sq, trace_all = both[0:1], both[1:2]
    shift = (decay_rate * trace_all + 2.0 * grad_sq) * (damping / (devices * BLOCK))
    shift = jnp.broadcast_to(shift, (1, 128))
    norm_sq, trace = facts[0:1, :], facts[1:2, :]
    frob = jnp.sqrt(norm_sq + 2.0 * shift * trace + BLOCK * shift * shift + epsilon)
    a = jnp.sqrt(norm_sq + epsilon) / frob
    e = shift / frob

    def taken(poly, outer):
        out = []
        for i in range(len(poly)):
            value = jnp.full_like(e, poly[-1] * math.comb(len(poly) - 1, i))
            for j in range(len(poly) - 2, i - 1, -1):
                value = value * e + math.comb(j, i) * poly[j]
            out.append((outer * value)[:, 0:1])
            outer = outer * a
        return out

    outer = 1.0 / jnp.sqrt(jnp.sqrt(frob))
    return taken(SMALL_CUBIC, jnp.ones_like(e)), taken(ROOT_FACTOR, outer), taken(ROOT_REST, outer), grad_sq


def root(devices, stat, g_in, square, cubed, facts, sums, out, totals, g, left, right, sem):
    fetch = pltpu.make_async_copy(g_in, g, sem)
    fetch.start()
    small, factor, rest, grad_sq = coefficients(devices, facts, sums)
    inv = 1.0 / jnp.sqrt(facts[0:1, 0:1] + epsilon)
    i, j = triangle()
    on_diagonal = i == j

    def polynomial(k, powers, part):
        value = sum(k[n] * powers[n - 1][part] for n in range(1, len(k)))
        if part == 1:
            return value + jnp.where(on_diagonal, k[0], 0.0)
        return jnp.concatenate([value[:, :HALF] + jnp.where(on_diagonal, k[0], 0.0), value[:, HALF:]], axis=1)

    powers = [[x * inv for x in unpack_upper(stat)], unpack_upper(square), unpack_upper(cubed)]
    for dst, k in ((left, small), (right, factor)):
        dst[LOW] = polynomial(k, powers, 0).astype(bf16)
        dst[TOP, TOP] = polynomial(k, powers, 1).astype(bf16)
        dst[TOP, LOW] = dst[LOW, TOP].T
    out[LOW] = mm(left[LOW], right[...]) + polynomial(rest, powers, 0)
    corner = mm(left[TOP], right[:, TOP]) + polynomial(rest, powers, 1)
    out[HALF:, LOW] = corner[: HALF // 2]
    out[HALF:, TOP] = corner[HALF // 2 :]
    totals[...] = jnp.broadcast_to(grad_sq, (1, 128))
    fetch.wait()


def root_corner(packed):
    return jnp.concatenate([packed[HALF:, LOW], packed[HALF:, TOP]], axis=0)


def half_way(g, packed, out, x):
    _, core = chip_core()
    spread(packed[LOW], root_corner(packed), x)

    @pl.when(core == 1)
    def _():
        y = dot3((x[0, TOP], x[1, TOP]), (g[0], g[1]))
        out[0, LOW], out[1, LOW] = split(y)

    @pl.when(core == 0)
    def _():
        out[0], out[1] = split(dot3((g[0], g[1]), (x[0], x[1])))


def last_product(middle, packed, mine, most, rest, sums, x):
    _, core = chip_core()

    @pl.when(core == 1)
    def _():
        spread(packed[LOW], root_corner(packed), x)
        mine[...] = dot3((middle[0, LOW], middle[1, LOW]), (x[0], x[1]))

    @pl.when(core == 0)
    def _():
        mine[...] = dot3(split(packed[LOW]), (middle[0], middle[1]))

    most[...], rest[...] = mine[:MOST], mine[MOST:]
    sums[...] = jnp.broadcast_to(lanes(mine[...] * mine[...])[None], sums.shape)


def unpack_stat(packed, out):
    sa, sc = unpack(packed[LOW, LOW], packed[HALF : HALF + 1, LOW])
    off = packed[LOW, TOP]
    out[LOW, LOW] = sa
    out[LOW, TOP] = off
    out[TOP, LOW] = off.T
    out[TOP, TOP] = sc


def write_pieces(pieces, scale, out, scaled, sems):
    copies, base = [], 0
    for first, src in pieces:
        for r in range(0, src.shape[0], CHUNK):
            here = pl.ds(base + r, CHUNK)
            scaled[here] = src[pl.ds(r, CHUNK)] * scale
            start = pl.multiple_of(first + r, CHUNK)
            copies.append(pltpu.make_async_copy(scaled.at[here], out.at[pl.ds(start, CHUNK)], sems.at[len(copies)]))
            copies[-1].start()
        base += src.shape[0]
    for copy in copies:
        copy.wait()


def first_row(rows, n):
    return rows[n, 0].astype(jnp.int32)


def place_first(plan, *refs):
    found, (sums, totals, rows, out, scale, scaled, sems) = refs[: len(plan)], refs[len(plan) :]
    prec_sq = jnp.sum(jnp.sum(sums[...], axis=0), axis=1, keepdims=True)
    factor = jnp.sqrt(totals[0:1, 0:1] / (prec_sq + epsilon))
    scale[...] = jnp.broadcast_to(factor, (1, 128))
    write_pieces([(first_row(rows, n) + r, x) for (n, r), x in zip(plan, found)], factor, out, scaled, sems)


def place_next(plan, *refs):
    found, (scale, rows, _, out, scaled, sems) = refs[: len(plan)], refs[len(plan) :]
    write_pieces(
        [(first_row(rows, n) + r, x) for (n, r), x in zip(plan, found)], scale[0:1, 0:1], out, scaled, sems
    )


def per_device(activations, out_grads, statistics, owner_blocks):
    rep_count = lax.axis_size("rep")
    pairs = rep_count // 2
    devices = rep_count * lax.axis_size("stripe")
    stripes = lax.axis_size("stripe")
    tokens = activations.shape[0]
    piece, square = (HALF, BLOCK), (BLOCK, BLOCK)
    unit = 6 * BLOCK**3

    whole = jax.ShapeDtypeStruct((2,) + square, bf16)
    split_square = pltpu.VMEM((2,) + square, bf16)
    m = pairs // 2

    def terms(*plan):
        return call(
            functools.partial(grad_terms, plan),
            [(len(chips), count, BLOCK) for chips, _, _, count in plan],
            [HBM] * 3,
            [
                pltpu.VMEM(activations.shape, bf16),
                pltpu.VMEM(out_grads.shape, bf16),
                pltpu.SMEM(owner_blocks.shape, jnp.int32),
                pltpu.SemaphoreType.DMA((3,)),
            ],
            flops=2 * tokens * HALF * BLOCK * len(plan),
        )(*(in_hbm(x) for x in (activations, out_grads, owner_blocks)))

    above, below = range(m, pairs), range(m)
    quarter = HALF // 2
    send_a, send_b, keep_a, keep_b = terms(
        (above, True, 0, quarter), (above, True, quarter, quarter), (above, False, 0, quarter), (above, False, quarter, quarter)
    )
    got_a = flip(send_a, 1)
    got_b = flip(send_b, 1)
    arrived_a = [flip(keep_a[j] + got_a[j], 2 * m) for j in range(m)]
    arrived_b = [flip(keep_b[j] + got_b[j], 2 * m) for j in range(m)]
    send_near, keep_near = terms((below, True, 0, HALF), (below, False, 0, HALF))
    got_near = flip(send_near, 1)
    arrived = list(zip(arrived_a, arrived_b))
    while m > 1:
        m //= 2
        arrived = [jnp.concatenate(x) for x in arrived]
        held = [keep_near[j] + got_near[j] + arrived[j] for j in range(m, 2 * m)]
        arrived = [x + flip(y, 2 * m) for x, y in zip(arrived, held)]
        arrived = [(x[:quarter], x[quarter:]) for x in arrived]
    shuffle = [(s * pairs + p, 2 * p + 1 - s) for s in range(2) for p in range(pairs)]
    packed, trace, rows = call(
        functools.partial(pack_stat, pairs),
        [(PACKED, BLOCK), (1, 128), (2 * pairs, 128)],
        [HBM, SMEM],
        [pltpu.VMEM(square, f32), pltpu.SemaphoreType.DMA],
    )(in_hbm(statistics[0, 0]), owner_blocks)
    old = lax.ppermute(packed, "rep", shuffle)
    half, sums = call(
        functools.partial(finish_half, devices), [(PACKED, BLOCK), (devices, 2, 128)], [VMEM] * 5
    )(keep_near, got_near, *arrived[0], trace)
    other = flip(half, 1)
    sums = lax.all_to_all(sums, AXES, 0, 0)
    facts, square_p, cube_p, out_packed, g_split = call(
        update_stat,
        [(2, 128)] + [(PACKED, BLOCK)] * 3 + [pltpu.HBM((2,) + square, bf16)],
        [VMEM] * 3,
        [pltpu.VMEM((2, 2) + square, bf16), split_square, split_square, pltpu.SemaphoreType.DMA],
        flops=3 * unit,
        out_specs=[VMEM] * 4 + [HBM],
        input_output_aliases={0: 3, 1: 2, 2: 1},
    )(half, other, old)
    new_packed = lax.ppermute(out_packed, "rep", [(t, s) for s, t in shuffle])
    mine_root, totals, g_split = call(
        functools.partial(root, devices),
        [(HALF + HALF // 2, BLOCK), (1, 128), whole],
        [VMEM, HBM] + [VMEM] * 4,
        [pltpu.VMEM(square, bf16)] * 2 + [pltpu.SemaphoreType.DMA],
        flops=unit,
    )(out_packed, in_hbm(g_split), square_p, cube_p, facts, sums)
    other_root = flip(mine_root, 1)
    (middle,) = call(half_way, [whole], [VMEM] * 2, [split_square], flops=unit)(g_split, mine_root)
    mine, most, rest, prec = call(last_product, [piece, (MOST, BLOCK), (HALF - MOST, BLOCK), (2 * stripes, 1, 128)], [VMEM] * 2, [split_square], flops=unit)(middle, other_root)

    bit = 2
    while bit < rep_count:
        prec = prec + flip(prec, bit)
        bit *= 2

    def spread_over_chips(x):
        found, bit = [x], 2
        while bit < rep_count:
            found = found + [flip(y, bit) for y in found]
            bit *= 2
        return found[1:]

    most = spread_over_chips(most)
    rest = spread_over_chips(rest)
    across = flip(mine, 1)
    near = [(s + stripes // 4) % stripes for s in range(stripes)]
    groups = [[(2 * q + c) * stripes + s for s in near for c in range(2)] for q in range(pairs)]
    prec = lax.all_to_all(prec, AXES, 0, 0, axis_index_groups=groups)
    (new_stat,) = call(unpack_stat, [square], [VMEM])(new_packed)
    slab = (pairs * BLOCK, out_grads.shape[1])

    def landing(found):
        count = sum(x.shape[0] for x in found)
        return [pltpu.VMEM((count, BLOCK), f32), pltpu.SemaphoreType.DMA((count // CHUNK,))]

    def place(placed, plan, *found):
        (placed,) = call(
            functools.partial(place_next, plan),
            [slab],
            [VMEM] * (len(plan) + 2) + [HBM],
            landing(found),
            out_specs=[HBM],
            input_output_aliases={len(plan) + 2: 0},
        )(*found, scale, rows, placed)
        return placed

    far = range(1, pairs)
    plan, found = [(0, 0)], (mine,)
    placed, scale = call(
        functools.partial(place_first, plan), [slab, (1, 128)], [VMEM] * 4, landing(found), out_specs=[HBM, VMEM]
    )(*found, prec, totals, rows)
    most_across = [flip(x, 1) for x in most]
    rest_across = [flip(x, 1) for x in rest]
    plan = [(pairs, 0)] + [(j, 0) for j in far] + [(pairs + j, 0) for j in far] + [(j, MOST) for j in far]
    placed = place(placed, plan, across, *most, *most_across, *rest)
    placed = place(placed, [(pairs + j, MOST) for j in far], *rest_across)
    return placed, new_stat[None, None]


def solution(mesh):
    in_specs = (
        P("rep", None),
        P("rep", "stripe"),
        P("rep", "stripe", None, None),
        P("stripe", None),
    )
    out_specs = (P(None, "stripe"), P("rep", "stripe", None, None))
    return jax.shard_map(per_device, mesh=mesh, in_specs=in_specs, out_specs=out_specs, check_vma=False)
```
